32 devices in a mesh: wide: 16 (over z, x, core), narrow: 2 (over y).
Axes of the slice: x: 2, y: 2, z: 4, core: 2. Of those that a mesh axis runs over, the one named last changes fastest.
Arguments:
- layer_in: bfloat16 [128, 256, 768], P(('wide', 'narrow')), may hold values from -6 to 6
- segment_ids: int32 [128, 256], P(('wide', 'narrow')), may hold values from 0 to 31, as said below
- live_mask: int32 [128, 256], P(('wide', 'narrow')), may hold values from 0 to 1, as said below
- expert_ids: int32 [128], P(('wide', 'narrow')), may hold values from 1 to 2
- cotangent: bfloat16 [128, 256, 768], P(('wide', 'narrow')), may hold values from -6 to 6
- norm1_gain: float32 [768], replicated, may hold values from 0.1 to 1.9
- norm1_bias: float32 [768], replicated, may hold values from -3 to 3
- q_weight: bfloat16 [768, 768], P('wide'), may hold values from -0.21875 to 0.21875
- q_bias: float32 [768], replicated, may hold values from -3 to 3
- k_weight: bfloat16 [768, 768], P('wide'), may hold values from -0.21875 to 0.21875
- v_weight: bfloat16 [768, 768], P('wide'), may hold values from -0.21875 to 0.21875
- v_bias: float32 [768], replicated, may hold values from -3 to 3
- o_weight: bfloat16 [768, 768], P('wide'), may hold values from -0.875 to 0.875
- o_bias: float32 [768], replicated, may hold values from -3 to 3
- norm2_gain: float32 [768], replicated, may hold values from 0.1 to 1.9
- norm2_bias: float32 [768], replicated, may hold values from -3 to 3
- in_weight: bfloat16 [768, 3072], P('wide'), may hold values from -0.21875 to 0.21875
- in_bias: float32 [3072], replicated, may hold values from -3 to 3
- out_weight: bfloat16 [3072, 768], P('wide'), may hold values from -0.109375 to 0.109375
- out_bias: float32 [768], replicated, may hold values from -3 to 3
Outputs:
- layer_out: bfloat16 [128, 256, 768], P(('wide', 'narrow'))
- input_grad: bfloat16 [128, 256, 768], P(('wide', 'narrow'))
- counts: int32 [3], replicated
- norm1_gain_grad: float32 [768], replicated
- norm1_bias_grad: float32 [768], replicated
- q_weight_grad: float32 [768, 768], P('wide')
- q_bias_grad: float32 [768], replicated
- k_weight_grad: float32 [768, 768], P('wide')
- v_weight_grad: float32 [768, 768], P('wide')
- v_bias_grad: float32 [768], replicated
- o_weight_grad: float32 [768, 768], P('wide')
- o_bias_grad: float32 [768], replicated
- norm2_gain_grad: float32 [768], replicated
- norm2_bias_grad: float32 [768], replicated
- in_weight_grad: float32 [768, 3072], P('wide')
- in_bias_grad: float32 [3072], replicated
- out_weight_grad: float32 [3072, 768], P('wide')
- out_bias_grad: float32 [768], replicated
The draws below stay inside these ranges and needn't reach their ends.
Inputs may be any that keep to these rules, and one draw needn't show every extreme that they name: `segment_ids`: in each row the captions, 8 to 40 tokens each, lie in order and are numbered from 0; after the last caption the padding slots carry the next number. `live_mask`: the live slots of a row are a prefix of it, at least 8 of them. `expert_ids`: no row names the vision expert.
All inputs are finite; a program needn't handle non-finite values.
Results may differ from the reference program's by a relative error of at most 0.018.
Values may be sent and summed in bfloat16 or wider, within the bound.
A program may use at most 192 MiB of HBM per device.

```python
import math
import jax
import jax.numpy as jnp
from jax import lax

D = 768
FF = 3072
HEADS = 12
SLOTS = 256
ROWS = 128


def packed_rows(key):
    length_key, row_key = jax.random.split(key)
    lengths = jax.random.randint(length_key, (ROWS, SLOTS // 8), 8, 41)
    short_row = jax.random.randint(row_key, (), 0, ROWS)
    row_pos = lax.broadcasted_iota(jnp.int32, (ROWS, SLOTS // 8), 0)
    lengths = jnp.where(row_pos == short_row, 8, lengths)
    ends = jnp.cumsum(lengths, axis=1)
    slot_pos = lax.broadcasted_iota(jnp.int32, (ROWS, SLOTS), 1)
    seg_vals = jnp.sum((ends[:, None, :] <= slot_pos[:, :, None]).astype(jnp.int32), axis=2)
    used_slots = jnp.max(jnp.where(ends <= SLOTS, ends, 0), axis=1)
    live_vals = (slot_pos < used_slots[:, None]).astype(jnp.int32)
    return (seg_vals.astype(jnp.int32), live_vals)


def draw_segment_ids(key, part):
    seg_vals, live_vals = packed_rows(jax.random.fold_in(key, 7))
    return seg_vals


def draw_live_mask(key, part):
    seg_vals, live_vals = packed_rows(jax.random.fold_in(key, 7))
    return live_vals


def set_ends(drawn, key, smallest, largest):
    longest = drawn.shape.index(max(drawn.shape))
    spots = []
    for shift in (0, 1):
        where = [jax.random.randint(jax.random.fold_in(key, axis), (), 0, length) for axis, length in enumerate(drawn.shape)]
        where[longest] = (where[longest] + shift) % drawn.shape[longest]
        spots.append(tuple(where))
    return drawn.at[spots[0]].set(smallest).at[spots[1]].set(largest)


def raised(array, own_key, source, target, shards_of, factor):
    owner, partner = [(jnp.arange(array.shape[axis_at]) // (array.shape[axis_at] // shards_of)).reshape([-1 if axis == axis_at else 1 for axis in range(array.ndim)]) for axis_at in (source, target)]
    chosen = jax.random.permutation(own_key, shards_of)[partner]
    strong = (owner == chosen) | (owner == (partner + shards_of // 2) % shards_of)
    return jnp.where(strong, factor * array, array)


def level_of(rng, shape, cuts, smallest, top_value):
    def one(position, parts):
        steps = jax.random.uniform(jax.random.fold_in(jax.random.fold_in(rng, 6), position), (parts,), jnp.float32, smallest / len(cuts), top_value / len(cuts))
        return jnp.repeat(jnp.exp(steps), shape[position] // parts).reshape((-1,) + (1,) * (len(shape) - position - 1))

    level = one(*cuts[0])
    for cut in cuts[1:]:
        level = level * one(*cut)
    return level


def gaussian(stream_key, extent, width, reach, cuts=(), kind=jnp.bfloat16):
    factor_of = level_of(stream_key, extent, cuts, -0.22, 0.18) if cuts else 1.0
    result = jax.random.normal(stream_key, extent, jnp.float32) * width * factor_of
    return jnp.minimum(jnp.maximum(result, -reach), reach).astype(kind)


def noise_with(stream_key, extent, width, bound, cuts, heavy, kind=jnp.bfloat16):
    drawn = width * jax.random.normal(stream_key, extent, jnp.float32)
    if cuts:
        drawn = drawn * level_of(stream_key, extent, cuts, -0.22, 0.18)
    return jnp.clip(raised(drawn, jax.random.fold_in(stream_key, 3), *heavy), -bound, bound).astype(kind)


def setup_inputs(seed: int = 0) -> dict:
    splits = jax.random.split(jax.random.key(seed), 21)
    return {
        "layer_in": gaussian(splits[0], (ROWS, SLOTS, D), 1.0, 6.0, ((0, 32),)),
        "segment_ids": draw_segment_ids(jax.random.fold_in(splits[20], 71), 0),
        "live_mask": draw_live_mask(jax.random.fold_in(splits[20], 71), 0),
        "expert_ids": set_ends(jax.random.randint(splits[3], (ROWS,), 1, 3), jax.random.fold_in(splits[3], 1), 1, 2).astype(jnp.int32),
        "cotangent": noise_with(splits[4], (ROWS, SLOTS, D), 1.0, 6.0, ((0, 32),), (0, 2, 32, 2.75)),
        "norm1_gain": jnp.clip(1.0 + 0.18 * jax.random.normal(splits[5], (D,), jnp.float32), 0.1, 1.9),
        "norm1_bias": gaussian(splits[6], (D,), 0.5, 3.0, (), jnp.float32),
        "q_weight": gaussian(splits[7], (D, D), D ** -0.5, 0.21875, ((0, 16),)),
        "q_bias": gaussian(splits[8], (D,), 0.5, 3.0, (), jnp.float32),
        "k_weight": gaussian(splits[9], (D, D), D ** -0.5, 0.21875, ((0, 16),)),
        "v_weight": gaussian(splits[10], (D, D), D ** -0.5, 0.21875, ((0, 16),)),
        "v_bias": gaussian(splits[11], (D,), 0.5, 3.0, (), jnp.float32),
        "o_weight": gaussian(splits[12], (D, D), (D // 16) ** -0.5, 0.875, ((0, 16),)),
        "o_bias": gaussian(splits[13], (D,), 0.5, 3.0, (), jnp.float32),
        "norm2_gain": jnp.clip(1.0 + 0.18 * jax.random.normal(splits[14], (D,), jnp.float32), 0.1, 1.9),
        "norm2_bias": gaussian(splits[15], (D,), 0.5, 3.0, (), jnp.float32),
        "in_weight": gaussian(splits[16], (D, FF), D ** -0.5, 0.21875, ((0, 16),)),
        "in_bias": gaussian(splits[17], (FF,), 0.5, 3.0, (), jnp.float32),
        "out_weight": gaussian(splits[18], (FF, D), FF ** -0.5, 0.109375, ((0, 16),)),
        "out_bias": gaussian(splits[19], (D,), 0.5, 3.0, (), jnp.float32),
    }


EPSILON = 1e-06
MASKED = -1e+30

@jax.custom_vjp
def low(v):
    return lax.optimization_barrier(v.astype(jnp.bfloat16)).astype(jnp.float32)

@jax.custom_vjp
def low_back(v):
    return v

def low_keep(v):
    return (low(v), None)

def low_pass(kept, grad):
    return (grad,)

def back_keep(v):
    return (v, None)

def back_low(kept, grad):
    return (low(grad),)
low.defvjp(low_keep, low_pass)
low_back.defvjp(back_keep, back_low)

def norm_rows(values, gain_vec, bias_vec):
    row_mean = lax.optimization_barrier(jnp.mean(values, axis=-1, keepdims=True))
    centred = values - row_mean
    variance = lax.optimization_barrier(jnp.mean(centred * centred, axis=-1, keepdims=True))
    return centred * lax.rsqrt(variance + EPSILON) * gain_vec + bias_vec

def dot_high(left, right):
    return jnp.dot(left, right, precision=lax.Precision.HIGHEST)

def allowed_pairs(seg_rows, live_rows):
    slot_total = seg_rows.shape[-1]
    same_seg = seg_rows[:, :, None] == seg_rows[:, None, :]
    diagonal = jnp.eye(slot_total, dtype=bool)
    return (same_seg & ((live_rows[:, None, :] > 0) | diagonal[None]))[:, None]

def layer_rows(params, x_rows, seg_rows, live_rows):
    norm1_gain, norm1_bias, q_weight, q_bias, k_weight, v_weight, v_bias, o_weight, o_bias, norm2_gain, norm2_bias, in_weight, in_bias, out_weight, out_bias = params
    group_rows, slot_total, width_all = x_rows.shape
    head_dim = width_all // HEADS
    tokens_here = group_rows * slot_total
    x_flat = x_rows.reshape(tokens_here, width_all)
    normed_one = low(norm_rows(x_flat, norm1_gain, norm1_bias))

    def heads_view(values):
        return values.reshape(group_rows, slot_total, HEADS, head_dim)
    query_heads = heads_view(low(low_back(dot_high(normed_one, q_weight) + q_bias)))
    key_heads = heads_view(low(low_back(dot_high(normed_one, k_weight))))
    value_heads = heads_view(low(low_back(dot_high(normed_one, v_weight) + v_bias)))
    scores = jnp.einsum('gqhe,gkhe->ghqk', query_heads, key_heads, precision=lax.Precision.HIGHEST) * 0.125
    scores = low_back(jnp.where(allowed_pairs(seg_rows, live_rows), scores, MASKED))
    row_top = lax.optimization_barrier(jnp.max(scores, axis=-1, keepdims=True))
    exp_terms = jnp.exp(scores - row_top)
    attn_probs = exp_terms / lax.optimization_barrier(jnp.sum(exp_terms, axis=-1, keepdims=True))
    mixed_heads = jnp.einsum('ghqk,gkhe->gqhe', low(attn_probs), value_heads, precision=lax.Precision.HIGHEST)
    mixed_flat = low(low_back(mixed_heads.reshape(tokens_here, width_all)))
    attn_out = low_back(dot_high(mixed_flat, o_weight) + o_bias)
    residual = x_flat + attn_out
    normed_two = low(norm_rows(residual, norm2_gain, norm2_bias))
    pre_act = low_back(dot_high(normed_two, in_weight) + in_bias)
    hidden = low(jax.nn.gelu(pre_act, approximate=False))
    branch = low_back(dot_high(hidden, out_weight) + out_bias)
    return (residual + branch).reshape(group_rows, slot_total, width_all)

def reference(layer_in, segment_ids, live_mask, expert_ids, cotangent, norm1_gain, norm1_bias, q_weight, q_bias, k_weight, v_weight, v_bias, o_weight, o_bias, norm2_gain, norm2_bias, in_weight, in_bias, out_weight, out_bias):
    row_all = layer_in.shape[0]
    group_rows = math.gcd(row_all, max(1, 4096 // SLOTS))
    live_tokens = lax.optimization_barrier(jnp.sum(live_mask, axis=1))
    counts = jnp.stack([jnp.sum(jnp.where(expert_ids == expert, live_tokens, 0)) for expert in range(3)]).astype(jnp.int32)
    count_float = counts.astype(jnp.float32)
    row_scale = (count_float[1] + count_float[2]) / (2.0 * count_float[expert_ids])
    grad_out = cotangent.astype(jnp.float32) * (live_mask.astype(jnp.float32) * row_scale[:, None])[:, :, None]
    params = tuple((item.astype(jnp.float32) for item in (norm1_gain, norm1_bias, q_weight, q_bias, k_weight, v_weight, v_bias, o_weight, o_bias, norm2_gain, norm2_bias, in_weight, in_bias, out_weight, out_bias)))
    block_total = row_all // group_rows
    seg_blocks = segment_ids.reshape(block_total, group_rows, SLOTS)
    live_blocks = live_mask.reshape(block_total, group_rows, SLOTS)

    def forward(x_all, weights):

        def one_group(carry, pieces):
            x_rows, seg_rows, live_rows = pieces
            return (carry, jax.checkpoint(layer_rows)(weights, x_rows, seg_rows, live_rows))
        x_blocks = x_all.reshape(block_total, group_rows, SLOTS, D)
        carry_end, outputs = lax.scan(one_group, jnp.zeros((), jnp.float32), (x_blocks, seg_blocks, live_blocks))
        return outputs.reshape(row_all, SLOTS, D)
    layer_out, pull = jax.vjp(forward, layer_in.astype(jnp.float32), params)
    input_grad, param_grads = pull(grad_out)
    return (layer_out.astype(jnp.bfloat16), input_grad.astype(jnp.bfloat16), counts, param_grads[0], param_grads[1], param_grads[2], param_grads[3], param_grads[4], param_grads[5], param_grads[6], param_grads[7], param_grads[8], param_grads[9], param_grads[10], param_grads[11], param_grads[12], param_grads[13], param_grads[14])
```

```python
import functools
import math

import jax
import jax.numpy as jnp
from jax import lax
from jax.experimental import pallas as pl
from jax.experimental.pallas import tpu as pltpu
from jax.sharding import PartitionSpec as P

HEADS = 12


MESH = pl.DeviceIdType.MESH
BF = jnp.bfloat16
F32 = jnp.float32


class Place:
    def __init__(self, depth, lanes):
        wide = lax.axis_index("wide")
        self.depth, self.lanes = depth, lanes
        self.n = lax.axis_index("narrow")
        self.c = lax.rem(wide, 2)
        self.x = lax.rem(wide // 2, 2)
        self.z = wide // 4
        self.y = lax.rem(self.n, 2)

    def at(self, z=None, x=None, c=None, n=None):
        z = self.z if z is None else z
        x = self.x if x is None else x
        c = self.c if c is None else c
        n = self.n if n is None else n
        return ((z * 2 + x) * 2 + c, n)

    def core(self):
        return self.at(c=1 - self.c)

    def across_x(self):
        return self.at(x=1 - self.x)

    def flip_n(self, bit):
        step = 1 << bit
        low = lax.rem(self.n // step, 2)
        return self.n + step * (1 - 2 * low)

    def across_y(self):
        return self.at(n=self.flip_n(0))

    def along_z(self, step):
        return self.at(z=lax.rem(self.z + step, self.depth))

    def greet(self):
        bits = self.lanes.bit_length() - 1
        others = [self.core(), self.across_x()]
        others += [self.at(n=self.flip_n(b)) for b in range(bits)]
        others += [self.along_z(d) for d in range(1, self.depth)]
        barrier = pltpu.get_barrier_semaphore()
        for other in others:
            pl.semaphore_signal(barrier, inc=1, device_id=other, device_id_type=MESH)
        pl.semaphore_wait(barrier, len(others))


class Sems:
    def __init__(self, send, recv):
        self.send, self.recv, self.used = send, recv, 0
        self.open = []

    def copy(self, src, dst, device):
        i = self.used
        self.used += 1
        made = pltpu.make_async_remote_copy(
            src_ref=src, dst_ref=dst, send_sem=self.send.at[i], recv_sem=self.recv.at[i],
            device_id=device, device_id_type=MESH,
        )
        made.start()
        self.open.append(made)
        return made

    def drain(self):
        for made in self.open:
            made.wait_send()
        self.open = []


def gather_part(me, sems, view):
    own = (2 * me.y, 2 * me.y + 1)
    far = (2 * (1 - me.y), 2 * (1 - me.y) + 1)
    x, c, z = me.x, me.c, me.z
    everything = slice(None)
    hops = []
    for u in own:
        hops.append([sems.copy(view(u, z, x, c), view(u, z, x, c), me.along_z(d)) for d in range(1, me.depth)])
    yield
    first = []
    for k, u in enumerate(own):
        for hop in hops[k]:
            hop.wait_recv()
        mine = view(u, everything, x, c)
        first.append((sems.copy(mine, mine, me.across_x()), sems.copy(mine, mine, me.across_y())))
        yield
    (x_a, y_a), (x_b, y_b) = first
    x_a.wait_recv()
    there = view(own[0], everything, 1 - x, c)
    y_fwd = sems.copy(there, there, me.across_y())
    block = view(own[0], everything, everything, c)
    cores = [sems.copy(block, block, me.core())]
    yield
    y_b.wait_recv()
    there = view(far[1], everything, x, c)
    x_fwd = sems.copy(there, there, me.across_x())
    yield
    x_b.wait_recv()
    block = view(own[1], everything, everything, c)
    cores.append(sems.copy(block, block, me.core()))
    yield
    y_a.wait_recv()
    y_fwd.wait_recv()
    block = view(far[0], everything, everything, c)
    cores.append(sems.copy(block, block, me.core()))
    yield
    x_fwd.wait_recv()
    block = view(far[1], everything, everything, c)
    cores.append(sems.copy(block, block, me.core()))
    yield
    for made in cores:
        made.wait_recv()
    yield


LAG = 2
SPACE = pltpu.VMEM
GATHER_COPIES = lambda depth: 2 * (depth - 1) + 4 + 2 + 4


def gather_kernel(depth, lanes, halves, q, k, v, o, w_in, w_out, ga, gi, go, local, send, recv):
    me = Place(depth, lanes)
    rows, width = q.shape
    x, c, z = me.x, me.c, me.z

    def fill(pairs):
        made = [pltpu.make_async_copy(s, d, local.at[i]) for i, (s, d) in enumerate(pairs)]
        for m in made:
            m.start()
        for m in made:
            m.wait()

    @pl.when(me.y == 0)
    def _():
        fill([(q, ga.at[0, z, x, c]), (k, ga.at[1, z, x, c])])

    @pl.when(me.y == 1)
    def _():
        fill([(v, ga.at[2, z, x, c]), (o, ga.at[3, z, x, c])])

    pairs = []
    for kk in range(2):
        u = 2 * me.y + kk
        pairs.append((w_in.at[:, pl.ds(pl.multiple_of(u * width, width), width)], gi.at[u, z, x, c]))
        pairs.append((w_out.at[pl.ds(pl.multiple_of(u * rows, rows), rows), :], go.at[z, x, c, u]))
    fill(pairs)
    me.greet()
    part = width // halves
    events = []
    per = GATHER_COPIES(depth)
    all_sems = []
    for g in range(3):
        for h in range(halves):
            cols = pl.ds(h * part, part)

            def view(u, zs, xs, cs, g=g, cols=cols):
                if g == 0:
                    return ga.at[u, zs, xs, cs, :, cols]
                if g == 1:
                    return gi.at[u, zs, xs, cs, :, cols]
                return go.at[zs, xs, cs, u, :, cols]

            i = g * halves + h
            sems = Sems(send.at[i], recv.at[i])
            all_sems.append(sems)
            events.append(gather_part(me, sems, view))
    order = []
    for lag in range(64):
        for i, e in enumerate(events):
            step = lag - LAG * i
            if 0 <= step < 10:
                next(e, None)
    for s in all_sems:
        s.drain()


def gather_all(depth, lanes, q, k, v, o, w_in, w_out, halves=2):
    rows, width = q.shape
    parts = 3 * halves
    per = GATHER_COPIES(depth)
    shape = jax.ShapeDtypeStruct((4, depth, 2, 2, rows, width), BF)
    shape_o = jax.ShapeDtypeStruct((depth, 2, 2, 4, rows, width), BF)
    anyspec = pl.BlockSpec(memory_space=pl.ANY); vspec = pl.BlockSpec(memory_space=SPACE)
    return pl.pallas_call(
        functools.partial(gather_kernel, depth, lanes, halves),
        out_shape=(shape, shape, shape_o),
        in_specs=[anyspec] * 6,
        out_specs=(vspec,) * 3,
        scratch_shapes=[
            pltpu.SemaphoreType.DMA((4,)),
            pltpu.SemaphoreType.DMA((parts, per)),
            pltpu.SemaphoreType.DMA((parts, per)),
        ],
        compiler_params=pltpu.CompilerParams(collective_id=0, has_side_effects=True, vmem_limit_bytes=60 << 20),
        name="gather_all",
    )(q, k, v, o, w_in, w_out)


def reduce_part(me, sems, view, far_view, bufs, emit):
    rc, ry, rx, rz, fin, far = bufs
    a, b = 2 * me.y, 2 * me.y + 1
    ta, tb = 2 * (1 - me.y), 2 * (1 - me.y) + 1
    x, c, z = me.x, me.c, me.z
    every = slice(None)
    bits = me.lanes.bit_length() - 1

    def add(dst, *terms):
        total = dst[...].astype(F32)
        for t in terms:
            total = total + t[...].astype(F32)
        dst[...] = total.astype(BF)

    cores = {}
    for i, u in enumerate((ta, tb, b, a)):
        cores[i] = sems.copy(view(u, every, every, 1 - c), rc.at[i], me.core())
    yield
    cores[0].wait_recv()
    add(view(ta, every, every, c), rc.at[0])
    y_diag = sems.copy(view(ta, every, 1 - x, c), ry.at[0], me.across_y())
    yield
    cores[1].wait_recv()
    add(view(tb, every, every, c), rc.at[1])
    x_diag = sems.copy(view(tb, every, 1 - x, c), rx.at[0], me.across_x())
    yield
    cores[2].wait_recv()
    add(view(b, every, every, c), rc.at[2])
    x_near = sems.copy(view(b, every, 1 - x, c), rx.at[1], me.across_x())
    y_near = sems.copy(view(ta, every, x, c), ry.at[1], me.across_y())
    cores[3].wait_recv()
    add(view(a, every, every, c), rc.at[3])
    yield
    y_diag.wait_recv()
    add(view(a, every, 1 - x, c), ry.at[0])
    x_last = sems.copy(view(a, every, 1 - x, c), rx.at[2], me.across_x())
    yield
    x_diag.wait_recv()
    add(view(tb, every, x, c), rx.at[0])
    y_last = sems.copy(view(tb, every, x, c), ry.at[2], me.across_y())
    yield
    y_near.wait_recv()
    x_last.wait_recv()
    add(view(a, every, x, c), ry.at[1], rx.at[2])
    z_hops = []
    hop = []
    for d in range(1, me.depth):
        to = lax.rem(z + d, me.depth)
        hop.append(sems.copy(view(a, to, x, c), rz.at[0, d - 1], me.along_z(d)))
    z_hops.append(hop)
    yield
    x_near.wait_recv()
    y_last.wait_recv()
    add(view(b, every, x, c), rx.at[1], ry.at[2])
    hop = []
    for d in range(1, me.depth):
        to = lax.rem(z + d, me.depth)
        hop.append(sems.copy(view(b, to, x, c), rz.at[1, d - 1], me.along_z(d)))
    z_hops.append(hop)
    yield
    sent = []
    for k, u in enumerate((a, b)):
        for h in z_hops[k]:
            h.wait_recv()
        total = view(u, z, x, c)[...].astype(F32)
        for d in range(1, me.depth):
            total = total + rz[k, d - 1].astype(F32)
        fin[0, k] = total.astype(BF)
        for bit in range(1, bits):
            swap = sems.copy(fin.at[bit - 1, k], far.at[bit, k], me.at(n=me.flip_n(bit)))
            swap.wait_recv()
            total = fin[bit - 1, k].astype(F32) + far[bit, k].astype(F32)
            fin[bit, k] = total.astype(BF)
        last = max(bits - 1, 0)
        sent.append(sems.copy(fin.at[last, k], far.at[0, k], me.across_y()))
        emit(u, fin[last, k])
        yield
    for k, u in enumerate((ta, tb)):
        sent[k].wait_recv()
        emit(u, far[0, k])
        yield


def reduce_copies(depth, lanes):
    bits = lanes.bit_length() - 1
    return 4 + 6 + 2 * (depth - 1) + 2 * (bits - 1) + 2


REDUCE_STEPS = 12


def reduce_kernel(depth, lanes, halves, ga, gi, go, ra, ri, ro, wa, wi, wo, rc, ry, rx, rz, fin, far, local, send, recv):
    me = Place(depth, lanes)
    loads = [pltpu.make_async_copy(s, d, local.at[i]) for i, (s, d) in enumerate(((ga, wa), (gi, wi), (go, wo)))]
    for m in loads:
        m.start()
    me.greet()
    for m in loads:
        m.wait()
    width = wa.shape[-1]
    part = width // halves
    events, all_sems = [], []
    for g in range(3):
        for h in range(halves):
            cols = pl.ds(h * part, part)
            i = g * halves + h

            def view(u, zs, xs, cs, g=g, cols=cols):
                if g == 0:
                    return wa.at[u, zs, xs, cs, :, cols]
                if g == 1:
                    return wi.at[u, zs, xs, cs, :, cols]
                return wo.at[zs, xs, cs, u, :, cols]

            def emit(u, value, g=g, cols=cols):
                (ra, ri, ro)[g][u, :, cols] = value.astype(F32)

            sems = Sems(send.at[i], recv.at[i])
            all_sems.append(sems)
            bufs = [t.at[i] for t in (rc, ry, rx, rz, fin, far)]
            events.append(reduce_part(me, sems, view, None, bufs, emit))
    for lag in range(100):
        for i, e in enumerate(events):
            step = lag - LAG * i
            if 0 <= step < REDUCE_STEPS + 1:
                next(e, None)
    for s in all_sems:
        s.drain()


def reduce_all(depth, lanes, ga, gi, go, halves=2):
    rows, width = ga.shape[-2:]
    parts, part = 3 * halves, width // halves
    per = reduce_copies(depth, lanes)
    bits = lanes.bit_length() - 1
    anyspec = pl.BlockSpec(memory_space=pl.ANY)
    vspec = pl.BlockSpec(memory_space=pltpu.VMEM)
    out = jax.ShapeDtypeStruct((4, rows, width), F32)
    v = lambda *s: pltpu.VMEM(s, BF)
    return pl.pallas_call(
        functools.partial(reduce_kernel, depth, lanes, halves),
        out_shape=(out, out, out),
        in_specs=[anyspec] * 3,
        out_specs=(vspec,) * 3,
        scratch_shapes=[
            v(*ga.shape), v(*gi.shape), v(*go.shape),
            v(parts, 4, depth, 2, rows, part), v(parts, 3, depth, rows, part), v(parts, 3, depth, rows, part),
            v(parts, 2, depth - 1, rows, part), v(parts, max(bits, 1), 2, rows, part), v(parts, max(bits, 1), 2, rows, part),
            pltpu.SemaphoreType.DMA((3,)),
            pltpu.SemaphoreType.DMA((parts, per)),
            pltpu.SemaphoreType.DMA((parts, per)),
        ],
        compiler_params=pltpu.CompilerParams(collective_id=1, has_side_effects=True, vmem_limit_bytes=60 << 20),
        name="reduce_all",
    )(ga, gi, go)


EPSILON = 1e-06
MASKED = -1e30


def norm_rows(values, gain_vec, bias_vec):
    row_mean = jnp.mean(values, axis=-1, keepdims=True)
    centred = values - row_mean
    variance = jnp.mean(centred * centred, axis=-1, keepdims=True)
    return centred * lax.rsqrt(variance + EPSILON) * gain_vec + bias_vec


def gelu_exact(values):
    return jax.nn.gelu(values, approximate=False)


def plain_product(left, right):
    return jnp.dot(left, right, preferred_element_type=jnp.float32)


def product_left_t(left, right):
    return lax.dot_general(
        left, right, (((0,), (0,)), ((), ())), preferred_element_type=jnp.float32
    )


def product_right_t(left, right):
    return lax.dot_general(
        left, right, (((1,), (1,)), ((), ())), preferred_element_type=jnp.float32
    )


def allowed_pairs(seg_rows, live_rows):
    slot_total = seg_rows.shape[-1]
    row_pos = lax.broadcasted_iota(jnp.int32, (slot_total, slot_total), 0)
    col_pos = lax.broadcasted_iota(jnp.int32, (slot_total, slot_total), 1)
    same_seg = seg_rows[:, :, None] == seg_rows[:, None, :]
    return (same_seg & ((live_rows[:, None, :] > 0) | (row_pos == col_pos)[None]))[:, None]


def masked_scores(query_heads, key_heads, seg_rows, live_rows):
    raw_scores = (
        jnp.einsum("gqhe,gkhe->ghqk", query_heads, key_heads, preferred_element_type=jnp.float32)
        * 0.125
    )
    return jnp.where(allowed_pairs(seg_rows, live_rows), raw_scores, MASKED)


def attend_block(pieces):
    query_heads, key_heads, value_heads, seg_rows, live_rows = pieces
    scores = masked_scores(query_heads, key_heads, seg_rows, live_rows)
    row_top = jnp.max(scores, axis=-1, keepdims=True)
    exp_terms = jnp.exp(scores - row_top)
    row_total = jnp.sum(exp_terms, axis=-1, keepdims=True)
    attn_probs = (exp_terms / row_total).astype(jnp.bfloat16)
    mixed_heads = jnp.einsum(
        "ghqk,gkhe->gqhe", attn_probs, value_heads, preferred_element_type=jnp.float32
    )
    return (mixed_heads.astype(jnp.bfloat16), row_top + jnp.log(row_total))


def attend_back(pieces):
    query_heads, key_heads, value_heads, seg_rows, live_rows, log_total, grad_mixed = pieces
    scores = masked_scores(query_heads, key_heads, seg_rows, live_rows)
    attn_probs = jnp.exp(scores - log_total)
    grad_probs = jnp.einsum(
        "gqhe,gkhe->ghqk", grad_mixed, value_heads, preferred_element_type=jnp.float32
    )
    inner_sum = jnp.sum(grad_probs * attn_probs, axis=-1, keepdims=True)
    grad_scores = (attn_probs * (grad_probs - inner_sum)).astype(jnp.bfloat16)
    grad_query = (
        jnp.einsum("ghqk,gkhe->gqhe", grad_scores, key_heads, preferred_element_type=jnp.float32)
        * 0.125
    ).astype(jnp.bfloat16)
    grad_keys = (
        jnp.einsum("ghqk,gqhe->gkhe", grad_scores, query_heads, preferred_element_type=jnp.float32)
        * 0.125
    ).astype(jnp.bfloat16)
    grad_values = jnp.einsum(
        "ghqk,gqhe->gkhe",
        attn_probs.astype(jnp.bfloat16),
        grad_mixed,
        preferred_element_type=jnp.float32,
    ).astype(jnp.bfloat16)
    return (grad_query, grad_keys, grad_values)


def body(
    layer_in,
    segment_ids,
    live_mask,
    expert_ids,
    cotangent,
    norm1_gain,
    norm1_bias,
    q_weight,
    q_bias,
    k_weight,
    v_weight,
    v_bias,
    o_weight,
    o_bias,
    norm2_gain,
    norm2_bias,
    in_weight,
    in_bias,
    out_weight,
    out_bias,
):
    row_local, slot_total, width_all = layer_in.shape
    head_dim = width_all // HEADS
    group_rows = math.gcd(row_local, max(1, 512 // slot_total))
    block_total = row_local // group_rows
    token_total = row_local * slot_total
    live_tokens = jnp.sum(live_mask, axis=1)
    local_counts = jnp.stack(
        [jnp.sum(jnp.where(expert_ids == expert, live_tokens, 0)) for expert in range(3)]
    )
    counts = lax.psum(local_counts, ("wide", "narrow"))
    count_float = counts.astype(jnp.float32)
    own_count = jnp.where(expert_ids == 1, count_float[1], count_float[2])
    row_scale = (count_float[1] + count_float[2]) / (2.0 * own_count)

    def heads_blocks(values):
        return values.reshape(block_total, group_rows, slot_total, HEADS, head_dim)

    seg_blocks = segment_ids.reshape(block_total, group_rows, slot_total)
    live_blocks = live_mask.reshape(block_total, group_rows, slot_total)
    x_rows = layer_in.astype(jnp.float32).reshape(token_total, width_all)
    normed_one = norm_rows(x_rows, norm1_gain, norm1_bias).astype(jnp.bfloat16)
    wide_total, narrow_total = lax.axis_size("wide"), lax.axis_size("narrow")
    depth = wide_total // 4
    got_a, got_i, got_o = gather_all(
        depth, narrow_total, q_weight, k_weight, v_weight, o_weight, in_weight, out_weight
    )
    full_q, full_k, full_v, full_o = (
        got_a[i].reshape(width_all, width_all) for i in range(4)
    )
    full_in = got_i.reshape(4, width_all, width_all).transpose(1, 0, 2).reshape(width_all, -1)
    full_out = got_o.reshape(-1, width_all)
    query_act = (plain_product(normed_one, full_q) + q_bias).astype(jnp.bfloat16)
    key_act = plain_product(normed_one, full_k).astype(jnp.bfloat16)
    value_act = (plain_product(normed_one, full_v) + v_bias).astype(jnp.bfloat16)
    mixed_blocks, log_total = lax.map(
        attend_block,
        (
            heads_blocks(query_act),
            heads_blocks(key_act),
            heads_blocks(value_act),
            seg_blocks,
            live_blocks,
        ),
    )
    mixed_act = mixed_blocks.reshape(token_total, width_all)
    residual = x_rows + plain_product(mixed_act, full_o) + o_bias
    normed_two = norm_rows(residual, norm2_gain, norm2_bias).astype(jnp.bfloat16)
    pre_act = plain_product(normed_two, full_in) + in_bias
    hidden = gelu_exact(pre_act).astype(jnp.bfloat16)
    result = residual + plain_product(hidden, full_out) + out_bias
    layer_out = result.astype(jnp.bfloat16).reshape(row_local, slot_total, width_all)
    token_scale = (live_mask.astype(jnp.float32) * row_scale[:, None]).reshape(token_total, 1)
    grad_y = cotangent.astype(jnp.float32).reshape(token_total, width_all) * token_scale
    grad_branch = grad_y.astype(jnp.bfloat16)
    back_in, back_out = full_in, full_out
    grad_hidden = product_right_t(grad_branch, back_out)
    gelu_pull = jax.vjp(gelu_exact, pre_act)[1]
    grad_pre = gelu_pull(grad_hidden)[0].astype(jnp.bfloat16)
    out_weight_grad = product_left_t(hidden, grad_branch)
    out_bias_grad = jnp.sum(grad_branch.astype(jnp.float32), axis=0)
    in_weight_grad = product_left_t(normed_two, grad_pre)
    in_bias_grad = jnp.sum(grad_pre.astype(jnp.float32), axis=0)
    grad_normed_two = product_right_t(grad_pre, back_in)
    norm_two_pull = jax.vjp(norm_rows, residual, norm2_gain, norm2_bias)[1]
    grad_resid_norm, norm2_gain_grad, norm2_bias_grad = norm_two_pull(grad_normed_two)
    grad_resid = grad_y + grad_resid_norm
    grad_attn = grad_resid.astype(jnp.bfloat16)
    back_q, back_k, back_v, back_o = full_q, full_k, full_v, full_o
    o_weight_grad = product_left_t(mixed_act, grad_attn)
    o_bias_grad = jnp.sum(grad_attn.astype(jnp.float32), axis=0)
    grad_mixed = product_right_t(grad_attn, back_o).astype(jnp.bfloat16)
    grad_query, grad_keys, grad_values = lax.map(
        attend_back,
        (
            heads_blocks(query_act),
            heads_blocks(key_act),
            heads_blocks(value_act),
            seg_blocks,
            live_blocks,
            log_total,
            heads_blocks(grad_mixed),
        ),
    )
    grad_query = grad_query.reshape(token_total, width_all)
    grad_keys = grad_keys.reshape(token_total, width_all)
    grad_values = grad_values.reshape(token_total, width_all)
    q_weight_grad = product_left_t(normed_one, grad_query)
    q_bias_grad = jnp.sum(grad_query.astype(jnp.float32), axis=0)
    k_weight_grad = product_left_t(normed_one, grad_keys)
    v_weight_grad = product_left_t(normed_one, grad_values)
    v_bias_grad = jnp.sum(grad_values.astype(jnp.float32), axis=0)
    grad_normed_one = (
        product_right_t(grad_query, back_q)
        + product_right_t(grad_keys, back_k)
        + product_right_t(grad_values, back_v)
    )
    norm_one_pull = jax.vjp(norm_rows, x_rows, norm1_gain, norm1_bias)[1]
    grad_x_norm, norm1_gain_grad, norm1_bias_grad = norm_one_pull(grad_normed_one)
    input_grad = (
        (grad_resid + grad_x_norm).astype(jnp.bfloat16).reshape(row_local, slot_total, width_all)
    )
    summed_vectors = lax.psum(
        (
            norm1_gain_grad,
            norm1_bias_grad,
            q_bias_grad,
            v_bias_grad,
            o_bias_grad,
            norm2_gain_grad,
            norm2_bias_grad,
            in_bias_grad,
            out_bias_grad,
        ),
        ("wide", "narrow"),
    )
    rows = width_all // wide_total
    low = lambda t: t.astype(jnp.bfloat16)
    split = (depth, 2, 2)
    term_a = jnp.stack(
        [low(t) for t in (q_weight_grad, k_weight_grad, v_weight_grad, o_weight_grad)]
    ).reshape(4, *split, rows, width_all)
    term_i = (
        low(in_weight_grad)
        .reshape(width_all, 4, width_all)
        .transpose(1, 0, 2)
        .reshape(4, *split, rows, width_all)
    )
    term_o = low(out_weight_grad).reshape(*split, 4, rows, width_all)
    sum_a, sum_i, sum_o = reduce_all(depth, narrow_total, term_a, term_i, term_o)
    row_pieces = (
        sum_a[0],
        sum_a[1],
        sum_a[2],
        sum_a[3],
        sum_i.transpose(1, 0, 2).reshape(rows, -1),
        sum_o.reshape(4 * rows, width_all),
    )
    return (
        layer_out,
        input_grad,
        counts,
        summed_vectors[0],
        summed_vectors[1],
        row_pieces[0],
        summed_vectors[2],
        row_pieces[1],
        row_pieces[2],
        summed_vectors[3],
        row_pieces[3],
        summed_vectors[4],
        summed_vectors[5],
        summed_vectors[6],
        row_pieces[4],
        summed_vectors[7],
        row_pieces[5],
        summed_vectors[8],
    )


def solution(mesh):
    placed = (
        P(("wide", "narrow"), None, None),
        P(("wide", "narrow"), None),
        P(("wide", "narrow"), None),
        P(("wide", "narrow")),
        P(("wide", "narrow"), None, None),
        P(),
        P(),
        P("wide", None),
        P(),
        P("wide", None),
        P("wide", None),
        P(),
        P("wide", None),
        P(),
        P(),
        P(),
        P("wide", None),
        P(),
        P("wide", None),
        P(),
    )
    return jax.shard_map(
        body,
        mesh=mesh,
        in_specs=placed,
        out_specs=(
            P(("wide", "narrow"), None, None),
            P(("wide", "narrow"), None, None),
            P(),
            P(),
            P(),
            P("wide", None),
            P(),
            P("wide", None),
            P("wide", None),
            P(),
            P("wide", None),
            P(),
            P(),
            P(),
            P("wide", None),
            P(),
            P("wide", None),
            P(),
        ),
        check_vma=False,
    )
```

```python
import functools

import jax
import jax.numpy as jnp
from jax import lax
from jax.experimental import pallas as pl
from jax.experimental.pallas import tpu as pltpu
from jax.sharding import PartitionSpec as P

HEADS = 12
EPSILON = 1e-06
MASKED = -1e30
HALVES = 2
LAG = 2

MESH = pl.DeviceIdType.MESH
BF = jnp.bfloat16
F32 = jnp.float32


class Place:
    def __init__(self, depth, lanes):
        wide = lax.axis_index("wide")
        self.depth, self.lanes = depth, lanes
        self.n = lax.axis_index("narrow")
        self.c = lax.rem(wide, 2)
        self.x = lax.rem(wide // 2, 2)
        self.z = wide // 4
        self.y = lax.rem(self.n, 2)

    def at(self, z=None, x=None, c=None, n=None):
        z = self.z if z is None else z
        x = self.x if x is None else x
        c = self.c if c is None else c
        n = self.n if n is None else n
        return ((z * 2 + x) * 2 + c, n)

    def core(self):
        return self.at(c=1 - self.c)

    def across_x(self):
        return self.at(x=1 - self.x)

    def flip_n(self, bit):
        step = 1 << bit
        low = lax.rem(self.n // step, 2)
        return self.n + step * (1 - 2 * low)

    def across_y(self):
        return self.at(n=self.flip_n(0))

    def along_z(self, step):
        return self.at(z=lax.rem(self.z + step, self.depth))

    def greet(self):
        bits = self.lanes.bit_length() - 1
        others = [self.core(), self.across_x()]
        others += [self.at(n=self.flip_n(b)) for b in range(bits)]
        others += [self.along_z(d) for d in range(1, self.depth)]
        barrier = pltpu.get_barrier_semaphore()
        for other in others:
            pl.semaphore_signal(barrier, inc=1, device_id=other, device_id_type=MESH)
        pl.semaphore_wait(barrier, len(others))


class Sems:
    def __init__(self, send, recv):
        self.send, self.recv, self.used = send, recv, 0
        self.open = []

    def copy(self, src, dst, device):
        i = self.used
        self.used += 1
        made = pltpu.make_async_remote_copy(
            src_ref=src, dst_ref=dst, send_sem=self.send.at[i], recv_sem=self.recv.at[i],
            device_id=device, device_id_type=MESH,
        )
        made.start()
        self.open.append(made)
        return made

    def drain(self):
        for made in self.open:
            made.wait_send()
        self.open = []


def gather_part(me, sems, view):
    own = (2 * me.y, 2 * me.y + 1)
    far = (2 * (1 - me.y), 2 * (1 - me.y) + 1)
    x, c, z = me.x, me.c, me.z
    everything = slice(None)
    hops = []
    for u in own:
        hops.append([sems.copy(view(u, z, x, c), view(u, z, x, c), me.along_z(d)) for d in range(1, me.depth)])
    yield
    first = []
    for k, u in enumerate(own):
        for hop in hops[k]:
            hop.wait_recv()
        mine = view(u, everything, x, c)
        first.append((sems.copy(mine, mine, me.across_x()), sems.copy(mine, mine, me.across_y())))
        yield
    (x_a, y_a), (x_b, y_b) = first
    x_a.wait_recv()
    there = view(own[0], everything, 1 - x, c)
    y_fwd = sems.copy(there, there, me.across_y())
    block = view(own[0], everything, everything, c)
    cores = [sems.copy(block, block, me.core())]
    yield
    y_b.wait_recv()
    there = view(far[1], everything, x, c)
    x_fwd = sems.copy(there, there, me.across_x())
    yield
    x_b.wait_recv()
    block = view(own[1], everything, everything, c)
    cores.append(sems.copy(block, block, me.core()))
    yield
    y_a.wait_recv()
    y_fwd.wait_recv()
    block = view(far[0], everything, everything, c)
    cores.append(sems.copy(block, block, me.core()))
    yield
    x_fwd.wait_recv()
    block = view(far[1], everything, everything, c)
    cores.append(sems.copy(block, block, me.core()))
    yield
    for made in cores:
        made.wait_recv()
    yield


def reduce_part(me, sems, view, bufs, emit, credit, wait_credit, give_credit):
    rc, ry, rx, rz, fin, far = bufs
    a, b = 2 * me.y, 2 * me.y + 1
    ta, tb = 2 * (1 - me.y), 2 * (1 - me.y) + 1
    x, c, z = me.x, me.c, me.z
    every = slice(None)
    bits = me.lanes.bit_length() - 1

    def add(dst, *terms):
        total = dst[...].astype(F32)
        for t in terms:
            total = total + t[...].astype(F32)
        dst[...] = total.astype(BF)

    cores = {}
    if wait_credit:
        pl.semaphore_wait(credit, 1)
    for i, u in enumerate((ta, tb, b, a)):
        cores[i] = sems.copy(view(u, every, every, 1 - c), rc.at[i], me.core())
    yield
    cores[0].wait_recv()
    add(view(ta, every, every, c), rc.at[0])
    y_diag = sems.copy(view(ta, every, 1 - x, c), ry.at[0], me.across_y())
    yield
    cores[1].wait_recv()
    add(view(tb, every, every, c), rc.at[1])
    x_diag = sems.copy(view(tb, every, 1 - x, c), rx.at[0], me.across_x())
    yield
    cores[2].wait_recv()
    add(view(b, every, every, c), rc.at[2])
    x_near = sems.copy(view(b, every, 1 - x, c), rx.at[1], me.across_x())
    y_near = sems.copy(view(ta, every, x, c), ry.at[1], me.across_y())
    cores[3].wait_recv()
    add(view(a, every, every, c), rc.at[3])
    if give_credit:
        pl.semaphore_signal(credit, inc=1, device_id=me.core(), device_id_type=MESH)
    yield
    y_diag.wait_recv()
    add(view(a, every, 1 - x, c), ry.at[0])
    x_last = sems.copy(view(a, every, 1 - x, c), rx.at[2], me.across_x())
    yield
    x_diag.wait_recv()
    add(view(tb, every, x, c), rx.at[0])
    y_last = sems.copy(view(tb, every, x, c), ry.at[2], me.across_y())
    yield
    y_near.wait_recv()
    x_last.wait_recv()
    add(view(a, every, x, c), ry.at[1], rx.at[2])
    z_hops = []
    hop = []
    for d in range(1, me.depth):
        to = lax.rem(z + d, me.depth)
        hop.append(sems.copy(view(a, to, x, c), rz.at[0, d - 1], me.along_z(d)))
    z_hops.append(hop)
    yield
    x_near.wait_recv()
    y_last.wait_recv()
    add(view(b, every, x, c), rx.at[1], ry.at[2])
    hop = []
    for d in range(1, me.depth):
        to = lax.rem(z + d, me.depth)
        hop.append(sems.copy(view(b, to, x, c), rz.at[1, d - 1], me.along_z(d)))
    z_hops.append(hop)
    yield
    sent = []
    for k, u in enumerate((a, b)):
        for h in z_hops[k]:
            h.wait_recv()
        total = view(u, z, x, c)[...].astype(F32)
        for d in range(1, me.depth):
            total = total + rz[k, d - 1].astype(F32)
        fin[0, k] = total.astype(BF)
        for bit in range(1, bits):
            swap = sems.copy(fin.at[bit - 1, k], far.at[bit, k], me.at(n=me.flip_n(bit)))
            swap.wait_recv()
            total = fin[bit - 1, k].astype(F32) + far[bit, k].astype(F32)
            fin[bit, k] = total.astype(BF)
        last = max(bits - 1, 0)
        sent.append(sems.copy(fin.at[last, k], far.at[0, k], me.across_y()))
        emit(u, True, k, fin[last, k])
        yield
    for k, u in enumerate((ta, tb)):
        sent[k].wait_recv()
        emit(u, False, k, far[0, k])
        yield


def reduce_copies(depth, lanes):
    bits = lanes.bit_length() - 1
    return 4 + 6 + 2 * (depth - 1) + 2 * (bits - 1) + 2


def gather_copies(depth):
    return 2 * (depth - 1) + 4 + 2 + 4


GATHER_STEPS = 10


class Pump:
    def __init__(self, parts, steps, lag):
        self.order = []
        last = max(steps) + lag * len(parts) + 1
        for tick in range(last):
            for i, e in enumerate(parts):
                step = tick - lag * i
                if 0 <= step < steps[i]:
                    self.order.append((i, step, e))
        self.steps = steps
        self.at = 0
        self.done = {}

    def run(self, count):
        for _ in range(count):
            if self.at < len(self.order):
                i, step, e = self.order[self.at]
                self.at += 1
                next(e, None)
                self.done[i] = step + 1

    def finish(self, part):
        while self.done.get(part, 0) < self.steps[part] and self.at < len(self.order):
            self.run(1)

    def finish_all(self):
        self.run(len(self.order))


def all_sum(me, sems, first, pair, stack, emit):
    hops = [me.core(), me.across_x()]
    hops += [me.at(n=me.flip_n(b)) for b in range(me.lanes.bit_length() - 1)]
    have = first
    for i, other in enumerate(hops):
        made = sems.copy(have, pair(2 * i), other)
        yield
        made.wait_recv()
        got = pair(2 * i + 1)
        got[...] = have[...] + pair(2 * i)[...]
        have = got
    stack[me.z] = have[...]
    made = [sems.copy(have, stack.at[me.z], me.along_z(d)) for d in range(1, me.depth)]
    yield
    for m in made:
        m.wait_recv()
    total = stack[0]
    for i in range(1, me.depth):
        total = total + stack[i]
    emit(total)
    yield


def all_sum_sizes(depth, lanes):
    hops = 2 + lanes.bit_length() - 1
    return 2 * hops, hops + depth - 1, hops + 2


def stats(values):
    mean = jnp.mean(values, axis=-1, keepdims=True)
    centred = values - mean
    rstd = lax.rsqrt(jnp.mean(centred * centred, axis=-1, keepdims=True) + EPSILON)
    return centred, rstd


def dot_nn(a, b):
    return jnp.dot(a, b, preferred_element_type=F32)


def dot_nt(a, b):
    return lax.dot_general(a, b, (((1,), (1,)), ((), ())), preferred_element_type=F32)


def dot_tn(a, b):
    return lax.dot_general(a, b, (((0,), (0,)), ((), ())), preferred_element_type=F32)


def lane_halves(width=128):
    lane = lax.broadcasted_iota(jnp.int32, (1, width), 1)
    low = (lane < width // 2).astype(F32)
    return low.astype(BF), (1.0 - low).astype(BF)


def forward_kernel(
    depth, lanes, halves,
    x, seg, live, expert, g1, b1, qb, vb, ob, g2, b2, ib, yb,
    q_w, k_w, v_w, o_w, w_in, w_out,
    out, counts, tok,
    ga_h, gi_h, go_h, qkv_h, o_h, pb_h, c_h, xh_h, rstd_h, z_h, gp_h, a_h,
    ga, gi, go, qkv, o_s, pb, c_s, xh, rstd_s, z_s, gp, a_s, h_s, bias,
    cnt, cnt_pair, cnt_stack,
    local, send, recv, csend, crecv,
):
    me = Place(depth, lanes)
    rows_w, width = q_w.shape
    row_total, slots = seg.shape
    x_, c_, z_ = me.x, me.c, me.z
    part = width // halves
    blocks = w_in.shape[1] // width
    pairs_half = part // 128

    def fill(pairs, base):
        made = [pltpu.make_async_copy(s, d, local.at[base + i]) for i, (s, d) in enumerate(pairs)]
        for m in made:
            m.start()
        for m in made:
            m.wait()

    @pl.when(me.y == 0)
    def _():
        fill([(q_w, ga.at[0, z_, x_, c_]), (k_w, ga.at[1, z_, x_, c_])], 0)

    @pl.when(me.y == 1)
    def _():
        fill([(v_w, ga.at[2, z_, x_, c_]), (o_w, ga.at[3, z_, x_, c_])], 0)

    pairs = []
    for kk in range(2):
        u = 2 * me.y + kk
        pairs.append((w_in.at[:, pl.ds(pl.multiple_of(u * width, width), width)], gi.at[u, z_, x_, c_]))
        pairs.append((w_out.at[pl.ds(pl.multiple_of(u * rows_w, rows_w), rows_w), :], go.at[z_, x_, c_, u]))
    fill(pairs, 2)
    me.greet()

    parts, all_sems, views = [], [], []
    for g in range(3):
        for h in range(halves):
            cols = pl.ds(h * part, part)

            def view(u, zs, xs, cs, g=g, cols=cols):
                if g == 0:
                    return ga.at[u, zs, xs, cs, :, cols]
                if g == 1:
                    return gi.at[u, zs, xs, cs, :, cols]
                return go.at[zs, xs, cs, u, :, cols]

            sems = Sems(send.at[g * halves + h], recv.at[g * halves + h])
            all_sems.append(sems)
            parts.append(gather_part(me, sems, view))
    pump = Pump(parts, [GATHER_STEPS] * len(parts), LAG)
    stores = []
    store_at = [6]

    def store(src, dst):
        made = pltpu.make_async_copy(src, dst, local.at[store_at[0]])
        store_at[0] += 1
        made.start()
        stores.append(made)

    def ready(i):
        pump.finish(i)
        g, cols = i // halves, pl.ds((i % halves) * part, part)
        src, dst = ((ga, ga_h), (gi, gi_h), (go, go_h))[g]
        store(src.at[:, :, :, :, :, cols], dst.at[:, :, :, :, :, cols])

    pump.run(1)

    cnt[...] = jnp.zeros_like(cnt)
    for r in range(row_total):
        for e in range(3):
            hit = (expert[r] == e).astype(jnp.int32)
            cnt[e : e + 1, :] += live[r : r + 1, :] * hit
    csems = Sems(csend, crecv)

    def count_out(total):
        summed = jnp.broadcast_to(jnp.sum(total, axis=1, keepdims=True), (8, 128))
        counts[...] = summed
        one = [summed[e : e + 1, :].astype(F32) for e in range(3)]
        for r in range(row_total):
            own = jnp.zeros_like(one[0])
            for e in range(3):
                own = own + one[e] * (expert[r] == e).astype(F32)
            scale = (one[1] + one[2]) / (2.0 * own)
            rows = pl.ds(r * slots, slots)
            tok[rows, :] = tok[rows, :] * scale

    counting = all_sum(me, csems, cnt, lambda i: cnt_pair.at[i], cnt_stack, count_out)
    next(counting)

    @pl.loop(0, row_total)
    def _(r):
        rows = pl.ds(pl.multiple_of(r * slots, slots), slots)
        centred, rstd = stats(x[rows, :].astype(F32))
        a_s[rows, :] = (centred * rstd * g1[...] + b1[...]).astype(BF)

    store(a_s, a_h)

    row_pos = lax.broadcasted_iota(jnp.int32, (slots, slots), 0)
    col_pos = lax.broadcasted_iota(jnp.int32, (slots, slots), 1)
    for r in range(row_total):
        seg_row = seg[r : r + 1, :]
        live_row = live[r : r + 1, :]
        down = jnp.transpose(jnp.broadcast_to(seg_row.astype(F32), (slots, slots)))
        across = jnp.where(live_row > 0, seg_row, -1 - col_pos[0:1, :]).astype(F32)
        allowed = (down == across) | (row_pos == col_pos)
        bias[r] = jnp.where(allowed, 0.0, MASKED)
        live_down = jnp.transpose(jnp.broadcast_to(live_row.astype(F32), (128, slots)))
        tok[pl.ds(r * slots, slots), :] = live_down
        pump.run(1)
        next(counting, None)
    for _ in range(all_sum_sizes(depth, lanes)[2]):
        pump.run(1)
        next(counting, None)

    low_lanes, high_lanes = lane_halves()
    masks = (low_lanes, high_lanes)

    def project(h):
        cols = pl.ds(h * part, part)

        @pl.loop(0, row_total)
        def _(r):
            rows = pl.ds(pl.multiple_of(r * slots, slots), slots)
            a_row = a_s[rows, :]
            for u, add in enumerate((qb, None, vb)):
                weight = ga[u, :, :, :, :, cols].reshape(width, part)
                value = dot_nn(a_row, weight)
                if add is not None:
                    value = value + add[:, cols]
                qkv[u, rows, cols] = value.astype(BF)

    def attend(h, first, count):
        @pl.loop(first, first + count)
        def _(r):
            rows = pl.ds(pl.multiple_of(r * slots, slots), slots)
            for p in range(pairs_half):
                cols = pl.ds(h * part + p * 128, 128)
                q2, k2, v2 = qkv[0, rows, cols], qkv[1, rows, cols], qkv[2, rows, cols]
                mixed = jnp.zeros((slots, 128), F32)
                for i in range(2):
                    scores = dot_nt(q2 * (masks[i] * 0.125), k2) + bias[r]
                    top = jnp.max(scores, axis=-1, keepdims=True)
                    terms = jnp.exp(scores - top)
                    inv = 1.0 / jnp.sum(terms, axis=-1, keepdims=True)
                    probs = (terms * inv).astype(BF)
                    head = (h * pairs_half + p) * 2 + i
                    pb[head // 3, rows, pl.ds((head % 3) * slots, slots)] = probs
                    mixed = mixed + dot_nn(probs, v2 * masks[i])
                o_s[rows, cols] = mixed.astype(BF)

    for h in range(halves):
        ready(h)
        project(h)
        pump.run(2)
        for first in range(0, row_total, 2):
            attend(h, first, min(2, row_total - first))
            pump.run(3)
    store(qkv, qkv_h)
    store(pb, pb_h)
    store(o_s, o_h)

    @pl.loop(0, row_total)
    def _(r):
        rows = pl.ds(pl.multiple_of(r * slots, slots), slots)
        weight = ga[3].reshape(width, width)
        h_row = x[rows, :].astype(F32) + dot_nn(o_s[rows, :], weight) + ob[...]
        h_s[rows, :] = h_row
        centred, rstd = stats(h_row)
        normed = centred * rstd
        xh[rows, :] = normed.astype(BF)
        rstd_s[rows, :] = jnp.broadcast_to(rstd, (slots, 128))
        c_s[rows, :] = (normed * g2[...] + b2[...]).astype(BF)

    pump.run(3)
    store(c_s, c_h)
    store(xh, xh_h)
    store(rstd_s, rstd_h)
    for h in range(halves):
        ready(halves + h)
        cols = pl.ds(h * part, part)
        for u in range(blocks):
            @pl.loop(0, row_total // 2)
            def _(t):
                for s in range(2):
                    rows = pl.ds(pl.multiple_of((2 * t + s) * slots, slots), slots)
                    weight = gi[u, :, :, :, :, cols].reshape(width, part)
                    pre = dot_nn(c_s[rows, :], weight) + ib[:, pl.ds(u * width + h * part, part)]
                    cdf = 0.5 * (1.0 + lax.erf(pre * 0.7071067811865476))
                    z_s[u, rows, cols] = (pre * cdf).astype(BF)
                    gp[u, rows, cols] = (cdf + pre * (jnp.exp(-0.5 * pre * pre) * 0.3989422804014327)).astype(BF)

            pump.run(1)
    store(z_s, z_h)
    store(gp, gp_h)
    per = depth // 4
    for h in range(halves):
        ready(2 * halves + h)
        cols = pl.ds(h * part, part)

        @pl.loop(0, row_total)
        def _(r):
            rows = pl.ds(pl.multiple_of(r * slots, slots), slots)
            value = h_s[rows, cols] + yb[:, cols]
            for u in range(blocks):
                weight = go[u * per : (u + 1) * per, :, :, :, :, cols].reshape(width, part)
                value = value + dot_nn(z_s[u, rows, :], weight)
            out[rows, cols] = value.astype(BF)

        pump.run(2)
    pump.finish_all()
    for s in all_sems:
        s.drain()
    csems.drain()
    for m in stores:
        m.wait()


def forward_layer(depth, lanes, halves, x, seg, live, expert, vectors, weights):
    tokens, width = x.shape
    row_total, slots = seg.shape
    rows_w = weights[0].shape[0]
    ff = weights[4].shape[1]
    blocks = ff // width
    parts, per = 3 * halves, gather_copies(depth)
    pair_n, pair_c, _ = all_sum_sizes(depth, lanes)
    anyspec = pl.BlockSpec(memory_space=pl.ANY)
    vspec = pl.BlockSpec(memory_space=pltpu.VMEM)
    sspec = pl.BlockSpec(memory_space=pltpu.SMEM)
    unit = (4, depth, 2, 2, rows_w, width)
    unit_o = (depth, 2, 2, 4, rows_w, width)
    kept = [
        (unit, BF), (unit, BF), (unit_o, BF), ((3, tokens, width), BF), ((tokens, width), BF),
        ((blocks, tokens, width), BF), ((tokens, width), BF), ((tokens, width), BF), ((tokens, 128), F32),
        ((blocks, tokens, width), BF), ((blocks, tokens, width), BF), ((tokens, width), BF),
    ]
    scratch = [pltpu.VMEM(*k) for k in kept]
    scratch += [pltpu.VMEM((tokens, width), F32), pltpu.VMEM((row_total, slots, slots), F32)]
    scratch += [
        pltpu.VMEM((8, slots), jnp.int32), pltpu.VMEM((pair_n, 8, slots), jnp.int32), pltpu.VMEM((depth, 8, slots), jnp.int32),
        pltpu.SemaphoreType.DMA((32,)),
        pltpu.SemaphoreType.DMA((parts, per)), pltpu.SemaphoreType.DMA((parts, per)),
        pltpu.SemaphoreType.DMA((pair_c,)), pltpu.SemaphoreType.DMA((pair_c,)),
    ]
    return pl.pallas_call(
        functools.partial(forward_kernel, depth, lanes, halves),
        out_shape=[
            jax.ShapeDtypeStruct((tokens, width), BF), jax.ShapeDtypeStruct((8, 128), jnp.int32),
            jax.ShapeDtypeStruct((tokens, 128), F32),
        ] + [jax.ShapeDtypeStruct(*k) for k in kept],
        in_specs=[vspec] * 3 + [sspec] + [vspec] * 9 + [anyspec] * 6,
        out_specs=[vspec] * 3 + [anyspec] * len(kept),
        scratch_shapes=scratch,
        compiler_params=pltpu.CompilerParams(collective_id=0, has_side_effects=True, vmem_limit_bytes=62 << 20),
        name="forward_layer",
    )(x, seg, live, expert, *vectors, *weights)


class Flow:
    def __init__(self):
        self.live = []

    def begin(self, part):
        next(part)
        self.live.append(part)

    def run(self, count=1):
        for _ in range(count):
            kept = []
            for part in self.live:
                try:
                    next(part)
                    kept.append(part)
                except StopIteration:
                    pass
            self.live = kept

    def finish(self):
        while self.live:
            self.run()


def norm_back(grad, normed, rstd):
    mean_g = jnp.mean(grad, axis=-1, keepdims=True)
    mean_gn = jnp.mean(grad * normed, axis=-1, keepdims=True)
    return (grad - mean_g - normed * mean_gn) * rstd


def down_sum(values):
    return jnp.sum(values, axis=0, keepdims=True)


def backward_kernel(
    depth, lanes, halves, row_total,
    x_h, cot_h, tok_h, g1, g2,
    ga_h, gi_h, go_h, qkv_h, o_h, pb_h, c_h, xh_h, rstd_h, z_h, gp_h, a_h,
    dx_h, d_q, d_k, d_v, d_o, d_in, d_out,
    d_g1, d_b1, d_qb, d_vb, d_ob, d_g2, d_b2, d_ib, d_yb,
    s1, s2, s3, s4, pa, pi, po, gb, c_s, xh, dattn, dh, tok, rstd_s,
    rc, ry, rx, rz, fin, far, vec, vec_pair, vec_stack,
    local, send, recv, vsend, vrecv, credit,
):
    me = Place(depth, lanes)
    blocks, tokens, width = s1.shape
    rows_w = s3.shape[4]
    slots = tokens // row_total
    part = width // halves
    pairs_half = part // 128
    per = depth // 4
    used = [0]

    def load(src, dst):
        made = pltpu.make_async_copy(src, dst, local.at[used[0]])
        used[0] += 1
        made.start()
        return made

    l_cot = load(cot_h, dattn)
    l_tok = load(tok_h, tok)
    l_z = load(z_h, s1)
    l_out = load(go_h, s3)
    l_gp = load(gp_h, s2)
    l_c = load(c_h, c_s)
    l_in = load(gi_h, s4)
    l_xh = load(xh_h, xh)
    l_rstd = load(rstd_h, rstd_s)
    me.greet()
    vec[...] = jnp.zeros_like(vec)

    flow, all_sems = Flow(), []
    part_total = 3 * halves

    def begin(g, h, i):
        cols = pl.ds(h * part, part)

        def view(u, zs, xs, cs):
            if g == 0:
                return pa.at[u, zs, xs, cs, :, cols]
            if g == 1:
                return pi.at[u, zs, xs, cs, :, cols]
            return po.at[zs, xs, cs, u, :, cols]

        def emit(u, mine, k, value):
            value = value.astype(F32)
            if g == 0:
                even = (me.y == 0) if mine else (me.y == 1)

                @pl.when(even)
                def _():
                    (d_q, d_k)[k][:, cols] = value

                @pl.when(jnp.logical_not(even))
                def _():
                    (d_v, d_o)[k][:, cols] = value
            elif g == 1:
                d_in[:, pl.ds(pl.multiple_of(u * width + h * part, 128), part)] = value
            else:
                d_out[pl.ds(pl.multiple_of(u * rows_w, 8), rows_w), cols] = value

        sems = Sems(send.at[i], recv.at[i])
        all_sems.append(sems)
        bufs = [rc.at[i % 2]] + [t.at[i] for t in (ry, rx, rz, fin, far)]
        flow.begin(reduce_part(me, sems, view, bufs, emit, credit, i >= 2, i < part_total - 2))

    def row(r):
        return pl.ds(pl.multiple_of(r * slots, slots), slots)

    l_cot.wait()
    l_tok.wait()

    @pl.loop(0, row_total)
    def _(r):
        rows = row(r)
        value = (dattn[rows, :].astype(F32) * tok[rows, 0:1]).astype(BF)
        gb[rows, :] = value
        vec[7:8, :] += down_sum(value.astype(F32))

    l_z.wait()
    for h in range(halves):
        cols = pl.ds(h * part, part)
        for first in range(0, blocks, 2):
            @pl.loop(first, first + 2)
            def _(u):
                value = dot_tn(s1[u], gb[:, cols]).astype(BF)
                po[pl.ds(u * per, per), :, :, :, :, cols] = value.reshape(per, 2, 2, 4, rows_w, part)

            flow.run()
        begin(2, h, h)
    l_q = [load(qkv_h.at[i], s1.at[i]) for i in range(3)] + [load(a_h, s1.at[3])]

    l_out.wait()
    l_gp.wait()
    for u in range(blocks):
        @pl.loop(0, row_total)
        def _(r):
            rows = row(r)
            weight = s3[u * per : (u + 1) * per].reshape(width, width)
            value = (dot_nt(gb[rows, :], weight) * s2[u, rows, :].astype(F32)).astype(BF)
            s2[u, rows, :] = value
            vec[8 + u : 9 + u, :] += down_sum(value.astype(F32))

        flow.run()
    l_w = [load(ga_h.at[u], s3.at[:, :, :, u]) for u in range(4)]
    l_c.wait()
    for h in range(halves):
        cols = pl.ds(h * part, part)
        for first in range(0, blocks, 2):
            @pl.loop(first, first + 2)
            def _(u):
                value = dot_tn(c_s[...], s2[u, :, cols]).astype(BF)
                pi[u, :, :, :, :, cols] = value.reshape(depth, 2, 2, rows_w, part)

            flow.run()
        begin(1, h, halves + h)
    l_o = load(o_h, c_s)
    l_in.wait()
    l_xh.wait()
    l_rstd.wait()
    for first in range(row_total):
        @pl.loop(first, first + 1)
        def _(r):
            rows = row(r)
            grad = dot_nt(s2[0, rows, :], s4[0].reshape(width, width))
            for u in range(1, blocks):
                grad = grad + dot_nt(s2[u, rows, :], s4[u].reshape(width, width))
            normed = xh[rows, :].astype(F32)
            vec[5:6, :] += down_sum(grad * normed)
            vec[6:7, :] += down_sum(grad)
            value = dattn[rows, :].astype(F32) * tok[rows, 0:1]
            value = value + norm_back(grad * g2[...], normed, rstd_s[rows, 0:1])
            dh[rows, :] = value
            value = value.astype(BF)
            dattn[rows, :] = value
            vec[4:5, :] += down_sum(value.astype(F32))

        flow.run()
    l_pb = load(pb_h, s2)
    for m in l_w:
        m.wait()
    l_o.wait()
    for h in range(halves):
        cols = pl.ds(h * part, part)
        value = dot_tn(c_s[...], dattn[:, cols]).astype(BF)
        pa[3, :, :, :, :, cols] = value.reshape(depth, 2, 2, rows_w, part)
        flow.run()
    l_x = load(x_h, c_s)

    @pl.loop(0, row_total)
    def _(r):
        rows = row(r)
        gb[rows, :] = dot_nt(dattn[rows, :], s3[:, :, :, 3].reshape(width, width)).astype(BF)

    flow.run()
    for m in l_q:
        m.wait()
    l_pb.wait()
    masks = lane_halves()
    for h in range(halves):
        for first in range(0, row_total, 2):
            @pl.loop(first, first + 2)
            def _(r):
                rows = row(r)
                for p in range(pairs_half):
                    cols = pl.ds(h * part + p * 128, 128)
                    q2, k2, v2, do2 = s1[0, rows, cols], s1[1, rows, cols], s1[2, rows, cols], gb[rows, cols]
                    dq = jnp.zeros((slots, 128), F32)
                    dk, dv = dq, dq
                    for i in range(2):
                        head = (h * pairs_half + p) * 2 + i
                        probs = s2[head // 3, rows, pl.ds((head % 3) * slots, slots)]
                        do1 = do2 * masks[i]
                        dp = dot_nt(do1, v2)
                        wide = probs.astype(F32)
                        inner = jnp.sum(dp * wide, axis=-1, keepdims=True)
                        ds = (wide * (dp - inner)).astype(BF)
                        dq = dq + dot_nn(ds, k2 * masks[i])
                        dk = dk + dot_tn(ds, q2 * masks[i])
                        dv = dv + dot_tn(probs, do1)
                    dq, dv = (dq * 0.125).astype(BF), dv.astype(BF)
                    s1[0, rows, cols] = dq
                    s1[1, rows, cols] = (dk * 0.125).astype(BF)
                    s1[2, rows, cols] = dv
                    vec[2:3, cols] += down_sum(dq.astype(F32))
                    vec[3:4, cols] += down_sum(dv.astype(F32))

            flow.run()
        cols = pl.ds(h * part, part)

        @pl.loop(0, 3)
        def _(u):
            value = dot_tn(s1[3], s1[u, :, cols]).astype(BF)
            pa[u, :, :, :, :, cols] = value.reshape(depth, 2, 2, rows_w, part)

        flow.run()
        begin(0, h, 2 * halves + h)
    l_x.wait()
    for first in range(row_total):
        @pl.loop(first, first + 1)
        def _(r):
            rows = row(r)
            grad = dot_nt(s1[0, rows, :], s3[:, :, :, 0].reshape(width, width))
            for u in (1, 2):
                grad = grad + dot_nt(s1[u, rows, :], s3[:, :, :, u].reshape(width, width))
            centred, rstd = stats(c_s[rows, :].astype(F32))
            normed = centred * rstd
            vec[0:1, :] += down_sum(grad * normed)
            vec[1:2, :] += down_sum(grad)
            dattn[rows, :] = (dh[rows, :] + norm_back(grad * g1[...], normed, rstd)).astype(BF)

        flow.run()
    l_dx = load(dattn, dx_h)
    vsems = Sems(vsend, vrecv)

    def vec_out(total):
        for i, ref in enumerate((d_g1, d_b1, d_qb, d_vb, d_ob, d_g2, d_b2, d_yb)):
            ref[...] = total[i : i + 1, :]
        for u in range(blocks):
            d_ib[:, pl.ds(u * width, width)] = total[8 + u : 9 + u, :]

    flow.begin(all_sum(me, vsems, vec, lambda i: vec_pair.at[i], vec_stack, vec_out))
    flow.finish()
    for s in all_sems:
        s.drain()
    vsems.drain()
    l_dx.wait()


def backward_layer(depth, lanes, halves, row_total, x, cot, tok, g1, g2, kept):
    tokens, width = x.shape
    rows_w = kept[0].shape[4]
    ff = kept[9].shape[0] * width
    blocks = ff // width
    parts, cols = 3 * halves, width // halves
    per = reduce_copies(depth, lanes)
    bits = max(lanes.bit_length() - 1, 1)
    pair_n, pair_c, _ = all_sum_sizes(depth, lanes)
    anyspec = pl.BlockSpec(memory_space=pl.ANY)
    vspec = pl.BlockSpec(memory_space=pltpu.VMEM)
    v = lambda *s: pltpu.VMEM(s, BF)
    f = lambda *s: pltpu.VMEM(s, F32)
    o = lambda *s: jax.ShapeDtypeStruct(s, F32)
    vec_rows = 8 + -(-blocks // 8) * 8
    dma = lambda *s: pltpu.SemaphoreType.DMA(s)
    return pl.pallas_call(
        functools.partial(backward_kernel, depth, lanes, halves, row_total),
        out_shape=[jax.ShapeDtypeStruct((tokens, width), BF)]
        + [o(rows_w, width)] * 4 + [o(rows_w, ff), o(4 * rows_w, width)]
        + [o(1, width)] * 7 + [o(1, ff), o(1, width)],
        in_specs=[anyspec] * 3 + [vspec] * 2 + [anyspec] * len(kept),
        out_specs=[anyspec] + [vspec] * 15,
        scratch_shapes=[
            v(blocks, tokens, width), v(blocks, tokens, width), v(*kept[2].shape), v(*kept[1].shape),
            v(*kept[0].shape), v(*kept[1].shape), v(*kept[2].shape),
            v(tokens, width), v(tokens, width), v(tokens, width), v(tokens, width), f(tokens, width),
            f(tokens, 128), f(tokens, 128),
            v(2, 4, depth, 2, rows_w, cols), v(parts, 3, depth, rows_w, cols), v(parts, 3, depth, rows_w, cols),
            v(parts, 2, depth - 1, rows_w, cols), v(parts, bits, 2, rows_w, cols), v(parts, bits, 2, rows_w, cols),
            f(vec_rows, width), f(pair_n, vec_rows, width), f(depth, vec_rows, width),
            dma(32), dma(parts, per), dma(parts, per), dma(pair_c), dma(pair_c), pltpu.SemaphoreType.REGULAR,
        ],
        compiler_params=pltpu.CompilerParams(collective_id=1, has_side_effects=True, vmem_limit_bytes=62 << 20),
        name="backward_layer",
    )(x, cot, tok, g1, g2, *kept)


def body(
    layer_in, segment_ids, live_mask, expert_ids, cotangent,
    norm1_gain, norm1_bias, q_weight, q_bias, k_weight, v_weight, v_bias, o_weight, o_bias,
    norm2_gain, norm2_bias, in_weight, in_bias, out_weight, out_bias,
):
    row_local, slot_total, width_all = layer_in.shape
    tokens = row_local * slot_total
    depth = lax.axis_size("wide") // 4
    lanes = lax.axis_size("narrow")
    flat = lambda t: t.reshape(1, -1)
    x = layer_in.reshape(tokens, width_all)
    vectors = [flat(t) for t in (norm1_gain, norm1_bias, q_bias, v_bias, o_bias, norm2_gain, norm2_bias, in_bias, out_bias)]
    weights = (q_weight, k_weight, v_weight, o_weight, in_weight, out_weight)
    layer_out, counts, tok, *kept = forward_layer(
        depth, lanes, HALVES, x, segment_ids, live_mask, expert_ids, vectors, weights
    )
    (
        input_grad, d_q, d_k, d_v, d_o, d_in, d_out,
        d_g1, d_b1, d_qb, d_vb, d_ob, d_g2, d_b2, d_ib, d_yb,
    ) = backward_layer(
        depth, lanes, HALVES, row_local, x, cotangent.reshape(tokens, width_all), tok, vectors[0], vectors[5], kept
    )
    line = lambda t: t.reshape(-1)
    return (
        layer_out.reshape(layer_in.shape), input_grad.reshape(layer_in.shape), counts[:3, 0],
        line(d_g1), line(d_b1), d_q, line(d_qb), d_k, d_v, line(d_vb), d_o, line(d_ob),
        line(d_g2), line(d_b2), d_in, line(d_ib), d_out, line(d_yb),
    )


def solution(mesh):
    rows, row_pair = P(("wide", "narrow"), None, None), P(("wide", "narrow"), None)
    whole, split = P(), P("wide", None)
    return jax.shard_map(
        body,
        mesh=mesh,
        in_specs=(
            rows, row_pair, row_pair, P(("wide", "narrow")), rows,
            whole, whole, split, whole, split, split, whole, split, whole,
            whole, whole, split, whole, split, whole,
        ),
        out_specs=(
            rows, rows, whole, whole, whole, split, whole, split, split, whole, split, whole,
            whole, whole, split, whole, split, whole,
        ),
        check_vma=False,
    )
```

```python
import functools

import jax
import jax.numpy as jnp
from jax import lax
from jax.experimental import pallas as pl
from jax.experimental.pallas import tpu as pltpu
from jax.sharding import PartitionSpec as P

HEADS = 12
EPSILON = 1e-06
MASKED = -1e30
HALVES = 2
VMEM_BYTES = 63 << 20
TABLE = (
    (0, 0),
    (6,),
    (),
    (6,),
    (),
    (),
    (),
    (6,),
    (),
    (),
    (6, 0, 1, 1, 0, 0, 0, 0, 1, 2, 2, 1, 0, 2, 3, 3, 2, 0, 0),
    (1, 1, 1),
    (),
    (),
    (),
    (),
    (),
    (2, 2, 2),
    (1, 3, 1, 4),
    (4, 3, 1),
    (),
    (),
    (),
    (),
    (2, 2),
    (),
    (2, 3, 3, 3),
    (4, 5),
    (5,),
    (),
    (4,),
    (),
    (),
    (),
    (3, 3),
    (),
    (),
    (3,),
    (4,),
    (),
    (4, 4),
    (),
    (),
    (5,),
    (),
    (),
    (),
    (4,),
    (5,),
    (),
    (),
    (),
    (),
    (),
    (4,),
    (),
    (4,),
    (5, 5),
    (),
    (5,),
    (),
    (7, 7),
    (),
    (5, 5, 7, 5),
    (8, 8),
    (),
    (),
    (7, 7),
    (),
    (),
    (),
    (),
    (),
    (),
    (8,),
    (),
    (),
    (),
    (),
    (),
    (8, 7, 8, 7),
    (),
    (),
    (8,),
    (),
    (7, 8, 7),
    (),
    (),
    (7, 7),
    (8,),
    (9, 9, 8),
    (8,),
    (9,),
    (8,),
    (),
    (),
    (10, 10),
    (),
    (9, 9),
    (),
    (10,),
    (),
    (10, 10),
    (9,),
    (9,),
    (),
    (10, 11, 11),
    (9, 10, 11),
    (9,),
    (),
    (9,),
    (10, 11, 9, 11),
    (10,),
    (10, 12, 12),
    (10, 11),
    (12,),
    (11, 13),
    (11, 12, 12),
    (),
    (11, 13, 11),
    (12, 11, 12, 12, 13, 12, 12, 12, 13),
)

MESH = pl.DeviceIdType.MESH
BF = jnp.bfloat16
F32 = jnp.float32


class Place:
    def __init__(self, depth, lanes):
        wide = lax.axis_index("wide")
        self.depth, self.lanes = depth, lanes
        self.bits = lanes.bit_length() - 1
        self.n = lax.axis_index("narrow")
        self.c = lax.rem(wide, 2)
        self.x = lax.rem(wide // 2, 2)
        self.z = wide // 4
        self.y = lax.rem(self.n, 2)
        self.c_far, self.x_far = 1 - self.c, 1 - self.x
        self.own = (2 * self.y, 2 * self.y + 1)
        self.far = (2 - 2 * self.y, 3 - 2 * self.y)
        self.core = self.at(c=self.c_far)
        self.across_x = self.at(x=self.x_far)
        self.flips = []
        for bit in range(self.bits):
            step = 1 << bit
            low = lax.rem(self.n // step, 2)
            self.flips.append(self.at(n=self.n + step * (1 - 2 * low)))
        self.across_y = self.flips[0]
        self.z_of = [lax.rem(self.z + d, depth) for d in range(depth)]
        self.along_z = [self.at(z=t) for t in self.z_of]

    def at(self, z=None, x=None, c=None, n=None):
        z = self.z if z is None else z
        x = self.x if x is None else x
        c = self.c if c is None else c
        n = self.n if n is None else n
        return ((z * 2 + x) * 2 + c, n)

    def greet(self):
        others = [self.core, self.across_x] + self.flips + self.along_z[1:]
        barrier = pltpu.get_barrier_semaphore()
        for other in others:
            pl.semaphore_signal(barrier, inc=1, device_id=other, device_id_type=MESH)
        pl.semaphore_wait(barrier, len(others))


class Copy:
    def __init__(self, sems, i, src, dst, device):
        self.parts = sems, i, src, dst, device

    def made(self):
        sems, i, src, dst, device = self.parts
        return pltpu.make_async_remote_copy(
            src_ref=src(), dst_ref=dst(), send_sem=sems.send.at[sems.row, i], recv_sem=sems.recv.at[sems.row, i],
            device_id=device, device_id_type=MESH,
        )

    def wait_recv(self):
        self.made().wait_recv()


class Sems:
    def __init__(self, send, recv, row):
        self.send, self.recv, self.row, self.used = send, recv, row, 0
        self.open = []

    def copy(self, src, dst, device):
        copy = Copy(self, self.used, src, dst, device)
        self.used += 1
        copy.made().start()
        self.open.append(copy)
        return copy

    def drain(self):
        for copy in self.open:
            copy.made().wait_send()
        self.open = []


def slot(ref, *at):
    return ref.at[at]


def gather_part(me, sems, view):
    own, far = me.own, me.far
    x, c, z = me.x, me.c, me.z
    every = slice(None)

    def send(u, zs, xs, device):
        block = functools.partial(view, u, zs, xs, c)
        return sems.copy(block, block, device)

    hops = []
    for u in own:
        hops.append([send(u, z, x, me.along_z[d]) for d in range(1, me.depth)])
        yield
    first = []
    for k, u in enumerate(own):
        for hop in hops[k]:
            hop.wait_recv()
        first.append((send(u, every, x, me.across_x), send(u, every, x, me.across_y)))
        yield
    (x_a, y_a), (x_b, y_b) = first
    x_a.wait_recv()
    y_fwd = send(own[0], every, me.x_far, me.across_y)
    cores = [send(own[0], every, every, me.core)]
    yield
    y_b.wait_recv()
    x_fwd = send(far[1], every, x, me.across_x)
    yield
    x_b.wait_recv()
    cores.append(send(own[1], every, every, me.core))
    yield
    y_a.wait_recv()
    y_fwd.wait_recv()
    cores.append(send(far[0], every, every, me.core))
    yield
    x_fwd.wait_recv()
    cores.append(send(far[1], every, every, me.core))
    yield
    for made in cores:
        made.wait_recv()
    yield


def reduce_part(me, sems, view, bufs, emit, credit, wait_credit, give_credit):
    rc, ry, rx, rz, fin, far = [functools.partial(slot, ref, i) for ref, i in bufs]
    (a, b), (ta, tb) = me.own, me.far
    x, c, z = me.x, me.c, me.z
    xo = me.x_far
    every = slice(None)

    def add(dst, *terms):
        total = dst[...].astype(F32)
        for t in terms:
            total = total + t[...].astype(F32)
        dst[...] = total.astype(BF)

    def send(u, zs, xs, device, buf, *at, core=c):
        return sems.copy(functools.partial(view, u, zs, xs, core), functools.partial(buf, *at), device)

    if wait_credit:
        pl.semaphore_wait(credit, 1)
    cores = [send(u, every, every, me.core, rc, i, core=me.c_far) for i, u in enumerate((ta, tb, b, a))]
    yield
    cores[0].wait_recv()
    add(view(ta, every, every, c), rc(0))
    y_diag = send(ta, every, xo, me.across_y, ry, 0)
    yield
    cores[1].wait_recv()
    add(view(tb, every, every, c), rc(1))
    x_diag = send(tb, every, xo, me.across_x, rx, 0)
    yield
    cores[2].wait_recv()
    add(view(b, every, every, c), rc(2))
    x_near = send(b, every, xo, me.across_x, rx, 1)
    y_near = send(ta, every, x, me.across_y, ry, 1)
    cores[3].wait_recv()
    add(view(a, every, every, c), rc(3))
    if give_credit:
        pl.semaphore_signal(credit, inc=1, device_id=me.core, device_id_type=MESH)
    yield
    y_diag.wait_recv()
    add(view(a, every, xo, c), ry(0))
    x_last = send(a, every, xo, me.across_x, rx, 2)
    yield
    x_diag.wait_recv()
    add(view(tb, every, x, c), rx(0))
    y_last = send(tb, every, x, me.across_y, ry, 2)
    yield
    z_hops = []
    y_near.wait_recv()
    x_last.wait_recv()
    add(view(a, every, x, c), ry(1), rx(2))
    z_hops.append([send(a, me.z_of[d], x, me.along_z[d], rz, 0, d - 1) for d in range(1, me.depth)])
    yield
    x_near.wait_recv()
    y_last.wait_recv()
    add(view(b, every, x, c), rx(1), ry(2))
    z_hops.append([send(b, me.z_of[d], x, me.along_z[d], rz, 1, d - 1) for d in range(1, me.depth)])
    yield
    sent = []
    last = max(me.bits - 1, 0)
    for k, u in enumerate((a, b)):
        for hop in z_hops[k]:
            hop.wait_recv()
        total = view(u, z, x, c)[...].astype(F32)
        for d in range(1, me.depth):
            total = total + rz(k, d - 1)[...].astype(F32)
        fin(0, k)[...] = total.astype(BF)
        for bit in range(1, me.bits):
            swap = sems.copy(functools.partial(fin, bit - 1, k), functools.partial(far, bit, k), me.flips[bit])
            swap.wait_recv()
            total = fin(bit - 1, k)[...].astype(F32) + far(bit, k)[...].astype(F32)
            fin(bit, k)[...] = total.astype(BF)
        sent.append(sems.copy(functools.partial(fin, last, k), functools.partial(far, 0, k), me.across_y))
        emit(u, True, k, fin(last, k)[...])
        yield
    for k, u in enumerate((ta, tb)):
        sent[k].wait_recv()
        emit(u, False, k, far(0, k)[...])
        yield


def reduce_copies(depth, lanes):
    bits = lanes.bit_length() - 1
    return 4 + 6 + 2 * (depth - 1) + 2 * (bits - 1) + 2


class Flow:
    def __init__(self, table):
        self.table, self.at, self.parts, self.count = list(table), 0, {}, {}

    def begin(self, i, part):
        self.parts[i], self.count[i] = part, 0

    def step(self, i):
        part = self.parts.get(i)
        if part is not None:
            self.count[i] += 1
            try:
                next(part)
            except StopIteration:
                self.parts[i] = None

    def peek(self, k):
        return self.table[self.at + k] if self.at + k < len(self.table) else ()

    def pump(self):
        for i in self.peek(0):
            self.step(i)
        self.at += 1

    def finish(self, i):
        while self.parts.get(i) is not None:
            self.step(i)

    def finish_all(self):
        while any(part is not None for part in self.parts.values()):
            for i in list(self.parts):
                self.step(i)


def stepped(flow, total, work):
    @pl.loop(0, total)
    def _(i):
        work(i)
        for k in range(total):
            if flow.peek(0):
                pl.when(i == k)(flow.pump)
            else:
                flow.pump()


def gather_copies(depth):
    return 2 * (depth - 1) + 4 + 2 + 4


GATHER_STEPS = 10


def all_sum(me, sems, first, pairs, stack, emit):
    hops = [me.core, me.across_x] + me.flips
    have = functools.partial(slot, first, slice(None))
    for i, other in enumerate(hops):
        came, total = functools.partial(slot, pairs, 2 * i), functools.partial(slot, pairs, 2 * i + 1)
        made = sems.copy(have, came, other)
        yield
        made.wait_recv()
        total()[...] = have()[...] + came()[...]
        have = total
    stack[me.z] = have()[...]
    mine = functools.partial(slot, stack, me.z)
    made = [sems.copy(have, mine, me.along_z[d]) for d in range(1, me.depth)]
    yield
    for m in made:
        m.wait_recv()
    total = stack[0]
    for i in range(1, me.depth):
        total = total + stack[i]
    emit(total)
    yield


def all_sum_sizes(depth, lanes):
    hops = 2 + lanes.bit_length() - 1
    return 2 * hops, hops + depth - 1, hops + 2


class Row:
    def __init__(self, ref):
        self.ref = ref

    def __getitem__(self, at):
        if at is Ellipsis:
            return self.ref[...].reshape(1, -1)
        return self.ref[at[1]].reshape(1, -1)


def stats(values):
    mean = jnp.mean(values, axis=-1, keepdims=True)
    centred = values - mean
    rstd = lax.rsqrt(jnp.mean(centred * centred, axis=-1, keepdims=True) + EPSILON)
    return centred, rstd


def dot_nn(a, b):
    return jnp.dot(a, b, preferred_element_type=F32)


def dot_nt(a, b):
    return lax.dot_general(a, b, (((1,), (1,)), ((), ())), preferred_element_type=F32)


def dot_tn(a, b):
    return lax.dot_general(a, b, (((0,), (0,)), ((), ())), preferred_element_type=F32)


def lane_halves(width=128):
    lane = lax.broadcasted_iota(jnp.int32, (1, width), 1)
    low = (lane < width // 2).astype(F32)
    return low.astype(BF), (1.0 - low).astype(BF)


def norm_back(grad, normed, rstd):
    mean_g = jnp.mean(grad, axis=-1, keepdims=True)
    mean_gn = jnp.mean(grad * normed, axis=-1, keepdims=True)
    return (grad - mean_g - normed * mean_gn) * rstd


def down_sum(values):
    return jnp.sum(values, axis=0, keepdims=True)


def layer_kernel(
    depth, lanes, halves,
    x_h, cot_h, seg, live, expert, g1, b1, qb, vb, ob, g2, b2, ib, yb,
    q_w, k_w, v_w, o_w, w_in, w_out,
    out_h, dx_h, counts, d_q, d_k, d_v, d_o, d_in, d_out,
    d_g1, d_b1, d_qb, d_vb, d_ob, d_g2, d_b2, d_ib, d_yb,
    qkv_h, a_h, pb_h, z_h, h_h,
    ga, gi, go, s1, s2, pa, po, x_s, o_s, c_s, xh, dattn, hd, tok, rstd_s,
    rc, ry, rx, rz, fin, far, vec, vec_pair, vec_stack, cnt, cnt_pair, cnt_stack, ib_s,
    local, send, recv, rsend, rrecv, csend, crecv, vsend, vrecv, credit,
):
    me = Place(depth, lanes)
    g1, b1, qb, vb, ob, g2, b2, ib, yb = [Row(t) for t in (g1, b1, qb, vb, ob, g2, b2, ib, yb)]
    rows_w, width = q_w.shape
    row_total, slots = seg.shape
    blocks = s1.shape[0]
    x_, c_, z_ = me.x, me.c, me.z
    part = width // halves
    pairs_half = part // 128
    per = depth // 4
    part_total = 3 * halves
    used = [2]

    def move(src, dst):
        made = pltpu.make_async_copy(src, dst, local.at[used[0]])
        used[0] += 1
        made.start()
        return made

    def row(r):
        return pl.ds(pl.multiple_of(r * slots, slots), slots)

    def fill(refs):
        for k, ref in enumerate(refs):
            pltpu.make_async_copy(ref, ga.at[me.own[k], z_, x_, c_], local.at[k]).start()

    @pl.when(me.y == 0)
    def _():
        fill((q_w, k_w))

    @pl.when(me.y == 1)
    def _():
        fill((v_w, o_w))

    filled = [pltpu.make_async_copy(q_w, ga.at[me.own[k], z_, x_, c_], local.at[k]) for k in range(2)]
    for u in me.own:
        filled.append(move(w_in.at[:, pl.ds(pl.multiple_of(u * width, width), width)], gi.at[u, z_, x_, c_]))
        filled.append(move(w_out.at[pl.ds(pl.multiple_of(u * rows_w, 8), rows_w), :], go.at[z_, x_, c_, u]))
    m_x = move(x_h, x_s)
    gb = x_s
    me.greet()
    for m in filled:
        m.wait()

    def view_of(g, h, first, second, third):
        cols = pl.ds(h * part, part)

        def view(u, zs, xs, cs):
            if g == 2:
                return third.at[zs, xs, cs, u, :, cols]
            return (first, second)[g].at[u, zs, xs, cs, :, cols]

        return view

    flow, gather_sems, reduce_sems = Flow(TABLE), [], []
    for g in range(3):
        for h in range(halves):
            sems = Sems(send, recv, g * halves + h)
            gather_sems.append(sems)
            flow.begin(g * halves + h, gather_part(me, sems, view_of(g, h, ga, gi, go)))
    flow.pump()
    m_cot = move(cot_h, dattn)
    vec[...] = jnp.zeros_like(vec)
    for u in range(blocks):
        ib_s[u : u + 1, :] = ib[:, pl.ds(u * width, width)]

    def ready(i):
        flow.pump()
        flow.finish(i)

    cnt[...] = jnp.zeros_like(cnt)
    for r in range(row_total):
        for e in range(3):
            hit = (expert[r] == e).astype(jnp.int32)
            cnt[e : e + 1, :] += live[r : r + 1, :] * hit
    csems = Sems(csend, crecv, 0)

    def count_out(total):
        summed = jnp.broadcast_to(jnp.sum(total, axis=1, keepdims=True), (8, 128))
        for e in range(3):
            counts[e] = jnp.sum(total[e : e + 1, :].astype(F32)).astype(jnp.int32)
        one = [summed[e : e + 1, :].astype(F32) for e in range(3)]
        for r in range(row_total):
            own = jnp.zeros_like(one[0])
            for e in range(3):
                own = own + one[e] * (expert[r] == e).astype(F32)
            scale = (one[1] + one[2]) / (2.0 * own)
            rows = pl.ds(r * slots, slots)
            tok[rows, :] = tok[rows, :] * scale

    flow.begin(part_total, all_sum(me, csems, cnt, cnt_pair, cnt_stack, count_out))
    flow.pump()
    m_x.wait()

    def first_norm(r):
        rows = row(r)
        centred, rstd = stats(x_s[rows, :].astype(F32))
        s1[3, rows, :] = (centred * rstd * g1[...] + b1[...]).astype(BF)

    stepped(flow, row_total, first_norm)
    m_a = move(s1.at[3], a_h)

    row_pos = lax.broadcasted_iota(jnp.int32, (slots, slots), 0)
    col_pos = lax.broadcasted_iota(jnp.int32, (slots, slots), 1)
    for r in range(row_total):
        seg_row = seg[r : r + 1, :]
        live_row = live[r : r + 1, :]
        down = jnp.transpose(jnp.broadcast_to(seg_row.astype(F32), (slots, slots)))
        across = jnp.where(live_row > 0, seg_row, -1 - col_pos[0:1, :]).astype(F32)
        allowed = (down == across) | (row_pos == col_pos)
        hd[pl.ds(r * slots, slots), pl.ds(0, slots)] = jnp.where(allowed, 0.0, MASKED)
        live_down = jnp.transpose(jnp.broadcast_to(live_row.astype(F32), (128, slots)))
        tok[pl.ds(r * slots, slots), :] = live_down
        flow.pump()

    masks = lane_halves()
    for h in range(halves):
        cols_h = pl.ds(h * part, part)
        ready(h)

        def project(r):
            rows = row(r)
            a_row = s1[3, rows, :]
            for u, add in enumerate((qb, None, vb)):
                value = dot_nn(a_row, ga[u, :, :, :, :, cols_h].reshape(width, part))
                if add is not None:
                    value = value + add[:, cols_h]
                s1[u, rows, cols_h] = value.astype(BF)

        stepped(flow, row_total, project)

        def attend(r):
            rows = row(r)
            for p in range(pairs_half):
                cols = pl.ds(h * part + p * 128, 128)
                q2, k2, v2 = s1[0, rows, cols], s1[1, rows, cols], s1[2, rows, cols]
                mixed = jnp.zeros((slots, 128), F32)
                for i in range(2):
                    scores = dot_nt(q2 * (masks[i] * 0.125), k2) + hd[rows, pl.ds(0, slots)]
                    top = jnp.max(scores, axis=-1, keepdims=True)
                    terms = jnp.exp(scores - top)
                    inv = 1.0 / jnp.sum(terms, axis=-1, keepdims=True)
                    probs = (terms * inv).astype(BF)
                    head = (h * pairs_half + p) * 2 + i
                    s2[head // 3, rows, pl.ds((head % 3) * slots, slots)] = probs
                    mixed = mixed + dot_nn(probs, v2 * masks[i])
                o_s[rows, cols] = mixed.astype(BF)

        stepped(flow, row_total, attend)
    m_qkv = [move(s1.at[u], qkv_h.at[u]) for u in range(3)]
    m_pb = move(s2, pb_h)

    def second_norm(r):
        rows = row(r)
        h_row = x_s[rows, :].astype(F32) + dot_nn(o_s[rows, :], ga[3].reshape(width, width)) + ob[...]
        hd[rows, :] = h_row
        centred, rstd = stats(h_row)
        normed = centred * rstd
        xh[rows, :] = normed.astype(BF)
        rstd_s[rows, :] = jnp.broadcast_to(rstd, (slots, 128))
        c_s[rows, :] = (normed * g2[...] + b2[...]).astype(BF)

    stepped(flow, row_total, second_norm)
    m_h = move(hd, h_h)
    for m in (m_a, *m_qkv, m_pb):
        m.wait()
    pair_rows = row_total // 2
    for h in range(halves):
        cols_h = pl.ds(h * part, part)
        ready(halves + h)

        def hidden(t):
            u, first = t // pair_rows, 2 * lax.rem(t, pair_rows)
            weight = gi[u, :, :, :, :, cols_h].reshape(width, part)
            for s in range(2):
                rows = row(first + s)
                pre = dot_nn(c_s[rows, :], weight) + ib_s[pl.ds(u, 1), cols_h]
                cdf = 0.5 * (1.0 + lax.erf(pre * 0.7071067811865476))
                s1[u, rows, cols_h] = (pre * cdf).astype(BF)
                s2[u, rows, cols_h] = (cdf + pre * (jnp.exp(-0.5 * pre * pre) * 0.3989422804014327)).astype(BF)

        stepped(flow, blocks * pair_rows, hidden)
    m_z = move(s1, z_h)
    flow.finish(part_total)
    m_cot.wait()

    def begin(g, h, i):
        cols = pl.ds(h * part, part)

        def emit(u, mine, k, value):
            value = value.astype(F32)
            if g == 0:
                even = (me.y == 0) if mine else (me.y == 1)

                @pl.when(even)
                def _():
                    (d_q, d_k)[k][:, cols] = value

                @pl.when(jnp.logical_not(even))
                def _():
                    (d_v, d_o)[k][:, cols] = value
            elif g == 1:
                d_in[:, pl.ds(pl.multiple_of(u * width + h * part, 128), part)] = value
            else:
                d_out[pl.ds(pl.multiple_of(u * rows_w, 8), rows_w), cols] = value

        sems = Sems(rsend, rrecv, i)
        reduce_sems.append(sems)
        bufs = [(rc, i % 2)] + [(t, i) for t in (ry, rx, rz, fin, far)]
        base = part_total + 1
        while i >= 2 and flow.count[base + i - 2] < 4:
            flow.step(base + i - 2)
        view = view_of(g, h, pa, gi, po)
        flow.begin(base + i, reduce_part(me, sems, view, bufs, emit, credit, i >= 2, i < part_total - 2))
        flow.step(base + i)

    def scaled(r):
        rows = row(r)
        value = (dattn[rows, :].astype(F32) * tok[rows, 0:1]).astype(BF)
        gb[rows, :] = value
        vec[7:8, :] += down_sum(value.astype(F32))

    stepped(flow, row_total, scaled)
    for h in range(halves):
        cols_h = pl.ds(h * part, part)

        def out_grad(u):
            value = dot_tn(s1[u], gb[:, cols_h]).astype(BF)
            po[pl.ds(u * per, per), :, :, :, :, cols_h] = value.reshape(per, 2, 2, 4, rows_w, part)

        stepped(flow, blocks, out_grad)
        begin(2, h, h)
    m_z.wait()
    m_q = [move(qkv_h.at[u], s1.at[u]) for u in range(3)] + [move(a_h, s1.at[3])]
    for h in range(halves):
        ready(2 * halves + h)

    def hidden_grad(t):
        u, rows = t // row_total, row(lax.rem(t, row_total))
        weight = go[pl.ds(u * per, per)].reshape(width, width)
        value = (dot_nt(gb[rows, :], weight) * s2[u, rows, :].astype(F32)).astype(BF)
        s2[u, rows, :] = value
        vec[pl.ds(8 + u, 1), :] += down_sum(value.astype(F32))

    stepped(flow, blocks * row_total, hidden_grad)
    m_h.wait()

    def mid_grad(r):
        rows = row(r)
        grad = dot_nt(s2[0, rows, :], gi[0].reshape(width, width))
        for u in range(1, blocks):
            grad = grad + dot_nt(s2[u, rows, :], gi[u].reshape(width, width))
        normed = xh[rows, :].astype(F32)
        vec[5:6, :] += down_sum(grad * normed)
        vec[6:7, :] += down_sum(grad)
        value = dattn[rows, :].astype(F32) * tok[rows, 0:1]
        value = value + norm_back(grad * g2[...], normed, rstd_s[rows, 0:1])
        hd[rows, :] = value
        value = value.astype(BF)
        dattn[rows, :] = value
        vec[4:5, :] += down_sum(value.astype(F32))

    stepped(flow, row_total, mid_grad)
    for s in gather_sems:
        s.drain()
    csems.drain()
    for h in range(halves):
        cols_h = pl.ds(h * part, part)

        def in_grad(u):
            value = dot_tn(c_s[...], s2[u, :, cols_h]).astype(BF)
            gi[u, :, :, :, :, cols_h] = value.reshape(depth, 2, 2, rows_w, part)

        stepped(flow, blocks, in_grad)
        begin(1, h, halves + h)
    m_p = move(pb_h, s2)
    for h in range(halves):
        cols_h = pl.ds(h * part, part)
        value = dot_tn(o_s[...], dattn[:, cols_h]).astype(BF)
        pa[3, :, :, :, :, cols_h] = value.reshape(depth, 2, 2, rows_w, part)
        flow.pump()

    def mixed_grad(r):
        rows = row(r)
        gb[rows, :] = dot_nt(dattn[rows, :], ga[3].reshape(width, width)).astype(BF)

    stepped(flow, row_total, mixed_grad)
    for m in m_q:
        m.wait()
    m_p.wait()
    for h in range(halves):
        cols_h = pl.ds(h * part, part)

        def attend_back(r):
            rows = row(r)
            for p in range(pairs_half):
                cols = pl.ds(h * part + p * 128, 128)
                q2, k2, v2, do2 = s1[0, rows, cols], s1[1, rows, cols], s1[2, rows, cols], gb[rows, cols]
                dq = jnp.zeros((slots, 128), F32)
                dk, dv = dq, dq
                for i in range(2):
                    head = (h * pairs_half + p) * 2 + i
                    probs = s2[head // 3, rows, pl.ds((head % 3) * slots, slots)]
                    do1 = do2 * masks[i]
                    dp = dot_nt(do1, v2)
                    wide = probs.astype(F32)
                    inner = jnp.sum(dp * wide, axis=-1, keepdims=True)
                    ds = (wide * (dp - inner)).astype(BF)
                    dq = dq + dot_nn(ds, k2 * masks[i])
                    dk = dk + dot_tn(ds, q2 * masks[i])
                    dv = dv + dot_tn(probs, do1)
                dq, dv = (dq * 0.125).astype(BF), dv.astype(BF)
                s1[0, rows, cols] = dq
                s1[1, rows, cols] = (dk * 0.125).astype(BF)
                s1[2, rows, cols] = dv
                vec[2:3, cols] += down_sum(dq.astype(F32))
                vec[3:4, cols] += down_sum(dv.astype(F32))

        stepped(flow, row_total, attend_back)
        if h == halves - 1:
            m_x = move(x_h, x_s)

        def project_grad(u):
            value = dot_tn(s1[3], s1[u, :, cols_h]).astype(BF)
            pa[u, :, :, :, :, cols_h] = value.reshape(depth, 2, 2, rows_w, part)

        stepped(flow, 3, project_grad)
        begin(0, h, 2 * halves + h)
    m_z = move(z_h, s2)
    m_x.wait()

    def last_grad(r):
        rows = row(r)
        grad = dot_nt(s1[0, rows, :], ga[0].reshape(width, width))
        for u in (1, 2):
            grad = grad + dot_nt(s1[u, rows, :], ga[u].reshape(width, width))
        centred, rstd = stats(x_s[rows, :].astype(F32))
        normed = centred * rstd
        vec[0:1, :] += down_sum(grad * normed)
        vec[1:2, :] += down_sum(grad)
        dattn[rows, :] = (hd[rows, :] + norm_back(grad * g1[...], normed, rstd)).astype(BF)

    stepped(flow, row_total, last_grad)
    m_h = move(h_h, hd)
    m_dx = move(dattn, dx_h)
    vsems = Sems(vsend, vrecv, 0)

    def vec_out(total):
        for i, ref in enumerate((d_g1, d_b1, d_qb, d_vb, d_ob, d_g2, d_b2, d_yb)):
            ref[...] = total[i]
        for u in range(blocks):
            d_ib[pl.ds(u * width, width)] = total[8 + u]

    vec_part = 2 * part_total + 1
    flow.begin(vec_part, all_sum(me, vsems, vec, vec_pair, vec_stack, vec_out))
    flow.step(vec_part)
    m_z.wait()
    m_h.wait()

    def outward(r):
        rows = row(r)
        value = hd[rows, :] + yb[...]
        for u in range(blocks):
            value = value + dot_nn(s2[u, rows, :], go[u * per : (u + 1) * per].reshape(width, width))
        gb[rows, :] = value.astype(BF)

    stepped(flow, row_total, outward)
    m_out = move(gb, out_h)
    flow.pump()
    flow.finish_all()
    for s in reduce_sems:
        s.drain()
    vsems.drain()
    m_dx.wait()
    m_out.wait()


def whole_layer(depth, lanes, halves, x, cot, seg, live, expert, vectors, weights):
    tokens, width = x.shape
    row_total, slots = seg.shape
    rows_w = weights[0].shape[0]
    ff = weights[4].shape[1]
    blocks = ff // width
    parts, cols = 3 * halves, width // halves
    g_per, r_per = gather_copies(depth), reduce_copies(depth, lanes)
    bits = max(lanes.bit_length() - 1, 1)
    pair_n, pair_c, _ = all_sum_sizes(depth, lanes)
    vec_rows = 8 + -(-blocks // 8) * 8
    anyspec = pl.BlockSpec(memory_space=pl.ANY)
    vspec = pl.BlockSpec(memory_space=pltpu.VMEM)
    sspec = pl.BlockSpec(memory_space=pltpu.SMEM)
    like = jax.ShapeDtypeStruct
    unit, unit_o = (4, depth, 2, 2, rows_w, width), (depth, 2, 2, 4, rows_w, width)
    flat, wide = (tokens, width), (blocks, tokens, width)
    o = lambda *s: like(s, F32)
    v = lambda *s: pltpu.VMEM(s, BF)
    f = lambda *s: pltpu.VMEM(s, F32)
    n = lambda *s: pltpu.VMEM(s, jnp.int32)
    dma = lambda *s: pltpu.SemaphoreType.DMA(s)
    return pl.pallas_call(
        functools.partial(layer_kernel, depth, lanes, halves),
        out_shape=[like(flat, BF), like(flat, BF), like((3,), jnp.int32)]
        + [o(rows_w, width)] * 4 + [o(rows_w, ff), o(4 * rows_w, width)]
        + [o(width)] * 7 + [o(ff), o(width)]
        + [like((3, *flat), BF), like(flat, BF), like(wide, BF), like(wide, BF), like(flat, F32)],
        in_specs=[anyspec] * 2 + [vspec] * 2 + [sspec] + [vspec] * 9 + [anyspec] * 6,
        out_specs=[anyspec] * 2 + [sspec] + [vspec] * 15 + [anyspec] * 5,
        scratch_shapes=[
            v(*unit), v(*unit), v(*unit_o), v(*wide), v(*wide), v(*unit), v(*unit_o),
            v(*flat), v(*flat), v(*flat), v(*flat), v(*flat), f(*flat), f(tokens, 128), f(tokens, 128),
            v(2, 4, depth, 2, rows_w, cols), v(parts, 3, depth, rows_w, cols), v(parts, 3, depth, rows_w, cols),
            v(parts, 2, depth - 1, rows_w, cols), v(parts, bits, 2, rows_w, cols), v(parts, bits, 2, rows_w, cols),
            f(vec_rows, width), f(pair_n, vec_rows, width), f(depth, vec_rows, width),
            n(8, slots), n(pair_n, 8, slots), n(depth, 8, slots), f(-(-blocks // 8) * 8, width),
            dma(40), dma(parts, g_per), dma(parts, g_per), dma(parts, r_per), dma(parts, r_per),
            dma(1, pair_c), dma(1, pair_c), dma(1, pair_c), dma(1, pair_c), pltpu.SemaphoreType.REGULAR,
        ],
        compiler_params=pltpu.CompilerParams(collective_id=0, has_side_effects=True, vmem_limit_bytes=VMEM_BYTES),
        name="whole_layer",
    )(x, cot, seg, live, expert, *vectors, *weights)


def hand_over_kernel(count, *refs):
    sources, targets = refs[:count], refs[count + 1 : 2 * count + 1]
    stage, sem = refs[2 * count + 2 : 3 * count + 2], refs[-1]
    into = [pltpu.make_async_copy(s, m, sem.at[0, i]) for i, (s, m) in enumerate(zip(sources, stage))]
    out = [pltpu.make_async_copy(m, t, sem.at[1, i]) for i, (m, t) in enumerate(zip(stage, targets))]
    for m in into:
        m.start()
    for i in range(3):
        refs[2 * count + 1][i] = refs[count][i]
    for first, second in zip(into, out):
        first.wait()
        second.start()
    for m in out:
        m.wait()


def hand_over(counts, arrays):
    anyspec = pl.BlockSpec(memory_space=pl.ANY)
    sspec = pl.BlockSpec(memory_space=pltpu.SMEM)
    count = len(arrays)
    return pl.pallas_call(
        functools.partial(hand_over_kernel, count),
        out_shape=[jax.ShapeDtypeStruct(t.shape, t.dtype) for t in (*arrays, counts)],
        in_specs=[anyspec] * count + [sspec],
        out_specs=[anyspec] * count + [sspec],
        scratch_shapes=[pltpu.VMEM(t.shape, t.dtype) for t in arrays] + [pltpu.SemaphoreType.DMA((2, count))],
        name="hand_over",
    )(*arrays, counts)


def body(
    layer_in, segment_ids, live_mask, expert_ids, cotangent,
    norm1_gain, norm1_bias, q_weight, q_bias, k_weight, v_weight, v_bias, o_weight, o_bias,
    norm2_gain, norm2_bias, in_weight, in_bias, out_weight, out_bias,
):
    row_local, slot_total, width_all = layer_in.shape
    tokens = row_local * slot_total
    depth = lax.axis_size("wide") // 4
    lanes = lax.axis_size("narrow")
    x = layer_in.reshape(tokens, width_all)
    vectors = [norm1_gain, norm1_bias, q_bias, v_bias, o_bias, norm2_gain, norm2_bias, in_bias, out_bias]
    weights = (q_weight, k_weight, v_weight, o_weight, in_weight, out_weight)
    layer_out, input_grad, counts, *grads = whole_layer(
        depth, lanes, HALVES, x, cotangent.reshape(tokens, width_all), segment_ids, live_mask, expert_ids, vectors, weights
    )
    (
        layer_out, input_grad, d_q, d_k, d_v, d_o, d_in, d_out,
        d_g1, d_b1, d_qb, d_vb, d_ob, d_g2, d_b2, d_ib, d_yb, counts,
    ) = hand_over(counts, (layer_out, input_grad, *grads[:15]))
    return (
        layer_out.reshape(layer_in.shape), input_grad.reshape(layer_in.shape), counts,
        d_g1, d_b1, d_q, d_qb, d_k, d_v, d_vb, d_o, d_ob, d_g2, d_b2, d_in, d_ib, d_out, d_yb,
    )


def solution(mesh):
    rows, row_pair = P(("wide", "narrow"), None, None), P(("wide", "narrow"), None)
    whole, split = P(), P("wide", None)
    return jax.shard_map(
        body,
        mesh=mesh,
        in_specs=(
            rows, row_pair, row_pair, P(("wide", "narrow")), rows,
            whole, whole, split, whole, split, split, whole, split, whole,
            whole, whole, split, whole, split, whole,
        ),
        out_specs=(
            rows, rows, whole, whole, whole, split, whole, split, split, whole, split, whole,
            whole, whole, split, whole, split, whole,
        ),
        check_vma=False,
    )
```

```python
import functools

import jax
import jax.numpy as jnp
from jax import lax
from jax.experimental import pallas as pl
from jax.experimental.pallas import tpu as pltpu
from jax.sharding import PartitionSpec as P

HEADS = 12
EPSILON = 1e-06
MASKED = -1e30
GATHER_CUTS = ((2, 2, 2), (2, 2, 2), (3, 3))
REDUCE_CUTS = ((3, 3), (3, 3), (2, 2, 1, 1))
VMEM_BYTES = 63 << 20
TABLE = (
    (0, 0),
    (8,),
    (),
    (),
    (8,),
    (),
    (),
    (),
    (8,),
    (),
    (0, 1, 1, 0, 8, 0, 0, 0, 1, 2, 2, 1, 0, 2, 3, 3, 2, 0, 0),
    (1, 1, 1),
    (),
    (),
    (),
    (),
    (3, 4, 4),
    (2, 2, 2),
    (),
    (3, 1, 1, 1),
    (),
    (),
    (4, 5, 5),
    (),
    (3,),
    (2, 2),
    (3, 4, 3),
    (2,),
    (),
    (4,),
    (),
    (),
    (),
    (5, 6),
    (3, 6),
    (3, 5),
    (4, 4),
    (3, 5),
    (4,),
    (),
    (6, 7),
    (),
    (),
    (4, 7),
    (5, 5),
    (),
    (4,),
    (),
    (5, 6),
    (),
    (),
    (),
    (),
    (),
    (),
    (),
    (),
    (),
    (7,),
    (5, 6, 7, 6, 5),
    (),
    (),
    (),
    (),
    (),
    (),
    (),
    (6,),
    (),
    (),
    (),
    (),
    (),
    (),
    (),
    (),
    (6, 7, 7),
    (),
    (6, 7),
    (9, 9),
    (9, 6),
    (7, 7, 10, 10, 10, 7),
    (),
    (),
    (),
    (),
    (),
    (),
    (),
    (),
    (),
    (),
    (),
    (9, 9),
    (),
    (),
    (),
    (),
    (),
    (10, 10),
    (),
    (),
    (9, 9),
    (),
    (11, 11),
    (),
    (10, 11),
    (10, 11, 12),
    (9, 9),
    (12, 11),
    (),
    (),
    (),
    (9, 9, 10, 11, 10),
    (),
    (),
    (),
    (12,),
    (),
    (10, 12, 10),
    (12,),
    (),
    (11, 11),
    (),
    (),
    (12,),
    (13, 13, 13),
    (11, 12, 11),
    (),
    (),
    (12,),
    (),
    (11,),
    (),
    (12, 13, 13),
    (12,),
    (14, 14),
    (),
    (),
    (),
    (14, 12),
    (),
    (),
    (13,),
    (15, 15),
    (),
    (13, 15, 16, 16),
    (13, 14, 14),
    (15,),
    (13, 15),
    (13, 16, 17, 16),
    (14, 15, 16),
    (),
    (13, 14),
    (15,),
    (15, 16, 17),
    (16,),
    (),
    (14, 17, 15, 15, 16, 14, 14, 15, 16, 16, 16, 14, 17),
)

MESH = pl.DeviceIdType.MESH
BF = jnp.bfloat16
F32 = jnp.float32


class Place:
    def __init__(self, depth, lanes):
        wide = lax.axis_index("wide")
        self.depth, self.lanes = depth, lanes
        self.bits = lanes.bit_length() - 1
        self.n = lax.axis_index("narrow")
        self.c = lax.rem(wide, 2)
        self.x = lax.rem(wide // 2, 2)
        self.z = wide // 4
        self.y = lax.rem(self.n, 2)
        self.c_far, self.x_far = 1 - self.c, 1 - self.x
        self.own = (2 * self.y, 2 * self.y + 1)
        self.far = (2 - 2 * self.y, 3 - 2 * self.y)
        self.core = self.at(c=self.c_far)
        self.across_x = self.at(x=self.x_far)
        self.flips = []
        for bit in range(self.bits):
            step = 1 << bit
            low = lax.rem(self.n // step, 2)
            self.flips.append(self.at(n=self.n + step * (1 - 2 * low)))
        self.across_y = self.flips[0]
        self.z_of = [lax.rem(self.z + d, depth) for d in range(depth)]
        self.along_z = [self.at(z=t) for t in self.z_of]

    def at(self, z=None, x=None, c=None, n=None):
        z = self.z if z is None else z
        x = self.x if x is None else x
        c = self.c if c is None else c
        n = self.n if n is None else n
        return ((z * 2 + x) * 2 + c, n)

    def greet(self):
        others = [self.core, self.across_x] + self.flips + self.along_z[1:]
        barrier = pltpu.get_barrier_semaphore()
        for other in others:
            pl.semaphore_signal(barrier, inc=1, device_id=other, device_id_type=MESH)
        pl.semaphore_wait(barrier, len(others))


class Copy:
    def __init__(self, sems, i, src, dst, device):
        self.parts = sems, i, src, dst, device

    def made(self):
        sems, i, src, dst, device = self.parts
        return pltpu.make_async_remote_copy(
            src_ref=src(), dst_ref=dst(), send_sem=sems.send.at[sems.row, i], recv_sem=sems.recv.at[sems.row, i],
            device_id=device, device_id_type=MESH,
        )

    def wait_recv(self):
        self.made().wait_recv()


class Sems:
    def __init__(self, send, recv, row):
        self.send, self.recv, self.row, self.used = send, recv, row, 0
        self.open = []

    def copy(self, src, dst, device):
        copy = Copy(self, self.used, src, dst, device)
        self.used += 1
        copy.made().start()
        self.open.append(copy)
        return copy

    def drain(self):
        for copy in self.open:
            copy.made().wait_send()
        self.open = []


def slot(ref, *at):
    return ref.at[at]


def strip(ref, cols, *at):
    return ref.at[(*at, *[slice(None)] * (len(ref.shape) - 1 - len(at)), cols)]


def gather_part(me, sems, view):
    own, far = me.own, me.far
    x, c, z = me.x, me.c, me.z
    every = slice(None)

    def send(u, zs, xs, device):
        block = functools.partial(view, u, zs, xs, c)
        return sems.copy(block, block, device)

    hops = []
    for u in own:
        hops.append([send(u, z, x, me.along_z[d]) for d in range(1, me.depth)])
        yield
    first = []
    for k, u in enumerate(own):
        for hop in hops[k]:
            hop.wait_recv()
        first.append((send(u, every, x, me.across_x), send(u, every, x, me.across_y)))
        yield
    (x_a, y_a), (x_b, y_b) = first
    x_a.wait_recv()
    y_fwd = send(own[0], every, me.x_far, me.across_y)
    cores = [send(own[0], every, every, me.core)]
    yield
    y_b.wait_recv()
    x_fwd = send(far[1], every, x, me.across_x)
    yield
    x_b.wait_recv()
    cores.append(send(own[1], every, every, me.core))
    yield
    y_a.wait_recv()
    y_fwd.wait_recv()
    cores.append(send(far[0], every, every, me.core))
    yield
    x_fwd.wait_recv()
    cores.append(send(far[1], every, every, me.core))
    yield
    for made in cores:
        made.wait_recv()
    yield


def reduce_part(me, sems, view, bufs, emit, credit, wait_credit, give_credit):
    rc, ry, rx, rz, fin, far = bufs
    (a, b), (ta, tb) = me.own, me.far
    x, c, z = me.x, me.c, me.z
    xo = me.x_far
    every = slice(None)

    def add(dst, *terms):
        total = dst[...].astype(F32)
        for t in terms:
            total = total + t[...].astype(F32)
        dst[...] = total.astype(BF)

    def send(u, zs, xs, device, buf, *at, core=c):
        return sems.copy(functools.partial(view, u, zs, xs, core), functools.partial(buf, *at), device)

    if wait_credit:
        pl.semaphore_wait(credit, 1)
    cores = [send(u, every, every, me.core, rc, i, core=me.c_far) for i, u in enumerate((ta, tb, b, a))]
    yield
    cores[0].wait_recv()
    add(view(ta, every, every, c), rc(0))
    y_diag = send(ta, every, xo, me.across_y, ry, 0)
    yield
    cores[1].wait_recv()
    add(view(tb, every, every, c), rc(1))
    x_diag = send(tb, every, xo, me.across_x, rx, 0)
    yield
    cores[2].wait_recv()
    add(view(b, every, every, c), rc(2))
    x_near = send(b, every, xo, me.across_x, rx, 1)
    y_near = send(ta, every, x, me.across_y, ry, 1)
    cores[3].wait_recv()
    add(view(a, every, every, c), rc(3))
    if give_credit:
        pl.semaphore_signal(credit, inc=1, device_id=me.core, device_id_type=MESH)
    yield
    y_diag.wait_recv()
    add(view(a, every, xo, c), ry(0))
    x_last = send(a, every, xo, me.across_x, rx, 2)
    yield
    x_diag.wait_recv()
    add(view(tb, every, x, c), rx(0))
    y_last = send(tb, every, x, me.across_y, ry, 2)
    yield
    z_hops = []
    y_near.wait_recv()
    x_last.wait_recv()
    add(view(a, every, x, c), ry(1), rx(2))
    z_hops.append([send(a, me.z_of[d], x, me.along_z[d], rz, 0, d - 1) for d in range(1, me.depth)])
    yield
    x_near.wait_recv()
    y_last.wait_recv()
    add(view(b, every, x, c), rx(1), ry(2))
    z_hops.append([send(b, me.z_of[d], x, me.along_z[d], rz, 1, d - 1) for d in range(1, me.depth)])
    yield
    sent = []
    last = max(me.bits - 1, 0)
    for k, u in enumerate((a, b)):
        for hop in z_hops[k]:
            hop.wait_recv()
        total = view(u, z, x, c)[...].astype(F32)
        for d in range(1, me.depth):
            total = total + rz(k, d - 1)[...].astype(F32)
        fin(0, k)[...] = total.astype(BF)
        for bit in range(1, me.bits):
            swap = sems.copy(functools.partial(fin, bit - 1, k), functools.partial(far, bit, k), me.flips[bit])
            swap.wait_recv()
            total = fin(bit - 1, k)[...].astype(F32) + far(bit, k)[...].astype(F32)
            fin(bit, k)[...] = total.astype(BF)
        sent.append(sems.copy(functools.partial(fin, last, k), functools.partial(far, 0, k), me.across_y))
        emit(u, True, k, fin(last, k)[...])
        yield
    for k, u in enumerate((ta, tb)):
        sent[k].wait_recv()
        emit(u, False, k, far(0, k)[...])
        yield


def reduce_copies(depth, lanes):
    bits = lanes.bit_length() - 1
    return 4 + 6 + 2 * (depth - 1) + 2 * (bits - 1) + 2


class Flow:
    def __init__(self, table):
        self.table, self.at, self.parts, self.count = list(table), 0, {}, {}

    def begin(self, i, part):
        self.parts[i], self.count[i] = part, 0

    def step(self, i):
        part = self.parts.get(i)
        if part is not None:
            self.count[i] += 1
            try:
                next(part)
            except StopIteration:
                self.parts[i] = None

    def peek(self, k):
        return self.table[self.at + k] if self.at + k < len(self.table) else ()

    def pump(self):
        for i in self.peek(0):
            self.step(i)
        self.at += 1

    def finish(self, i):
        while self.parts.get(i) is not None:
            self.step(i)

    def finish_all(self):
        while any(part is not None for part in self.parts.values()):
            for i in list(self.parts):
                self.step(i)


def stepped(flow, total, work):
    @pl.loop(0, total)
    def _(i):
        work(i)
        for k in range(total):
            if flow.peek(0):
                pl.when(i == k)(flow.pump)
            else:
                flow.pump()


def gather_copies(depth):
    return 2 * (depth - 1) + 4 + 2 + 4


GATHER_STEPS = 10


def all_sum(me, sems, first, pairs, stack, emit):
    hops = [me.core, me.across_x] + me.flips
    have = functools.partial(slot, first, slice(None))
    for i, other in enumerate(hops):
        came, total = functools.partial(slot, pairs, 2 * i), functools.partial(slot, pairs, 2 * i + 1)
        made = sems.copy(have, came, other)
        yield
        made.wait_recv()
        total()[...] = have()[...] + came()[...]
        have = total
    stack[me.z] = have()[...]
    mine = functools.partial(slot, stack, me.z)
    made = [sems.copy(have, mine, me.along_z[d]) for d in range(1, me.depth)]
    yield
    for m in made:
        m.wait_recv()
    total = stack[0]
    for i in range(1, me.depth):
        total = total + stack[i]
    emit(total)
    yield


def all_sum_sizes(depth, lanes):
    hops = 2 + lanes.bit_length() - 1
    return 2 * hops, hops + depth - 1, hops + 2


class Row:
    def __init__(self, ref):
        self.ref = ref

    def __getitem__(self, at):
        if at is Ellipsis:
            return self.ref[...].reshape(1, -1)
        return self.ref[at[1]].reshape(1, -1)


def stats(values):
    mean = jnp.mean(values, axis=-1, keepdims=True)
    centred = values - mean
    rstd = lax.rsqrt(jnp.mean(centred * centred, axis=-1, keepdims=True) + EPSILON)
    return centred, rstd


def dot_nn(a, b):
    return jnp.dot(a, b, preferred_element_type=F32)


def dot_nt(a, b):
    return lax.dot_general(a, b, (((1,), (1,)), ((), ())), preferred_element_type=F32)


def dot_tn(a, b):
    return lax.dot_general(a, b, (((0,), (0,)), ((), ())), preferred_element_type=F32)


def lane_halves(width=128):
    lane = lax.broadcasted_iota(jnp.int32, (1, width), 1)
    low = (lane < width // 2).astype(F32)
    return low.astype(BF), (1.0 - low).astype(BF)


def norm_back(grad, normed, rstd):
    mean_g = jnp.mean(grad, axis=-1, keepdims=True)
    mean_gn = jnp.mean(grad * normed, axis=-1, keepdims=True)
    return (grad - mean_g - normed * mean_gn) * rstd


def down_sum(values):
    return jnp.sum(values, axis=0, keepdims=True)


def cut(sizes):
    return [pl.ds(128 * sum(sizes[:i]), 128 * size) for i, size in enumerate(sizes)]


def layer_kernel(
    depth, lanes,
    x_h, cot_h, seg, live, expert, g1, b1, qb, vb, ob, g2, b2, ib, yb,
    q_w, k_w, v_w, o_w, w_in, w_out,
    out_h, dx_h, counts, d_q, d_k, d_v, d_o, d_in, d_out,
    d_g1, d_b1, d_qb, d_vb, d_ob, d_g2, d_b2, d_ib, d_yb,
    qkv_h, a_h, pb_h, z_h, h_h, go_h,
    ga, gi, go, s1, s2, pa, po, x_s, o_s, c_s, xh, dattn, hd, tok, rstd_s,
    rc, ry, rx, rz, fin, far, vec, vec_pair, vec_stack, cnt, cnt_pair, cnt_stack, ib_s, yb_s,
    local, send, recv, rsend, rrecv, csend, crecv, vsend, vrecv, credit,
):
    me = Place(depth, lanes)
    g1, b1, qb, vb, ob, g2, b2, ib, yb = [Row(t) for t in (g1, b1, qb, vb, ob, g2, b2, ib, yb)]
    rows_w, width = q_w.shape
    row_total, slots = seg.shape
    blocks = s1.shape[0]
    x_, c_, z_ = me.x, me.c, me.z
    per = depth // 4
    gathered, reduced = [[cut(sizes) for sizes in cuts] for cuts in (GATHER_CUTS, REDUCE_CUTS)]
    count_part = sum(len(cuts) for cuts in gathered)
    reduce_base = count_part + 1
    reduce_total = sum(len(cuts) for cuts in reduced)
    vec_part = reduce_base + reduce_total
    used = [2]

    def move(src, dst):
        made = pltpu.make_async_copy(src, dst, local.at[used[0]])
        used[0] += 1
        made.start()
        return made

    def row(r):
        return pl.ds(pl.multiple_of(r * slots, slots), slots)

    def fill(refs):
        for k, ref in enumerate(refs):
            pltpu.make_async_copy(ref, ga.at[me.own[k], z_, x_, c_], local.at[k]).start()

    @pl.when(me.y == 0)
    def _():
        fill((q_w, k_w))

    @pl.when(me.y == 1)
    def _():
        fill((v_w, o_w))

    filled = [pltpu.make_async_copy(q_w, ga.at[me.own[k], z_, x_, c_], local.at[k]) for k in range(2)]
    for u in me.own:
        filled.append(move(w_in.at[:, pl.ds(pl.multiple_of(u * width, width), width)], gi.at[u, z_, x_, c_]))
        filled.append(move(w_out.at[pl.ds(pl.multiple_of(u * rows_w, 8), rows_w), :], go.at[z_, x_, c_, u]))
    m_x = move(x_h, x_s)
    gb = x_s
    me.greet()
    for m in filled:
        m.wait()

    def view_of(g, cols, first, second, third):
        def view(u, zs, xs, cs):
            if g > 1:
                return third.at[zs, xs, cs, u, :, cols]
            return (first, second)[g].at[u, zs, xs, cs, :, cols]

        return view

    flow, gather_sems, reduce_sems = Flow(TABLE), [], []
    for g in range(3):
        for cols_g in gathered[g]:
            sems = Sems(send, recv, len(gather_sems))
            flow.begin(len(gather_sems), gather_part(me, sems, view_of(g, cols_g, ga, gi, go)))
            gather_sems.append(sems)
    flow.pump()
    m_cot = move(cot_h, dattn)
    vec[...] = jnp.zeros_like(vec)
    for u in range(blocks):
        ib_s[u : u + 1, :] = ib[:, pl.ds(u * width, width)]
    yb_s[0:1, :] = yb[...]

    arrived = [0]

    def ready():
        flow.pump()
        flow.finish(arrived[0])
        arrived[0] += 1

    cnt[...] = jnp.zeros_like(cnt)
    for r in range(row_total):
        for e in range(3):
            hit = (expert[r] == e).astype(jnp.int32)
            cnt[e : e + 1, :] += live[r : r + 1, :] * hit
    csems = Sems(csend, crecv, 0)

    def count_out(total):
        summed = jnp.broadcast_to(jnp.sum(total, axis=1, keepdims=True), (8, 128))
        for e in range(3):
            counts[e] = jnp.sum(total[e : e + 1, :].astype(F32)).astype(jnp.int32)
        one = [summed[e : e + 1, :].astype(F32) for e in range(3)]
        for r in range(row_total):
            own = jnp.zeros_like(one[0])
            for e in range(3):
                own = own + one[e] * (expert[r] == e).astype(F32)
            scale = (one[1] + one[2]) / (2.0 * own)
            rows = pl.ds(r * slots, slots)
            tok[rows, :] = tok[rows, :] * scale

    flow.begin(count_part, all_sum(me, csems, cnt, cnt_pair, cnt_stack, count_out))
    flow.pump()
    m_x.wait()

    def first_norm(r):
        rows = row(r)
        centred, rstd = stats(x_s[rows, :].astype(F32))
        s1[3, rows, :] = (centred * rstd * g1[...] + b1[...]).astype(BF)

    stepped(flow, row_total, first_norm)
    m_a = move(s1.at[3], a_h)

    row_pos = lax.broadcasted_iota(jnp.int32, (slots, slots), 0)
    col_pos = lax.broadcasted_iota(jnp.int32, (slots, slots), 1)
    for r in range(row_total):
        seg_row = seg[r : r + 1, :]
        live_row = live[r : r + 1, :]
        down = jnp.transpose(jnp.broadcast_to(seg_row.astype(F32), (slots, slots)))
        across = jnp.where(live_row > 0, seg_row, -1 - col_pos[0:1, :]).astype(F32)
        allowed = (down == across) | (row_pos == col_pos)
        hd[pl.ds(r * slots, slots), pl.ds(0, slots)] = jnp.where(allowed, 0.0, MASKED)
        live_down = jnp.transpose(jnp.broadcast_to(live_row.astype(F32), (128, slots)))
        tok[pl.ds(r * slots, slots), :] = live_down
        flow.pump()

    masks = lane_halves()
    for cols_h in gathered[0]:
        ready()

        def project(r, cols_h=cols_h):
            rows = row(r)
            a_row = s1[3, rows, :]
            for u, add in enumerate((qb, None, vb)):
                value = dot_nn(a_row, ga[u, :, :, :, :, cols_h].reshape(width, cols_h.size))
                if add is not None:
                    value = value + add[:, cols_h]
                s1[u, rows, cols_h] = value.astype(BF)

        stepped(flow, row_total, project)

        def attend(r, cols_h=cols_h):
            rows = row(r)
            for start in range(cols_h.start, cols_h.start + cols_h.size, 128):
                cols = pl.ds(start, 128)
                q2, k2, v2 = s1[0, rows, cols], s1[1, rows, cols], s1[2, rows, cols]
                mixed = jnp.zeros((slots, 128), F32)
                for i in range(2):
                    scores = dot_nt(q2 * (masks[i] * 0.125), k2) + hd[rows, pl.ds(0, slots)]
                    top = jnp.max(scores, axis=-1, keepdims=True)
                    terms = jnp.exp(scores - top)
                    inv = 1.0 / jnp.sum(terms, axis=-1, keepdims=True)
                    probs = (terms * inv).astype(BF)
                    head = start // 64 + i
                    s2[head // 3, rows, pl.ds((head % 3) * slots, slots)] = probs
                    mixed = mixed + dot_nn(probs, v2 * masks[i])
                o_s[rows, cols] = mixed.astype(BF)

        stepped(flow, row_total, attend)
    m_qkv = [move(s1.at[u], qkv_h.at[u]) for u in range(3)]
    m_pb = move(s2, pb_h)

    def second_norm(r):
        rows = row(r)
        h_row = x_s[rows, :].astype(F32) + dot_nn(o_s[rows, :], ga[3].reshape(width, width)) + ob[...]
        hd[rows, :] = h_row
        centred, rstd = stats(h_row)
        normed = centred * rstd
        xh[rows, :] = normed.astype(BF)
        rstd_s[rows, :] = jnp.broadcast_to(rstd, (slots, 128))
        c_s[rows, :] = (normed * g2[...] + b2[...]).astype(BF)

    stepped(flow, row_total, second_norm)
    m_h = move(hd, h_h)
    for m in (m_a, *m_qkv, m_pb):
        m.wait()
    pair_rows = row_total // 2
    for cols_h in gathered[1]:
        ready()

        def hidden(t, cols_h=cols_h):
            u, first = t // pair_rows, 2 * lax.rem(t, pair_rows)
            weight = gi[u, :, :, :, :, cols_h].reshape(width, cols_h.size)
            for s in range(2):
                rows = row(first + s)
                pre = dot_nn(c_s[rows, :], weight) + ib_s[pl.ds(u, 1), cols_h]
                cdf = 0.5 * (1.0 + lax.erf(pre * 0.7071067811865476))
                s1[u, rows, cols_h] = (pre * cdf).astype(BF)
                s2[u, rows, cols_h] = (cdf + pre * (jnp.exp(-0.5 * pre * pre) * 0.3989422804014327)).astype(BF)

        stepped(flow, blocks * pair_rows, hidden)
    m_z = move(s1, z_h)
    flow.finish(count_part)
    m_cot.wait()

    def begin(g, cols):
        i = len(reduce_sems)
        at = pl.ds((2 - g) * width + cols.start, cols.size)

        def emit(u, mine, k, value):
            value = value.astype(F32)
            if g == 0:
                even = (me.y == 0) if mine else (me.y == 1)

                @pl.when(even)
                def _():
                    (d_q, d_k)[k][:, cols] = value

                @pl.when(jnp.logical_not(even))
                def _():
                    (d_v, d_o)[k][:, cols] = value
            elif g == 1:
                d_in[:, pl.ds(pl.multiple_of(u * width + cols.start, 128), cols.size)] = value
            else:
                d_out[pl.ds(pl.multiple_of(u * rows_w, 8), rows_w), cols] = value

        sems = Sems(rsend, rrecv, i)
        reduce_sems.append(sems)
        bufs = [functools.partial(strip, rc, pl.ds(0, cols.size), i % 2)]
        bufs += [functools.partial(strip, t, at) for t in (ry, rx, rz, fin, far)]
        while i >= 2 and flow.count[reduce_base + i - 2] < 4:
            flow.step(reduce_base + i - 2)
        view = view_of(g, cols, pa, None, po) if g != 1 else view_of(2, cols, None, None, go)
        give = i < reduce_total - 2
        flow.begin(reduce_base + i, reduce_part(me, sems, view, bufs, emit, credit, i >= 2, give))
        flow.step(reduce_base + i)

    def scaled(r):
        rows = row(r)
        value = (dattn[rows, :].astype(F32) * tok[rows, 0:1]).astype(BF)
        gb[rows, :] = value
        vec[7:8, :] += down_sum(value.astype(F32))

    stepped(flow, row_total, scaled)
    for cols_h in reduced[0]:
        def out_grad(u, cols_h=cols_h):
            value = dot_tn(s1[u], gb[:, cols_h]).astype(BF)
            po[pl.ds(u * per, per), :, :, :, :, cols_h] = value.reshape(per, 2, 2, 4, rows_w, cols_h.size)

        stepped(flow, blocks, out_grad)
        begin(2, cols_h)
    m_z.wait()
    m_q = [move(qkv_h.at[u], s1.at[u]) for u in range(3)] + [move(a_h, s1.at[3])]
    for _ in gathered[2]:
        ready()
    m_go = move(go, go_h)

    def hidden_grad(t):
        u, rows = t // row_total, row(lax.rem(t, row_total))
        weight = go[pl.ds(u * per, per)].reshape(width, width)
        value = (dot_nt(gb[rows, :], weight) * s2[u, rows, :].astype(F32)).astype(BF)
        s2[u, rows, :] = value
        vec[pl.ds(8 + u, 1), :] += down_sum(value.astype(F32))

    stepped(flow, blocks * row_total, hidden_grad)
    for s in gather_sems:
        s.drain()
    csems.drain()
    m_go.wait()
    for cols_h in reduced[1]:
        def in_grad(u, cols_h=cols_h):
            value = dot_tn(c_s[...], s2[u, :, cols_h]).astype(BF)
            go[:, :, :, u, :, cols_h] = value.reshape(depth, 2, 2, rows_w, cols_h.size)

        stepped(flow, blocks, in_grad)
        begin(1, cols_h)
    m_h.wait()

    def mid_grad(r):
        rows = row(r)
        grad = dot_nt(s2[0, rows, :], gi[0].reshape(width, width))
        for u in range(1, blocks):
            grad = grad + dot_nt(s2[u, rows, :], gi[u].reshape(width, width))
        normed = xh[rows, :].astype(F32)
        vec[5:6, :] += down_sum(grad * normed)
        vec[6:7, :] += down_sum(grad)
        value = dattn[rows, :].astype(F32) * tok[rows, 0:1]
        value = value + norm_back(grad * g2[...], normed, rstd_s[rows, 0:1])
        hd[rows, :] = value
        value = value.astype(BF)
        dattn[rows, :] = value
        vec[4:5, :] += down_sum(value.astype(F32))

    stepped(flow, row_total, mid_grad)
    m_p = move(pb_h, s2)
    for cols_h in reduced[2]:
        value = dot_tn(o_s[...], dattn[:, cols_h]).astype(BF)
        pa[3, :, :, :, :, cols_h] = value.reshape(depth, 2, 2, rows_w, cols_h.size)
        flow.pump()

    def mixed_grad(r):
        rows = row(r)
        gb[rows, :] = dot_nt(dattn[rows, :], ga[3].reshape(width, width)).astype(BF)

    stepped(flow, row_total, mixed_grad)
    for m in m_q:
        m.wait()
    m_p.wait()
    for cols_h in reduced[2]:
        def attend_back(r, cols_h=cols_h):
            rows = row(r)
            for start in range(cols_h.start, cols_h.start + cols_h.size, 128):
                cols = pl.ds(start, 128)
                q2, k2, v2, do2 = s1[0, rows, cols], s1[1, rows, cols], s1[2, rows, cols], gb[rows, cols]
                dq = jnp.zeros((slots, 128), F32)
                dk, dv = dq, dq
                both = do2.astype(F32) * o_s[rows, cols].astype(F32)
                for i in range(2):
                    head = start // 64 + i
                    probs = s2[head // 3, rows, pl.ds((head % 3) * slots, slots)]
                    do1 = do2 * masks[i]
                    dp = dot_nt(do1, v2)
                    wide = probs.astype(F32)
                    inner = jnp.sum(both * masks[i].astype(F32), axis=-1, keepdims=True)
                    ds = (wide * (dp - inner)).astype(BF)
                    dq = dq + dot_nn(ds, k2 * masks[i])
                    dk = dk + dot_tn(ds, q2 * masks[i])
                    dv = dv + dot_tn(probs, do1)
                dq, dv = (dq * 0.125).astype(BF), dv.astype(BF)
                s1[0, rows, cols] = dq
                s1[1, rows, cols] = (dk * 0.125).astype(BF)
                s1[2, rows, cols] = dv
                vec[2:3, cols] += down_sum(dq.astype(F32))
                vec[3:4, cols] += down_sum(dv.astype(F32))

        stepped(flow, row_total, attend_back)
        if cols_h is reduced[2][-1]:
            m_x = move(x_h, x_s)

        def project_grad(u, cols_h=cols_h):
            value = dot_tn(s1[3], s1[u, :, cols_h]).astype(BF)
            pa[u, :, :, :, :, cols_h] = value.reshape(depth, 2, 2, rows_w, cols_h.size)

        stepped(flow, 3, project_grad)
        begin(0, cols_h)
    m_z = move(z_h, s2)
    for i, sems in enumerate(reduce_sems):
        if len(reduced[0]) <= i < len(reduced[0]) + len(reduced[1]):
            flow.finish(reduce_base + i)
            sems.drain()
    m_go = move(go_h, go)
    m_x.wait()

    def last_grad(r):
        rows = row(r)
        grad = dot_nt(s1[0, rows, :], ga[0].reshape(width, width))
        for u in (1, 2):
            grad = grad + dot_nt(s1[u, rows, :], ga[u].reshape(width, width))
        centred, rstd = stats(x_s[rows, :].astype(F32))
        normed = centred * rstd
        vec[0:1, :] += down_sum(grad * normed)
        vec[1:2, :] += down_sum(grad)
        dattn[rows, :] = (hd[rows, :] + norm_back(grad * g1[...], normed, rstd)).astype(BF)

    stepped(flow, row_total, last_grad)
    m_h = move(h_h, hd)
    m_dx = move(dattn, dx_h)
    vsems = Sems(vsend, vrecv, 0)

    def vec_out(total):
        for i, ref in enumerate((d_g1, d_b1, d_qb, d_vb, d_ob, d_g2, d_b2, d_yb)):
            ref[...] = total[i]
        for u in range(blocks):
            d_ib[pl.ds(u * width, width)] = total[8 + u]

    flow.begin(vec_part, all_sum(me, vsems, vec, vec_pair, vec_stack, vec_out))
    flow.step(vec_part)
    m_z.wait()
    m_h.wait()
    m_go.wait()

    half = width // 2

    def outward(t):
        rows, cols = row(t // 2), pl.ds(pl.multiple_of(lax.rem(t, 2) * half, half), half)
        value = hd[rows, cols] + yb_s[0:1, cols]
        for u in range(blocks):
            value = value + dot_nn(s2[u, rows, :], go[u * per : (u + 1) * per, :, :, :, :, cols].reshape(width, half))
        gb[rows, cols] = value.astype(BF)

    stepped(flow, 2 * row_total, outward)
    m_out = move(gb, out_h)
    flow.pump()
    flow.finish_all()
    for s in reduce_sems:
        s.drain()
    vsems.drain()
    m_dx.wait()
    m_out.wait()


def whole_layer(depth, lanes, x, cot, seg, live, expert, vectors, weights):
    tokens, width = x.shape
    row_total, slots = seg.shape
    rows_w = weights[0].shape[0]
    ff = weights[4].shape[1]
    blocks = ff // width
    g_parts, r_parts = [sum(len(sizes) for sizes in cuts) for cuts in (GATHER_CUTS, REDUCE_CUTS)]
    cols = 128 * max(max(sizes) for sizes in REDUCE_CUTS)
    g_per, r_per = gather_copies(depth), reduce_copies(depth, lanes)
    bits = max(lanes.bit_length() - 1, 1)
    pair_n, pair_c, _ = all_sum_sizes(depth, lanes)
    vec_rows = 8 + -(-blocks // 8) * 8
    anyspec = pl.BlockSpec(memory_space=pl.ANY)
    vspec = pl.BlockSpec(memory_space=pltpu.VMEM)
    sspec = pl.BlockSpec(memory_space=pltpu.SMEM)
    like = jax.ShapeDtypeStruct
    unit, unit_o = (4, depth, 2, 2, rows_w, width), (depth, 2, 2, 4, rows_w, width)
    flat, wide = (tokens, width), (blocks, tokens, width)
    o = lambda *s: like(s, F32)
    v = lambda *s: pltpu.VMEM(s, BF)
    f = lambda *s: pltpu.VMEM(s, F32)
    n = lambda *s: pltpu.VMEM(s, jnp.int32)
    dma = lambda *s: pltpu.SemaphoreType.DMA(s)
    return pl.pallas_call(
        functools.partial(layer_kernel, depth, lanes),
        out_shape=[like(flat, BF), like(flat, BF), like((3,), jnp.int32)]
        + [o(rows_w, width)] * 4 + [o(rows_w, ff), o(4 * rows_w, width)]
        + [o(width)] * 7 + [o(ff), o(width)]
        + [like((3, *flat), BF), like(flat, BF), like(wide, BF), like(wide, BF), like(flat, F32), like(unit_o, BF)],
        in_specs=[anyspec] * 2 + [vspec] * 2 + [sspec] + [vspec] * 9 + [anyspec] * 6,
        out_specs=[anyspec] * 2 + [sspec] + [vspec] * 15 + [anyspec] * 6,
        scratch_shapes=[
            v(*unit), v(*unit), v(*unit_o), v(*wide), v(*wide), v(*unit), v(*unit_o),
            v(*flat), v(*flat), v(*flat), v(*flat), v(*flat), f(*flat), f(tokens, 128), f(tokens, 128),
            v(2, 4, depth, 2, rows_w, cols), v(3, depth, rows_w, 3 * width), v(3, depth, rows_w, 3 * width),
            v(2, depth - 1, rows_w, 3 * width), v(bits, 2, rows_w, 3 * width), v(bits, 2, rows_w, 3 * width),
            f(vec_rows, width), f(pair_n, vec_rows, width), f(depth, vec_rows, width),
            n(8, slots), n(pair_n, 8, slots), n(depth, 8, slots), f(-(-blocks // 8) * 8, width), f(8, width),
            dma(40), dma(g_parts, g_per), dma(g_parts, g_per), dma(r_parts, r_per), dma(r_parts, r_per),
            dma(1, pair_c), dma(1, pair_c), dma(1, pair_c), dma(1, pair_c), pltpu.SemaphoreType.REGULAR,
        ],
        compiler_params=pltpu.CompilerParams(collective_id=0, has_side_effects=True, vmem_limit_bytes=VMEM_BYTES),
        name="whole_layer",
    )(x, cot, seg, live, expert, *vectors, *weights)


def hand_over_kernel(count, *refs):
    sources, targets = refs[:count], refs[count + 1 : 2 * count + 1]
    stage, sem = refs[2 * count + 2 : 3 * count + 2], refs[-1]
    into = [pltpu.make_async_copy(s, m, sem.at[0, i]) for i, (s, m) in enumerate(zip(sources, stage))]
    out = [pltpu.make_async_copy(m, t, sem.at[1, i]) for i, (m, t) in enumerate(zip(stage, targets))]
    for m in into:
        m.start()
    for i in range(3):
        refs[2 * count + 1][i] = refs[count][i]
    for first, second in zip(into, out):
        first.wait()
        second.start()
    for m in out:
        m.wait()


def hand_over(counts, arrays):
    anyspec = pl.BlockSpec(memory_space=pl.ANY)
    sspec = pl.BlockSpec(memory_space=pltpu.SMEM)
    count = len(arrays)
    return pl.pallas_call(
        functools.partial(hand_over_kernel, count),
        out_shape=[jax.ShapeDtypeStruct(t.shape, t.dtype) for t in (*arrays, counts)],
        in_specs=[anyspec] * count + [sspec],
        out_specs=[anyspec] * count + [sspec],
        scratch_shapes=[pltpu.VMEM(t.shape, t.dtype) for t in arrays] + [pltpu.SemaphoreType.DMA((2, count))],
        name="hand_over",
    )(*arrays, counts)


def body(
    layer_in, segment_ids, live_mask, expert_ids, cotangent,
    norm1_gain, norm1_bias, q_weight, q_bias, k_weight, v_weight, v_bias, o_weight, o_bias,
    norm2_gain, norm2_bias, in_weight, in_bias, out_weight, out_bias,
):
    row_local, slot_total, width_all = layer_in.shape
    tokens = row_local * slot_total
    depth = lax.axis_size("wide") // 4
    lanes = lax.axis_size("narrow")
    x = layer_in.reshape(tokens, width_all)
    vectors = [norm1_gain, norm1_bias, q_bias, v_bias, o_bias, norm2_gain, norm2_bias, in_bias, out_bias]
    weights = (q_weight, k_weight, v_weight, o_weight, in_weight, out_weight)
    layer_out, input_grad, counts, *grads = whole_layer(
        depth, lanes, x, cotangent.reshape(tokens, width_all), segment_ids, live_mask, expert_ids, vectors, weights
    )
    (
        layer_out, input_grad, d_q, d_k, d_v, d_o, d_in, d_out,
        d_g1, d_b1, d_qb, d_vb, d_ob, d_g2, d_b2, d_ib, d_yb, counts,
    ) = hand_over(counts, (layer_out, input_grad, *grads[:15]))
    return (
        layer_out.reshape(layer_in.shape), input_grad.reshape(layer_in.shape), counts,
        d_g1, d_b1, d_q, d_qb, d_k, d_v, d_vb, d_o, d_ob, d_g2, d_b2, d_in, d_ib, d_out, d_yb,
    )


def solution(mesh):
    rows, row_pair = P(("wide", "narrow"), None, None), P(("wide", "narrow"), None)
    whole, split = P(), P("wide", None)
    return jax.shard_map(
        body,
        mesh=mesh,
        in_specs=(
            rows, row_pair, row_pair, P(("wide", "narrow")), rows,
            whole, whole, split, whole, split, split, whole, split, whole,
            whole, whole, split, whole, split, whole,
        ),
        out_specs=(
            rows, rows, whole, whole, whole, split, whole, split, split, whole, split, whole,
            whole, whole, split, whole, split, whole,
        ),
        check_vma=False,
    )
```

```python
import functools

import jax
import jax.numpy as jnp
from jax import lax
from jax.experimental import pallas as pl
from jax.experimental.pallas import tpu as pltpu
from jax.sharding import PartitionSpec as P

HEADS = 12
EPSILON = 1e-06
MASKED = -1e30
GATHER_CUTS = ((2, 2, 2), (2, 2, 2), (3, 3))
REDUCE_CUTS = ((3, 3), (3, 3), (2, 2, 1, 1))
VMEM_BYTES = 63 << 20
TABLE = (
    (0, 0),
    (8,),
    (),
    (),
    (),
    (8,),
    (),
    (),
    (),
    (),
    (8, 0, 1, 1, 0, 8, 0, 0, 0, 1, 2, 2, 1, 0, 2, 3, 3, 0, 2, 1, 1, 1, 0),
    (),
    (),
    (),
    (),
    (),
    (3, 4),
    (2, 4),
    (1, 2, 1, 2),
    (3, 1),
    (3,),
    (),
    (),
    (4, 5),
    (2, 5),
    (2, 3, 3),
    (4,),
    (4, 3, 2),
    (),
    (),
    (),
    (5, 6),
    (),
    (3, 6),
    (4, 4),
    (3, 5),
    (4, 5),
    (),
    (6, 7),
    (4,),
    (7, 5, 5),
    (),
    (),
    (),
    (4,),
    (6,),
    (5,),
    (),
    (),
    (),
    (),
    (6,),
    (),
    (),
    (),
    (),
    (5,),
    (7,),
    (),
    (7, 5),
    (6, 6),
    (),
    (),
    (),
    (),
    (),
    (),
    (),
    (6,),
    (),
    (),
    (),
    (),
    (),
    (),
    (7, 7),
    (7,),
    (6,),
    (),
    (),
    (9, 9, 6),
    (7, 7, 9, 7),
    (),
    (10, 10),
    (),
    (),
    (),
    (),
    (9, 9),
    (),
    (),
    (),
    (),
    (),
    (10,),
    (),
    (),
    (),
    (10, 10),
    (),
    (9, 9),
    (),
    (),
    (),
    (10,),
    (11, 11),
    (10, 11),
    (9, 9),
    (10, 11),
    (10, 11),
    (9, 9),
    (),
    (10,),
    (12, 12),
    (),
    (11, 10),
    (),
    (),
    (12,),
    (11,),
    (),
    (11, 12, 12),
    (),
    (),
    (),
    (11, 11),
    (),
    (12, 13, 13),
    (11, 12, 13),
    (),
    (),
    (),
    (),
    (13, 13),
    (),
    (),
    (12,),
    (14, 14),
    (),
    (12,),
    (),
    (13, 14),
    (13,),
    (12,),
    (15, 15),
    (),
    (14, 14),
    (13, 15),
    (13, 15, 16, 16),
    (14, 15, 16),
    (13, 14),
    (13, 17),
    (15, 16, 16),
    (),
    (14, 15),
    (17,),
    (14, 15, 16, 16),
    (14,),
    (15, 17, 15, 14, 15, 16, 16, 16, 16, 17),
)

MESH = pl.DeviceIdType.MESH
BF = jnp.bfloat16
F32 = jnp.float32


class Place:
    def __init__(self, depth, lanes):
        wide = lax.axis_index("wide")
        self.depth, self.lanes = depth, lanes
        self.bits = lanes.bit_length() - 1
        self.n = lax.axis_index("narrow")
        self.c = lax.rem(wide, 2)
        self.x = lax.rem(wide // 2, 2)
        self.z = wide // 4
        self.y = lax.rem(self.n, 2)
        self.c_far, self.x_far = 1 - self.c, 1 - self.x
        self.own = (2 * self.y, 2 * self.y + 1)
        self.far = (2 - 2 * self.y, 3 - 2 * self.y)
        self.core = self.at(c=self.c_far)
        self.across_x = self.at(x=self.x_far)
        self.flips = []
        for bit in range(self.bits):
            step = 1 << bit
            low = lax.rem(self.n // step, 2)
            self.flips.append(self.at(n=self.n + step * (1 - 2 * low)))
        self.across_y = self.flips[0]
        self.z_of = [lax.rem(self.z + d, depth) for d in range(depth)]
        self.along_z = [self.at(z=t) for t in self.z_of]

    def at(self, z=None, x=None, c=None, n=None):
        z = self.z if z is None else z
        x = self.x if x is None else x
        c = self.c if c is None else c
        n = self.n if n is None else n
        return ((z * 2 + x) * 2 + c, n)

    def greet(self):
        others = [self.core, self.across_x] + self.flips + self.along_z[1:]
        barrier = pltpu.get_barrier_semaphore()
        for other in others:
            pl.semaphore_signal(barrier, inc=1, device_id=other, device_id_type=MESH)
        pl.semaphore_wait(barrier, len(others))


class Copy:
    def __init__(self, sems, i, src, dst, device):
        self.parts = sems, i, src, dst, device

    def made(self):
        sems, i, src, dst, device = self.parts
        return pltpu.make_async_remote_copy(
            src_ref=src(), dst_ref=dst(), send_sem=sems.send.at[sems.row, i], recv_sem=sems.recv.at[sems.row, i],
            device_id=device, device_id_type=MESH,
        )

    def wait_recv(self):
        self.made().wait_recv()


class Sems:
    def __init__(self, send, recv, row):
        self.send, self.recv, self.row, self.used = send, recv, row, 0
        self.open = []

    def copy(self, src, dst, device):
        copy = Copy(self, self.used, src, dst, device)
        self.used += 1
        copy.made().start()
        self.open.append(copy)
        return copy

    def drain(self):
        for copy in self.open:
            copy.made().wait_send()
        self.open = []


def slot(ref, *at):
    return ref.at[at]


def strip(ref, cols, *at):
    return ref.at[(*at, *[slice(None)] * (len(ref.shape) - 1 - len(at)), cols)]


def gather_part(me, sems, view):
    own, far = me.own, me.far
    x, c, z = me.x, me.c, me.z
    every = slice(None)

    def send(u, zs, xs, device):
        block = functools.partial(view, u, zs, xs, c)
        return sems.copy(block, block, device)

    hops = []
    for u in own:
        hops.append([send(u, z, x, me.along_z[d]) for d in range(1, me.depth)])
        yield
    first = []
    for k, u in enumerate(own):
        for hop in hops[k]:
            hop.wait_recv()
        first.append((send(u, every, x, me.across_x), send(u, every, x, me.across_y)))
        yield
    (x_a, y_a), (x_b, y_b) = first
    x_a.wait_recv()
    y_fwd = send(own[0], every, me.x_far, me.across_y)
    cores = [send(own[0], every, every, me.core)]
    yield
    y_b.wait_recv()
    x_fwd = send(far[1], every, x, me.across_x)
    yield
    x_b.wait_recv()
    cores.append(send(own[1], every, every, me.core))
    yield
    y_a.wait_recv()
    y_fwd.wait_recv()
    cores.append(send(far[0], every, every, me.core))
    yield
    x_fwd.wait_recv()
    cores.append(send(far[1], every, every, me.core))
    yield
    for made in cores:
        made.wait_recv()
    yield


def reduce_part(me, sems, view, bufs, emit, credit, wait_credit, give_credit):
    rc, ry, rx, rz, fin, far = bufs
    (a, b), (ta, tb) = me.own, me.far
    x, c, z = me.x, me.c, me.z
    xo = me.x_far
    every = slice(None)

    def add(dst, *terms):
        total = dst[...].astype(F32)
        for t in terms:
            total = total + t[...].astype(F32)
        dst[...] = total.astype(BF)

    def send(u, zs, xs, device, buf, *at, core=c):
        return sems.copy(functools.partial(view, u, zs, xs, core), functools.partial(buf, *at), device)

    if wait_credit:
        pl.semaphore_wait(credit, 1)
    cores = [send(u, every, every, me.core, rc, i, core=me.c_far) for i, u in enumerate((ta, tb, b, a))]
    yield
    cores[0].wait_recv()
    add(view(ta, every, every, c), rc(0))
    y_diag = send(ta, every, xo, me.across_y, ry, 0)
    yield
    cores[1].wait_recv()
    add(view(tb, every, every, c), rc(1))
    x_diag = send(tb, every, xo, me.across_x, rx, 0)
    yield
    cores[2].wait_recv()
    add(view(b, every, every, c), rc(2))
    x_near = send(b, every, xo, me.across_x, rx, 1)
    y_near = send(ta, every, x, me.across_y, ry, 1)
    cores[3].wait_recv()
    add(view(a, every, every, c), rc(3))
    if give_credit:
        pl.semaphore_signal(credit, inc=1, device_id=me.core, device_id_type=MESH)
    yield
    y_diag.wait_recv()
    add(view(a, every, xo, c), ry(0))
    x_last = send(a, every, xo, me.across_x, rx, 2)
    yield
    x_diag.wait_recv()
    add(view(tb, every, x, c), rx(0))
    y_last = send(tb, every, x, me.across_y, ry, 2)
    yield
    z_hops = []
    y_near.wait_recv()
    x_last.wait_recv()
    add(view(a, every, x, c), ry(1), rx(2))
    z_hops.append([send(a, me.z_of[d], x, me.along_z[d], rz, 0, d - 1) for d in range(1, me.depth)])
    yield
    x_near.wait_recv()
    y_last.wait_recv()
    add(view(b, every, x, c), rx(1), ry(2))
    z_hops.append([send(b, me.z_of[d], x, me.along_z[d], rz, 1, d - 1) for d in range(1, me.depth)])
    yield
    sent = []
    last = max(me.bits - 1, 0)
    for k, u in enumerate((a, b)):
        for hop in z_hops[k]:
            hop.wait_recv()
        total = view(u, z, x, c)[...].astype(F32)
        for d in range(1, me.depth):
            total = total + rz(k, d - 1)[...].astype(F32)
        fin(0, k)[...] = total.astype(BF)
        for bit in range(1, me.bits):
            swap = sems.copy(functools.partial(fin, bit - 1, k), functools.partial(far, bit, k), me.flips[bit])
            swap.wait_recv()
            total = fin(bit - 1, k)[...].astype(F32) + far(bit, k)[...].astype(F32)
            fin(bit, k)[...] = total.astype(BF)
        sent.append(sems.copy(functools.partial(fin, last, k), functools.partial(far, 0, k), me.across_y))
        emit(u, True, k, fin(last, k)[...])
        yield
    for k, u in enumerate((ta, tb)):
        sent[k].wait_recv()
        emit(u, False, k, far(0, k)[...])
        yield


def reduce_copies(depth, lanes):
    bits = lanes.bit_length() - 1
    return 4 + 6 + 2 * (depth - 1) + 2 * (bits - 1) + 2


class Flow:
    def __init__(self, table):
        self.table, self.at, self.parts, self.count = list(table), 0, {}, {}

    def begin(self, i, part):
        self.parts[i], self.count[i] = part, 0

    def step(self, i):
        part = self.parts.get(i)
        if part is not None:
            self.count[i] += 1
            try:
                next(part)
            except StopIteration:
                self.parts[i] = None

    def peek(self, k):
        return self.table[self.at + k] if self.at + k < len(self.table) else ()

    def pump(self):
        for i in self.peek(0):
            self.step(i)
        self.at += 1

    def finish(self, i):
        while self.parts.get(i) is not None:
            self.step(i)

    def finish_all(self):
        while any(part is not None for part in self.parts.values()):
            for i in list(self.parts):
                self.step(i)


def stepped(flow, total, work):
    @pl.loop(0, total)
    def _(i):
        work(i)
        for k in range(total):
            if flow.peek(0):
                pl.when(i == k)(flow.pump)
            else:
                flow.pump()


def gather_copies(depth):
    return 2 * (depth - 1) + 4 + 2 + 4


GATHER_STEPS = 10


def all_sum(me, sems, first, pairs, stack, emit):
    hops = [me.core, me.across_x] + me.flips
    have = functools.partial(slot, first, slice(None))
    for i, other in enumerate(hops):
        came, total = functools.partial(slot, pairs, 2 * i), functools.partial(slot, pairs, 2 * i + 1)
        made = sems.copy(have, came, other)
        yield
        made.wait_recv()
        total()[...] = have()[...] + came()[...]
        have = total
    stack[me.z] = have()[...]
    mine = functools.partial(slot, stack, me.z)
    made = [sems.copy(have, mine, me.along_z[d]) for d in range(1, me.depth)]
    yield
    for m in made:
        m.wait_recv()
    total = stack[0]
    for i in range(1, me.depth):
        total = total + stack[i]
    emit(total)
    yield


def all_sum_sizes(depth, lanes):
    hops = 2 + lanes.bit_length() - 1
    return 2 * hops, hops + depth - 1, hops + 2


class Row:
    def __init__(self, ref):
        self.ref = ref

    def __getitem__(self, at):
        if at is Ellipsis:
            return self.ref[...].reshape(1, -1)
        return self.ref[at[1]].reshape(1, -1)


def stats(values):
    mean = jnp.mean(values, axis=-1, keepdims=True)
    centred = values - mean
    rstd = lax.rsqrt(jnp.mean(centred * centred, axis=-1, keepdims=True) + EPSILON)
    return centred, rstd


def dot_nn(a, b):
    return jnp.dot(a, b, preferred_element_type=F32)


def dot_nt(a, b):
    return lax.dot_general(a, b, (((1,), (1,)), ((), ())), preferred_element_type=F32)


def dot_tn(a, b):
    return lax.dot_general(a, b, (((0,), (0,)), ((), ())), preferred_element_type=F32)


def lane_halves(width=128):
    lane = lax.broadcasted_iota(jnp.int32, (1, width), 1)
    low = (lane < width // 2).astype(F32)
    return low.astype(BF), (1.0 - low).astype(BF)


def norm_back(grad, normed, rstd):
    mean_g = jnp.mean(grad, axis=-1, keepdims=True)
    mean_gn = jnp.mean(grad * normed, axis=-1, keepdims=True)
    return (grad - mean_g - normed * mean_gn) * rstd


def down_sum(values):
    return jnp.sum(values, axis=0, keepdims=True)


def cut(sizes):
    return [pl.ds(128 * sum(sizes[:i]), 128 * size) for i, size in enumerate(sizes)]


def layer_kernel(
    depth, lanes,
    x_h, cot_h, seg, live, expert, g1, b1, qb, vb, ob, g2, b2, ib, yb,
    q_w, k_w, v_w, o_w, w_in, w_out,
    out_h, dx_h, counts, d_q, d_k, d_v, d_o, d_in, d_out,
    d_g1, d_b1, d_qb, d_vb, d_ob, d_g2, d_b2, d_ib, d_yb,
    qkv_h, a_h, pb_h, z_h, h_h, go_h,
    ga, gi, go, s1, s2, pa, po, x_s, o_s, c_s, xh, dattn, hd, tok, rstd_s,
    rc, ry, rx, rz, fin, far, vec, vec_pair, vec_stack, cnt, cnt_pair, cnt_stack, ib_s, yb_s,
    local, by_row, send, recv, rsend, rrecv, csend, crecv, vsend, vrecv, credit,
):
    me = Place(depth, lanes)
    g1, b1, qb, vb, ob, g2, b2, ib, yb = [Row(t) for t in (g1, b1, qb, vb, ob, g2, b2, ib, yb)]
    rows_w, width = q_w.shape
    row_total, slots = seg.shape
    blocks = s1.shape[0]
    x_, c_, z_ = me.x, me.c, me.z
    per = depth // 4
    gathered, reduced = [[cut(sizes) for sizes in cuts] for cuts in (GATHER_CUTS, REDUCE_CUTS)]
    count_part = sum(len(cuts) for cuts in gathered)
    reduce_base = count_part + 1
    reduce_total = sum(len(cuts) for cuts in reduced)
    vec_part = reduce_base + reduce_total
    used = [2]

    def move(src, dst):
        made = pltpu.make_async_copy(src, dst, local.at[used[0]])
        used[0] += 1
        made.start()
        return made

    def row(r):
        return pl.ds(pl.multiple_of(r * slots, slots), slots)

    def fill(refs):
        for k, ref in enumerate(refs):
            pltpu.make_async_copy(ref, ga.at[me.own[k], z_, x_, c_], local.at[k]).start()

    @pl.when(me.y == 0)
    def _():
        fill((q_w, k_w))

    @pl.when(me.y == 1)
    def _():
        fill((v_w, o_w))

    filled = [pltpu.make_async_copy(q_w, ga.at[me.own[k], z_, x_, c_], local.at[k]) for k in range(2)]
    for u in me.own:
        filled.append(move(w_in.at[:, pl.ds(pl.multiple_of(u * width, width), width)], gi.at[u, z_, x_, c_]))
        filled.append(move(w_out.at[pl.ds(pl.multiple_of(u * rows_w, 8), rows_w), :], go.at[z_, x_, c_, u]))
    m_x = move(x_h, x_s)
    gb = x_s
    me.greet()
    for m in filled:
        m.wait()

    def view_of(g, cols, first, second, third):
        def view(u, zs, xs, cs):
            if g > 1:
                return third.at[zs, xs, cs, u, :, cols]
            return (first, second)[g].at[u, zs, xs, cs, :, cols]

        return view

    flow, gather_sems, reduce_sems = Flow(TABLE), [], []
    for g in range(3):
        for cols_g in gathered[g]:
            sems = Sems(send, recv, len(gather_sems))
            flow.begin(len(gather_sems), gather_part(me, sems, view_of(g, cols_g, ga, gi, go)))
            gather_sems.append(sems)
    flow.pump()
    m_cot = move(cot_h, dattn)
    vec[...] = jnp.zeros_like(vec)
    for u in range(blocks):
        ib_s[u : u + 1, :] = ib[:, pl.ds(u * width, width)]
    yb_s[0:1, :] = yb[...]

    arrived = [0]

    def ready():
        flow.pump()
        flow.finish(arrived[0])
        arrived[0] += 1

    cnt[...] = jnp.zeros_like(cnt)
    for r in range(row_total):
        for e in range(3):
            hit = (expert[r] == e).astype(jnp.int32)
            cnt[e : e + 1, :] += live[r : r + 1, :] * hit
    csems = Sems(csend, crecv, 0)

    def count_out(total):
        summed = jnp.broadcast_to(jnp.sum(total, axis=1, keepdims=True), (8, 128))
        for e in range(3):
            counts[e] = jnp.sum(total[e : e + 1, :].astype(F32)).astype(jnp.int32)
        one = [summed[e : e + 1, :].astype(F32) for e in range(3)]
        for r in range(row_total):
            own = jnp.zeros_like(one[0])
            for e in range(3):
                own = own + one[e] * (expert[r] == e).astype(F32)
            scale = (one[1] + one[2]) / (2.0 * own)
            rows = pl.ds(r * slots, slots)
            tok[rows, :] = tok[rows, :] * scale

    flow.begin(count_part, all_sum(me, csems, cnt, cnt_pair, cnt_stack, count_out))
    flow.pump()
    m_x.wait()

    def first_norm(r):
        rows = row(r)
        centred, rstd = stats(x_s[rows, :].astype(F32))
        s1[3, rows, :] = (centred * rstd * g1[...] + b1[...]).astype(BF)

    stepped(flow, row_total, first_norm)
    spilled = [move(s1.at[3], a_h)]

    row_pos = lax.broadcasted_iota(jnp.int32, (slots, slots), 0)
    col_pos = lax.broadcasted_iota(jnp.int32, (slots, slots), 1)
    for r in range(row_total):
        seg_row = seg[r : r + 1, :]
        live_row = live[r : r + 1, :]
        down = jnp.transpose(jnp.broadcast_to(seg_row.astype(F32), (slots, slots)))
        across = jnp.where(live_row > 0, seg_row, -1 - col_pos[0:1, :]).astype(F32)
        allowed = (down == across) | (row_pos == col_pos)
        hd[pl.ds(r * slots, slots), pl.ds(0, slots)] = jnp.where(allowed, 0.0, MASKED)
        live_down = jnp.transpose(jnp.broadcast_to(live_row.astype(F32), (128, slots)))
        tok[pl.ds(r * slots, slots), :] = live_down
        flow.pump()

    masks = lane_halves()
    for cols_h in gathered[0]:
        ready()

        def project(r, cols_h=cols_h):
            rows = row(r)
            a_row = s1[3, rows, :]
            for u, add in enumerate((qb, None, vb)):
                value = dot_nn(a_row, ga[u, :, :, :, :, cols_h].reshape(width, cols_h.size))
                if add is not None:
                    value = value + add[:, cols_h]
                s1[u, rows, cols_h] = value.astype(BF)

        stepped(flow, row_total, project)

        def attend(r, cols_h=cols_h):
            rows = row(r)
            for start in range(cols_h.start, cols_h.start + cols_h.size, 128):
                cols = pl.ds(start, 128)
                q2, k2, v2 = s1[0, rows, cols], s1[1, rows, cols], s1[2, rows, cols]
                mixed = jnp.zeros((slots, 128), F32)
                for i in range(2):
                    scores = dot_nt(q2 * (masks[i] * 0.125), k2) + hd[rows, pl.ds(0, slots)]
                    top = jnp.max(scores, axis=-1, keepdims=True)
                    terms = jnp.exp(scores - top)
                    inv = 1.0 / jnp.sum(terms, axis=-1, keepdims=True)
                    probs = (terms * inv).astype(BF)
                    head = start // 64 + i
                    s2[head // 3, rows, pl.ds((head % 3) * slots, slots)] = probs
                    mixed = mixed + dot_nn(probs, v2 * masks[i])
                o_s[rows, cols] = mixed.astype(BF)

        stepped(flow, row_total, attend)
        for u in range(3):
            spilled.append(move(s1.at[u, :, cols_h], qkv_h.at[u, :, cols_h]))
        for head in range(cols_h.start // 64, (cols_h.start + cols_h.size) // 64):
            cols = pl.ds((head % 3) * slots, slots)
            spilled.append(move(s2.at[head // 3, :, cols], pb_h.at[head // 3, :, cols]))

    def second_norm(r):
        rows = row(r)
        h_row = x_s[rows, :].astype(F32) + dot_nn(o_s[rows, :], ga[3].reshape(width, width)) + ob[...]
        hd[rows, :] = h_row
        centred, rstd = stats(h_row)
        normed = centred * rstd
        xh[rows, :] = normed.astype(BF)
        rstd_s[rows, :] = jnp.broadcast_to(rstd, (slots, 128))
        c_s[rows, :] = (normed * g2[...] + b2[...]).astype(BF)

    stepped(flow, row_total, second_norm)
    m_h = move(hd, h_h)
    for m in spilled:
        m.wait()
    pair_rows = row_total // 2
    for cols_h in gathered[1]:
        ready()

        def hidden(t, cols_h=cols_h):
            u, first = t // pair_rows, 2 * lax.rem(t, pair_rows)
            weight = gi[u, :, :, :, :, cols_h].reshape(width, cols_h.size)
            for s in range(2):
                rows = row(first + s)
                pre = dot_nn(c_s[rows, :], weight) + ib_s[pl.ds(u, 1), cols_h]
                cdf = 0.5 * (1.0 + lax.erf(pre * 0.7071067811865476))
                s1[u, rows, cols_h] = (pre * cdf).astype(BF)
                s2[u, rows, cols_h] = (cdf + pre * (jnp.exp(-0.5 * pre * pre) * 0.3989422804014327)).astype(BF)

        stepped(flow, blocks * pair_rows, hidden)
    m_z = move(s1, z_h)
    flow.finish(count_part)
    m_cot.wait()

    def begin(g, cols):
        i = len(reduce_sems)
        at = pl.ds((2 - g) * width + cols.start, cols.size)

        def emit(u, mine, k, value):
            value = value.astype(F32)
            if g == 0:
                even = (me.y == 0) if mine else (me.y == 1)

                @pl.when(even)
                def _():
                    (d_q, d_k)[k][:, cols] = value

                @pl.when(jnp.logical_not(even))
                def _():
                    (d_v, d_o)[k][:, cols] = value
            elif g == 1:
                d_in[:, pl.ds(pl.multiple_of(u * width + cols.start, 128), cols.size)] = value
            else:
                d_out[pl.ds(pl.multiple_of(u * rows_w, 8), rows_w), cols] = value

        sems = Sems(rsend, rrecv, i)
        reduce_sems.append(sems)
        bufs = [functools.partial(strip, rc, pl.ds(0, cols.size), i % 2)]
        bufs += [functools.partial(strip, t, at) for t in (ry, rx, rz, fin, far)]
        while i >= 2 and flow.count[reduce_base + i - 2] < 4:
            flow.step(reduce_base + i - 2)
        view = view_of(g, cols, pa, None, po) if g != 1 else view_of(2, cols, None, None, go)
        give = i < reduce_total - 2
        flow.begin(reduce_base + i, reduce_part(me, sems, view, bufs, emit, credit, i >= 2, give))
        flow.step(reduce_base + i)

    def scaled(r):
        rows = row(r)
        value = (dattn[rows, :].astype(F32) * tok[rows, 0:1]).astype(BF)
        gb[rows, :] = value
        vec[7:8, :] += down_sum(value.astype(F32))

    stepped(flow, row_total, scaled)
    for cols_h in reduced[0]:
        def out_grad(u, cols_h=cols_h):
            value = dot_tn(s1[u], gb[:, cols_h]).astype(BF)
            po[pl.ds(u * per, per), :, :, :, :, cols_h] = value.reshape(per, 2, 2, 4, rows_w, cols_h.size)

        stepped(flow, blocks, out_grad)
        begin(2, cols_h)
    m_z.wait()
    m_q = [move(qkv_h.at[u], s1.at[u]) for u in range(3)] + [move(a_h, s1.at[3])]
    for _ in gathered[2]:
        ready()
    m_go = move(go, go_h)

    def hidden_grad(t):
        u, rows = t // row_total, row(lax.rem(t, row_total))
        weight = go[pl.ds(u * per, per)].reshape(width, width)
        value = (dot_nt(gb[rows, :], weight) * s2[u, rows, :].astype(F32)).astype(BF)
        s2[u, rows, :] = value
        vec[pl.ds(8 + u, 1), :] += down_sum(value.astype(F32))

    stepped(flow, blocks * row_total, hidden_grad)
    for s in gather_sems:
        s.drain()
    csems.drain()
    m_go.wait()
    for cols_h in reduced[1]:
        def in_grad(u, cols_h=cols_h):
            value = dot_tn(c_s[...], s2[u, :, cols_h]).astype(BF)
            go[:, :, :, u, :, cols_h] = value.reshape(depth, 2, 2, rows_w, cols_h.size)

        stepped(flow, blocks, in_grad)
        begin(1, cols_h)
    m_h.wait()

    def mid_grad(r):
        rows = row(r)
        grad = dot_nt(s2[0, rows, :], gi[0].reshape(width, width))
        for u in range(1, blocks):
            grad = grad + dot_nt(s2[u, rows, :], gi[u].reshape(width, width))
        normed = xh[rows, :].astype(F32)
        vec[5:6, :] += down_sum(grad * normed)
        vec[6:7, :] += down_sum(grad)
        value = dattn[rows, :].astype(F32) * tok[rows, 0:1]
        value = value + norm_back(grad * g2[...], normed, rstd_s[rows, 0:1])
        hd[rows, :] = value
        value = value.astype(BF)
        dattn[rows, :] = value
        vec[4:5, :] += down_sum(value.astype(F32))

    stepped(flow, row_total, mid_grad)
    m_p = move(pb_h, s2)
    for cols_h in reduced[2]:
        value = dot_tn(o_s[...], dattn[:, cols_h]).astype(BF)
        pa[3, :, :, :, :, cols_h] = value.reshape(depth, 2, 2, rows_w, cols_h.size)
        flow.pump()

    def mixed_grad(r):
        rows = row(r)
        gb[rows, :] = dot_nt(dattn[rows, :], ga[3].reshape(width, width)).astype(BF)

    stepped(flow, row_total, mixed_grad)
    for m in m_q:
        m.wait()
    m_p.wait()
    for cols_h in reduced[2]:
        def attend_back(r, cols_h=cols_h):
            rows = row(r)
            for start in range(cols_h.start, cols_h.start + cols_h.size, 128):
                cols = pl.ds(start, 128)
                q2, k2, v2, do2 = s1[0, rows, cols], s1[1, rows, cols], s1[2, rows, cols], gb[rows, cols]
                dq = jnp.zeros((slots, 128), F32)
                dk, dv = dq, dq
                both = do2.astype(F32) * o_s[rows, cols].astype(F32)
                for i in range(2):
                    head = start // 64 + i
                    probs = s2[head // 3, rows, pl.ds((head % 3) * slots, slots)]
                    do1 = do2 * masks[i]
                    dp = dot_nt(do1, v2)
                    wide = probs.astype(F32)
                    inner = jnp.sum(both * masks[i].astype(F32), axis=-1, keepdims=True)
                    ds = (wide * (dp - inner)).astype(BF)
                    dq = dq + dot_nn(ds, k2 * masks[i])
                    dk = dk + dot_tn(ds, q2 * masks[i])
                    dv = dv + dot_tn(probs, do1)
                dq, dv = (dq * 0.125).astype(BF), dv.astype(BF)
                s1[0, rows, cols] = dq
                s1[1, rows, cols] = (dk * 0.125).astype(BF)
                s1[2, rows, cols] = dv
                vec[2:3, cols] += down_sum(dq.astype(F32))
                vec[3:4, cols] += down_sum(dv.astype(F32))

        stepped(flow, row_total, attend_back)
        if cols_h is reduced[2][-1]:
            m_x = move(x_h, x_s)

        def project_grad(u, cols_h=cols_h):
            value = dot_tn(s1[3], s1[u, :, cols_h]).astype(BF)
            pa[u, :, :, :, :, cols_h] = value.reshape(depth, 2, 2, rows_w, cols_h.size)

        stepped(flow, 3, project_grad)
        begin(0, cols_h)
    m_z = move(z_h, s2)
    for i, sems in enumerate(reduce_sems):
        if len(reduced[0]) <= i < len(reduced[0]) + len(reduced[1]):
            flow.finish(reduce_base + i)
            sems.drain()
    m_go = move(go_h, go)
    m_x.wait()

    def h_back(r):
        return pltpu.make_async_copy(h_h.at[row(r), :], hd.at[row(r), :], by_row.at[0, r])

    def dx_back(r):
        return pltpu.make_async_copy(dattn.at[row(r), :], dx_h.at[row(r), :], by_row.at[1, r])

    def last_grad(r):
        rows = row(r)
        grad = dot_nt(s1[0, rows, :], ga[0].reshape(width, width))
        for u in (1, 2):
            grad = grad + dot_nt(s1[u, rows, :], ga[u].reshape(width, width))
        centred, rstd = stats(x_s[rows, :].astype(F32))
        normed = centred * rstd
        vec[0:1, :] += down_sum(grad * normed)
        vec[1:2, :] += down_sum(grad)
        dattn[rows, :] = (hd[rows, :] + norm_back(grad * g1[...], normed, rstd)).astype(BF)
        dx_back(r).start()
        h_back(r).start()

    stepped(flow, row_total, last_grad)
    vsems = Sems(vsend, vrecv, 0)

    def vec_out(total):
        for i, ref in enumerate((d_g1, d_b1, d_qb, d_vb, d_ob, d_g2, d_b2, d_yb)):
            ref[...] = total[i]
        for u in range(blocks):
            d_ib[pl.ds(u * width, width)] = total[8 + u]

    flow.begin(vec_part, all_sum(me, vsems, vec, vec_pair, vec_stack, vec_out))
    flow.step(vec_part)
    m_z.wait()
    m_go.wait()
    for r in range(row_total):
        h_back(r).wait()
        dx_back(r).wait()

    half = width // 2

    def outward(t):
        rows, cols = row(t // 2), pl.ds(pl.multiple_of(lax.rem(t, 2) * half, half), half)
        value = hd[rows, cols] + yb_s[0:1, cols]
        for u in range(blocks):
            value = value + dot_nn(s2[u, rows, :], go[u * per : (u + 1) * per, :, :, :, :, cols].reshape(width, half))
        gb[rows, cols] = value.astype(BF)

    stepped(flow, 2 * row_total, outward)
    m_out = move(gb, out_h)
    flow.pump()
    flow.finish_all()
    for s in reduce_sems:
        s.drain()
    vsems.drain()
    m_out.wait()


def whole_layer(depth, lanes, x, cot, seg, live, expert, vectors, weights):
    tokens, width = x.shape
    row_total, slots = seg.shape
    rows_w = weights[0].shape[0]
    ff = weights[4].shape[1]
    blocks = ff // width
    g_parts, r_parts = [sum(len(sizes) for sizes in cuts) for cuts in (GATHER_CUTS, REDUCE_CUTS)]
    cols = 128 * max(max(sizes) for sizes in REDUCE_CUTS)
    g_per, r_per = gather_copies(depth), reduce_copies(depth, lanes)
    bits = max(lanes.bit_length() - 1, 1)
    pair_n, pair_c, _ = all_sum_sizes(depth, lanes)
    vec_rows = 8 + -(-blocks // 8) * 8
    anyspec = pl.BlockSpec(memory_space=pl.ANY)
    vspec = pl.BlockSpec(memory_space=pltpu.VMEM)
    sspec = pl.BlockSpec(memory_space=pltpu.SMEM)
    like = jax.ShapeDtypeStruct
    unit, unit_o = (4, depth, 2, 2, rows_w, width), (depth, 2, 2, 4, rows_w, width)
    flat, wide = (tokens, width), (blocks, tokens, width)
    o = lambda *s: like(s, F32)
    v = lambda *s: pltpu.VMEM(s, BF)
    f = lambda *s: pltpu.VMEM(s, F32)
    n = lambda *s: pltpu.VMEM(s, jnp.int32)
    dma = lambda *s: pltpu.SemaphoreType.DMA(s)
    return pl.pallas_call(
        functools.partial(layer_kernel, depth, lanes),
        out_shape=[like(flat, BF), like(flat, BF), like((3,), jnp.int32)]
        + [o(rows_w, width)] * 4 + [o(rows_w, ff), o(4 * rows_w, width)]
        + [o(width)] * 7 + [o(ff), o(width)]
        + [like((3, *flat), BF), like(flat, BF), like(wide, BF), like(wide, BF), like(flat, F32), like(unit_o, BF)],
        in_specs=[anyspec] * 2 + [vspec] * 2 + [sspec] + [vspec] * 9 + [anyspec] * 6,
        out_specs=[anyspec] * 2 + [sspec] + [vspec] * 15 + [anyspec] * 6,
        scratch_shapes=[
            v(*unit), v(*unit), v(*unit_o), v(*wide), v(*wide), v(*unit), v(*unit_o),
            v(*flat), v(*flat), v(*flat), v(*flat), v(*flat), f(*flat), f(tokens, 128), f(tokens, 128),
            v(2, 4, depth, 2, rows_w, cols), v(3, depth, rows_w, 3 * width), v(3, depth, rows_w, 3 * width),
            v(2, depth - 1, rows_w, 3 * width), v(bits, 2, rows_w, 3 * width), v(bits, 2, rows_w, 3 * width),
            f(vec_rows, width), f(pair_n, vec_rows, width), f(depth, vec_rows, width),
            n(8, slots), n(pair_n, 8, slots), n(depth, 8, slots), f(-(-blocks // 8) * 8, width), f(8, width),
            dma(64), dma(2, row_total), dma(g_parts, g_per), dma(g_parts, g_per), dma(r_parts, r_per), dma(r_parts, r_per),
            dma(1, pair_c), dma(1, pair_c), dma(1, pair_c), dma(1, pair_c), pltpu.SemaphoreType.REGULAR,
        ],
        compiler_params=pltpu.CompilerParams(collective_id=0, has_side_effects=True, vmem_limit_bytes=VMEM_BYTES),
        name="whole_layer",
    )(x, cot, seg, live, expert, *vectors, *weights)


def hand_over_kernel(count, *refs):
    sources, targets = refs[:count], refs[count + 1 : 2 * count + 1]
    stage, sem = refs[2 * count + 2 : 3 * count + 2], refs[-1]
    into = [pltpu.make_async_copy(s, m, sem.at[0, i]) for i, (s, m) in enumerate(zip(sources, stage))]
    out = [pltpu.make_async_copy(m, t, sem.at[1, i]) for i, (m, t) in enumerate(zip(stage, targets))]
    for m in into:
        m.start()
    for i in range(3):
        refs[2 * count + 1][i] = refs[count][i]
    for first, second in zip(into, out):
        first.wait()
        second.start()
    for m in out:
        m.wait()


def hand_over(counts, arrays):
    anyspec = pl.BlockSpec(memory_space=pl.ANY)
    sspec = pl.BlockSpec(memory_space=pltpu.SMEM)
    count = len(arrays)
    return pl.pallas_call(
        functools.partial(hand_over_kernel, count),
        out_shape=[jax.ShapeDtypeStruct(t.shape, t.dtype) for t in (*arrays, counts)],
        in_specs=[anyspec] * count + [sspec],
        out_specs=[anyspec] * count + [sspec],
        scratch_shapes=[pltpu.VMEM(t.shape, t.dtype) for t in arrays] + [pltpu.SemaphoreType.DMA((2, count))],
        name="hand_over",
    )(*arrays, counts)


def body(
    layer_in, segment_ids, live_mask, expert_ids, cotangent,
    norm1_gain, norm1_bias, q_weight, q_bias, k_weight, v_weight, v_bias, o_weight, o_bias,
    norm2_gain, norm2_bias, in_weight, in_bias, out_weight, out_bias,
):
    row_local, slot_total, width_all = layer_in.shape
    tokens = row_local * slot_total
    depth = lax.axis_size("wide") // 4
    lanes = lax.axis_size("narrow")
    x = layer_in.reshape(tokens, width_all)
    vectors = [norm1_gain, norm1_bias, q_bias, v_bias, o_bias, norm2_gain, norm2_bias, in_bias, out_bias]
    weights = (q_weight, k_weight, v_weight, o_weight, in_weight, out_weight)
    layer_out, input_grad, counts, *grads = whole_layer(
        depth, lanes, x, cotangent.reshape(tokens, width_all), segment_ids, live_mask, expert_ids, vectors, weights
    )
    (
        layer_out, input_grad, d_q, d_k, d_v, d_o, d_in, d_out,
        d_g1, d_b1, d_qb, d_vb, d_ob, d_g2, d_b2, d_ib, d_yb, counts,
    ) = hand_over(counts, (layer_out, input_grad, *grads[:15]))
    return (
        layer_out.reshape(layer_in.shape), input_grad.reshape(layer_in.shape), counts,
        d_g1, d_b1, d_q, d_qb, d_k, d_v, d_vb, d_o, d_ob, d_g2, d_b2, d_in, d_ib, d_out, d_yb,
    )


def solution(mesh):
    rows, row_pair = P(("wide", "narrow"), None, None), P(("wide", "narrow"), None)
    whole, split = P(), P("wide", None)
    return jax.shard_map(
        body,
        mesh=mesh,
        in_specs=(
            rows, row_pair, row_pair, P(("wide", "narrow")), rows,
            whole, whole, split, whole, split, split, whole, split, whole,
            whole, whole, split, whole, split, whole,
        ),
        out_specs=(
            rows, rows, whole, whole, whole, split, whole, split, split, whole, split, whole,
            whole, whole, split, whole, split, whole,
        ),
        check_vma=False,
    )
```

```python
import functools
import math

import jax
import jax.numpy as jnp
from jax import lax
from jax.experimental import pallas as pl
from jax.experimental.pallas import tpu as pltpu
from jax.sharding import PartitionSpec as P

HEADS = 12
EPSILON = 1e-06
MASKED = -1e30
GATHER_CUTS = ((2, 2, 2), (2, 2, 2), (3, 3))
REDUCE_CUTS = ((3, 3), (3, 3), (2, 2, 1, 1))
VMEM_BYTES = 63 << 20
TABLE = (
    (0, 0),
    (8,),
    (),
    (),
    (),
    (8,),
    (),
    (),
    (),
    (),
    (8, 0, 1, 1, 0, 8, 0, 0, 0, 1, 2, 2, 1, 0, 2, 3, 3, 0, 2, 1, 1, 1, 0),
    (),
    (),
    (),
    (),
    (),
    (3, 4),
    (2, 4),
    (1, 2, 1, 2),
    (3, 1),
    (3,),
    (),
    (),
    (4, 5),
    (2, 5),
    (2, 3, 3),
    (4,),
    (4, 3, 2),
    (),
    (),
    (),
    (5, 6),
    (),
    (3, 6),
    (4, 4),
    (3, 5),
    (4, 5),
    (),
    (6, 7),
    (4,),
    (7, 5, 5),
    (),
    (),
    (),
    (4,),
    (6,),
    (5,),
    (),
    (),
    (),
    (),
    (6,),
    (),
    (),
    (),
    (),
    (5,),
    (7,),
    (),
    (7, 5),
    (6, 6),
    (),
    (),
    (),
    (),
    (),
    (),
    (),
    (6,),
    (),
    (),
    (),
    (),
    (),
    (),
    (7, 7),
    (7,),
    (6,),
    (),
    (),
    (9, 9, 6),
    (7, 7, 9, 7),
    (),
    (10, 10),
    (),
    (),
    (),
    (),
    (9, 9),
    (),
    (),
    (),
    (),
    (),
    (10,),
    (),
    (),
    (),
    (10, 10),
    (),
    (9, 9),
    (),
    (),
    (),
    (10,),
    (11, 11),
    (10, 11),
    (9, 9),
    (10, 11),
    (10, 11),
    (9, 9),
    (),
    (10,),
    (12, 12),
    (),
    (11, 10),
    (),
    (),
    (12,),
    (11,),
    (),
    (11, 12, 12),
    (),
    (),
    (),
    (11, 11),
    (),
    (12, 13, 13),
    (11, 12, 13),
    (),
    (),
    (),
    (),
    (13, 13),
    (),
    (),
    (12,),
    (14, 14),
    (),
    (12,),
    (),
    (13, 14),
    (13,),
    (12,),
    (15, 15),
    (),
    (14, 14),
    (13, 15),
    (13, 15, 16, 16),
    (14, 15, 16),
    (13, 14),
    (13, 17),
    (15, 16, 16),
    (),
    (14, 15),
    (17,),
    (14, 15, 16, 16),
    (14,),
    (15, 17, 15, 14, 15, 16, 16, 16, 16, 17),
)

MESH = pl.DeviceIdType.MESH
BF = jnp.bfloat16
F32 = jnp.float32


class Place:
    def __init__(self, depth, lanes):
        wide = lax.axis_index("wide")
        self.depth, self.lanes = depth, lanes
        self.bits = lanes.bit_length() - 1
        self.n = lax.axis_index("narrow")
        self.c = lax.rem(wide, 2)
        self.x = lax.rem(wide // 2, 2)
        self.z = wide // 4
        self.y = lax.rem(self.n, 2)
        self.c_far, self.x_far = 1 - self.c, 1 - self.x
        self.own = (2 * self.y, 2 * self.y + 1)
        self.far = (2 - 2 * self.y, 3 - 2 * self.y)
        self.core = self.at(c=self.c_far)
        self.across_x = self.at(x=self.x_far)
        self.flips = []
        for bit in range(self.bits):
            step = 1 << bit
            low = lax.rem(self.n // step, 2)
            self.flips.append(self.at(n=self.n + step * (1 - 2 * low)))
        self.across_y = self.flips[0]
        self.z_of = [lax.rem(self.z + d, depth) for d in range(depth)]
        self.along_z = [self.at(z=t) for t in self.z_of]

    def at(self, z=None, x=None, c=None, n=None):
        z = self.z if z is None else z
        x = self.x if x is None else x
        c = self.c if c is None else c
        n = self.n if n is None else n
        return ((z * 2 + x) * 2 + c, n)

    def greet(self):
        others = [self.core, self.across_x] + self.flips + self.along_z[1:]
        barrier = pltpu.get_barrier_semaphore()
        for other in others:
            pl.semaphore_signal(barrier, inc=1, device_id=other, device_id_type=MESH)
        pl.semaphore_wait(barrier, len(others))


class Copy:
    def __init__(self, sems, i, src, dst, device):
        self.parts = sems, i, src, dst, device

    def made(self):
        sems, i, src, dst, device = self.parts
        return pltpu.make_async_remote_copy(
            src_ref=src(), dst_ref=dst(), send_sem=sems.send.at[sems.row, i], recv_sem=sems.recv.at[sems.row, i],
            device_id=device, device_id_type=MESH,
        )

    def wait_recv(self):
        self.made().wait_recv()


class Sems:
    def __init__(self, send, recv, row):
        self.send, self.recv, self.row, self.used = send, recv, row, 0
        self.open = []

    def copy(self, src, dst, device):
        copy = Copy(self, self.used, src, dst, device)
        self.used += 1
        copy.made().start()
        self.open.append(copy)
        return copy

    def drain(self):
        for copy in self.open:
            copy.made().wait_send()
        self.open = []


def slot(ref, *at):
    return ref.at[at]


def strip(ref, cols, *at):
    return ref.at[(*at, *[slice(None)] * (len(ref.shape) - 1 - len(at)), cols)]


def gather_part(me, sems, view):
    own, far = me.own, me.far
    x, c, z = me.x, me.c, me.z
    every = slice(None)

    def send(u, zs, xs, device):
        block = functools.partial(view, u, zs, xs, c)
        return sems.copy(block, block, device)

    hops = []
    for u in own:
        hops.append([send(u, z, x, me.along_z[d]) for d in range(1, me.depth)])
        yield
    first = []
    for k, u in enumerate(own):
        for hop in hops[k]:
            hop.wait_recv()
        first.append((send(u, every, x, me.across_x), send(u, every, x, me.across_y)))
        yield
    (x_a, y_a), (x_b, y_b) = first
    x_a.wait_recv()
    y_fwd = send(own[0], every, me.x_far, me.across_y)
    cores = [send(own[0], every, every, me.core)]
    yield
    y_b.wait_recv()
    x_fwd = send(far[1], every, x, me.across_x)
    yield
    x_b.wait_recv()
    cores.append(send(own[1], every, every, me.core))
    yield
    y_a.wait_recv()
    y_fwd.wait_recv()
    cores.append(send(far[0], every, every, me.core))
    yield
    x_fwd.wait_recv()
    cores.append(send(far[1], every, every, me.core))
    yield
    for made in cores:
        made.wait_recv()
    yield


def reduce_part(me, sems, view, bufs, emit, credit, wait_credit, give_credit):
    rc, ry, rx, rz, fin, far = bufs
    (a, b), (ta, tb) = me.own, me.far
    x, c, z = me.x, me.c, me.z
    xo = me.x_far
    every = slice(None)

    def add(dst, *terms):
        total = dst[...].astype(F32)
        for t in terms:
            total = total + t[...].astype(F32)
        dst[...] = total.astype(BF)

    def send(u, zs, xs, device, buf, *at, core=c):
        return sems.copy(functools.partial(view, u, zs, xs, core), functools.partial(buf, *at), device)

    if wait_credit:
        pl.semaphore_wait(credit, 1)
    cores = [send(u, every, every, me.core, rc, i, core=me.c_far) for i, u in enumerate((ta, tb, b, a))]
    yield
    cores[0].wait_recv()
    add(view(ta, every, every, c), rc(0))
    y_diag = send(ta, every, xo, me.across_y, ry, 0)
    yield
    cores[1].wait_recv()
    add(view(tb, every, every, c), rc(1))
    x_diag = send(tb, every, xo, me.across_x, rx, 0)
    yield
    cores[2].wait_recv()
    add(view(b, every, every, c), rc(2))
    x_near = send(b, every, xo, me.across_x, rx, 1)
    y_near = send(ta, every, x, me.across_y, ry, 1)
    cores[3].wait_recv()
    add(view(a, every, every, c), rc(3))
    if give_credit:
        pl.semaphore_signal(credit, inc=1, device_id=me.core, device_id_type=MESH)
    yield
    y_diag.wait_recv()
    add(view(a, every, xo, c), ry(0))
    x_last = send(a, every, xo, me.across_x, rx, 2)
    yield
    x_diag.wait_recv()
    add(view(tb, every, x, c), rx(0))
    y_last = send(tb, every, x, me.across_y, ry, 2)
    yield
    z_hops = []
    y_near.wait_recv()
    x_last.wait_recv()
    add(view(a, every, x, c), ry(1), rx(2))
    z_hops.append([send(a, me.z_of[d], x, me.along_z[d], rz, 0, d - 1) for d in range(1, me.depth)])
    yield
    x_near.wait_recv()
    y_last.wait_recv()
    add(view(b, every, x, c), rx(1), ry(2))
    z_hops.append([send(b, me.z_of[d], x, me.along_z[d], rz, 1, d - 1) for d in range(1, me.depth)])
    yield
    sent = []
    last = max(me.bits - 1, 0)
    for k, u in enumerate((a, b)):
        for hop in z_hops[k]:
            hop.wait_recv()
        total = view(u, z, x, c)[...].astype(F32)
        for d in range(1, me.depth):
            total = total + rz(k, d - 1)[...].astype(F32)
        fin(0, k)[...] = total.astype(BF)
        for bit in range(1, me.bits):
            swap = sems.copy(functools.partial(fin, bit - 1, k), functools.partial(far, bit, k), me.flips[bit])
            swap.wait_recv()
            total = fin(bit - 1, k)[...].astype(F32) + far(bit, k)[...].astype(F32)
            fin(bit, k)[...] = total.astype(BF)
        sent.append(sems.copy(functools.partial(fin, last, k), functools.partial(far, 0, k), me.across_y))
        emit(u, True, k, fin(last, k)[...])
        yield
    for k, u in enumerate((ta, tb)):
        sent[k].wait_recv()
        emit(u, False, k, far(0, k)[...])
        yield


def reduce_copies(depth, lanes):
    bits = lanes.bit_length() - 1
    return 4 + 6 + 2 * (depth - 1) + 2 * (bits - 1) + 2


class Flow:
    def __init__(self, table):
        self.table, self.at, self.parts, self.count = list(table), 0, {}, {}

    def begin(self, i, part):
        self.parts[i], self.count[i] = part, 0

    def step(self, i):
        part = self.parts.get(i)
        if part is not None:
            self.count[i] += 1
            try:
                next(part)
            except StopIteration:
                self.parts[i] = None

    def peek(self, k):
        return self.table[self.at + k] if self.at + k < len(self.table) else ()

    def pump(self):
        for i in self.peek(0):
            self.step(i)
        self.at += 1

    def finish(self, i):
        while self.parts.get(i) is not None:
            self.step(i)

    def finish_all(self):
        while any(part is not None for part in self.parts.values()):
            for i in list(self.parts):
                self.step(i)


def stepped(flow, total, work):
    @pl.loop(0, total)
    def _(i):
        work(i)
        for k in range(total):
            if flow.peek(0):
                pl.when(i == k)(flow.pump)
            else:
                flow.pump()


def gather_copies(depth):
    return 2 * (depth - 1) + 4 + 2 + 4


GATHER_STEPS = 10


def all_sum(me, sems, first, pairs, stack, emit):
    hops = [me.core, me.across_x] + me.flips
    have = functools.partial(slot, first, slice(None))
    for i, other in enumerate(hops):
        came, total = functools.partial(slot, pairs, 2 * i), functools.partial(slot, pairs, 2 * i + 1)
        made = sems.copy(have, came, other)
        yield
        made.wait_recv()
        total()[...] = have()[...] + came()[...]
        have = total
    stack[me.z] = have()[...]
    mine = functools.partial(slot, stack, me.z)
    made = [sems.copy(have, mine, me.along_z[d]) for d in range(1, me.depth)]
    yield
    for m in made:
        m.wait_recv()
    total = stack[0]
    for i in range(1, me.depth):
        total = total + stack[i]
    emit(total)
    yield


def all_sum_sizes(depth, lanes):
    hops = 2 + lanes.bit_length() - 1
    return 2 * hops, hops + depth - 1, hops + 2


class Row:
    def __init__(self, ref):
        self.ref = ref

    def __getitem__(self, at):
        if at is Ellipsis:
            return self.ref[...].reshape(1, -1)
        return self.ref[at[1]].reshape(1, -1)


def stats(values):
    mean = jnp.mean(values, axis=-1, keepdims=True)
    centred = values - mean
    rstd = lax.rsqrt(jnp.mean(centred * centred, axis=-1, keepdims=True) + EPSILON)
    return centred, rstd


def dot_nn(a, b):
    return jnp.dot(a, b, preferred_element_type=F32)


def dot_nt(a, b):
    return lax.dot_general(a, b, (((1,), (1,)), ((), ())), preferred_element_type=F32)


def dot_tn(a, b):
    return lax.dot_general(a, b, (((0,), (0,)), ((), ())), preferred_element_type=F32)


def lane_halves(width=128):
    lane = lax.broadcasted_iota(jnp.int32, (1, width), 1)
    low = (lane < width // 2).astype(F32)
    return low.astype(BF), (1.0 - low).astype(BF)


def norm_back(grad, normed, rstd):
    mean_g = jnp.mean(grad, axis=-1, keepdims=True)
    mean_gn = jnp.mean(grad * normed, axis=-1, keepdims=True)
    return (grad - mean_g - normed * mean_gn) * rstd


def down_sum(values):
    return jnp.sum(values, axis=0, keepdims=True)


def cut(sizes):
    return [pl.ds(128 * sum(sizes[:i]), 128 * size) for i, size in enumerate(sizes)]


def layer_kernel(
    depth, lanes,
    x_h, cot_h, seg, live, expert, g1, b1, qb, vb, ob, g2, b2, ib, yb,
    q_w, k_w, v_w, o_w, w_in, w_out,
    out_h, dx_h, counts, d_q, d_k, d_v, d_o, d_in, d_out,
    d_g1, d_b1, d_qb, d_vb, d_ob, d_g2, d_b2, d_ib, d_yb,
    qkv_h, a_h, pb_h, z_h, h_h, go_h,
    ga, gi, go, s1, s2, pa, po, x_s, o_s, c_s, xh, dattn, hd, tok, rstd_s,
    rc, ry, rx, rz, fin, far, vec, vec_pair, vec_stack, cnt, cnt_pair, cnt_stack, ib_s, yb_s,
    local, by_row, send, recv, rsend, rrecv, csend, crecv, vsend, vrecv, credit,
):
    me = Place(depth, lanes)
    g1, b1, qb, vb, ob, g2, b2, ib, yb = [Row(t) for t in (g1, b1, qb, vb, ob, g2, b2, ib, yb)]
    rows_w, width = q_w.shape
    row_total, slots = seg.shape
    blocks = s1.shape[0]
    x_, c_, z_ = me.x, me.c, me.z
    per = depth // 4
    gathered, reduced = [[cut(sizes) for sizes in cuts] for cuts in (GATHER_CUTS, REDUCE_CUTS)]
    count_part = sum(len(cuts) for cuts in gathered)
    reduce_base = count_part + 1
    reduce_total = sum(len(cuts) for cuts in reduced)
    vec_part = reduce_base + reduce_total
    used = [2]

    def move(src, dst):
        made = pltpu.make_async_copy(src, dst, local.at[used[0]])
        used[0] += 1
        made.start()
        return made

    def row(r):
        return pl.ds(pl.multiple_of(r * slots, slots), slots)

    def fill(refs):
        for k, ref in enumerate(refs):
            pltpu.make_async_copy(ref, ga.at[me.own[k], z_, x_, c_], local.at[k]).start()

    @pl.when(me.y == 0)
    def _():
        fill((q_w, k_w))

    @pl.when(me.y == 1)
    def _():
        fill((v_w, o_w))

    filled = [pltpu.make_async_copy(q_w, ga.at[me.own[k], z_, x_, c_], local.at[k]) for k in range(2)]
    for u in me.own:
        filled.append(move(w_in.at[:, pl.ds(pl.multiple_of(u * width, width), width)], gi.at[u, z_, x_, c_]))
        filled.append(move(w_out.at[pl.ds(pl.multiple_of(u * rows_w, 8), rows_w), :], go.at[z_, x_, c_, u]))
    m_x = move(x_h, x_s)
    gb = x_s
    me.greet()
    for m in filled:
        m.wait()

    def view_of(g, cols, first, second, third):
        def view(u, zs, xs, cs):
            if g > 1:
                return third.at[zs, xs, cs, u, :, cols]
            return (first, second)[g].at[u, zs, xs, cs, :, cols]

        return view

    flow, gather_sems, reduce_sems = Flow(TABLE), [], []
    for g in range(3):
        for cols_g in gathered[g]:
            sems = Sems(send, recv, len(gather_sems))
            flow.begin(len(gather_sems), gather_part(me, sems, view_of(g, cols_g, ga, gi, go)))
            gather_sems.append(sems)
    flow.pump()
    m_cot = move(cot_h, dattn)
    vec[...] = jnp.zeros_like(vec)
    for u in range(blocks):
        ib_s[u : u + 1, :] = ib[:, pl.ds(u * width, width)]
    yb_s[0:1, :] = yb[...]

    arrived = [0]

    def ready():
        flow.pump()
        flow.finish(arrived[0])
        arrived[0] += 1

    cnt[...] = jnp.zeros_like(cnt)
    for r in range(row_total):
        for e in range(3):
            hit = (expert[r] == e).astype(jnp.int32)
            cnt[e : e + 1, :] += live[r : r + 1, :] * hit
    csems = Sems(csend, crecv, 0)

    def count_out(total):
        summed = jnp.broadcast_to(jnp.sum(total, axis=1, keepdims=True), (8, 128))
        for e in range(3):
            counts[e] = jnp.sum(total[e : e + 1, :].astype(F32)).astype(jnp.int32)
        one = [summed[e : e + 1, :].astype(F32) for e in range(3)]
        for r in range(row_total):
            own = jnp.zeros_like(one[0])
            for e in range(3):
                own = own + one[e] * (expert[r] == e).astype(F32)
            scale = (one[1] + one[2]) / (2.0 * own)
            rows = pl.ds(r * slots, slots)
            tok[rows, :] = tok[rows, :] * scale

    flow.begin(count_part, all_sum(me, csems, cnt, cnt_pair, cnt_stack, count_out))
    flow.pump()
    m_x.wait()

    def first_norm(r):
        rows = row(r)
        centred, rstd = stats(x_s[rows, :].astype(F32))
        s1[3, rows, :] = (centred * rstd * g1[...] + b1[...]).astype(BF)

    stepped(flow, row_total, first_norm)
    spilled = [move(s1.at[3], a_h)]

    row_pos = lax.broadcasted_iota(jnp.int32, (slots, slots), 0)
    col_pos = lax.broadcasted_iota(jnp.int32, (slots, slots), 1)
    for r in range(row_total):
        seg_row = seg[r : r + 1, :]
        live_row = live[r : r + 1, :]
        down = jnp.transpose(jnp.broadcast_to(seg_row.astype(F32), (slots, slots)))
        across = jnp.where(live_row > 0, seg_row, -1 - col_pos[0:1, :]).astype(F32)
        allowed = (down == across) | (row_pos == col_pos)
        hd[pl.ds(r * slots, slots), pl.ds(0, slots)] = jnp.where(allowed, 0.0, MASKED)
        live_down = jnp.transpose(jnp.broadcast_to(live_row.astype(F32), (128, slots)))
        tok[pl.ds(r * slots, slots), :] = live_down
        flow.pump()

    masks = lane_halves()
    for cols_h in gathered[0]:
        ready()

        def project(r, cols_h=cols_h):
            rows = row(r)
            a_row = s1[3, rows, :]
            for u, add in enumerate((qb, None, vb)):
                value = dot_nn(a_row, ga[u, :, :, :, :, cols_h].reshape(width, cols_h.size))
                if add is not None:
                    value = value + add[:, cols_h]
                s1[u, rows, cols_h] = value.astype(BF)

        stepped(flow, row_total, project)

        def attend(r, cols_h=cols_h):
            rows = row(r)
            for start in range(cols_h.start, cols_h.start + cols_h.size, 128):
                cols = pl.ds(start, 128)
                q2, k2, v2 = s1[0, rows, cols], s1[1, rows, cols], s1[2, rows, cols]
                mixed = jnp.zeros((slots, 128), F32)
                for i in range(2):
                    scores = dot_nt(q2 * (masks[i] * 0.125), k2) + hd[rows, pl.ds(0, slots)]
                    top = jnp.max(scores, axis=-1, keepdims=True)
                    terms = jnp.exp(scores - top)
                    inv = 1.0 / jnp.sum(terms, axis=-1, keepdims=True)
                    probs = (terms * inv).astype(BF)
                    head = start // 64 + i
                    s2[head // 3, rows, pl.ds((head % 3) * slots, slots)] = probs
                    mixed = mixed + dot_nn(probs, v2 * masks[i])
                o_s[rows, cols] = mixed.astype(BF)

        stepped(flow, row_total, attend)
        for u in range(3):
            spilled.append(move(s1.at[u, :, cols_h], qkv_h.at[u, :, cols_h]))
        for head in range(cols_h.start // 64, (cols_h.start + cols_h.size) // 64):
            cols = pl.ds((head % 3) * slots, slots)
            spilled.append(move(s2.at[head // 3, :, cols], pb_h.at[head // 3, :, cols]))

    def second_norm(r):
        rows = row(r)
        h_row = x_s[rows, :].astype(F32) + dot_nn(o_s[rows, :], ga[3].reshape(width, width)) + ob[...]
        hd[rows, :] = h_row
        centred, rstd = stats(h_row)
        normed = centred * rstd
        xh[rows, :] = normed.astype(BF)
        rstd_s[rows, :] = jnp.broadcast_to(rstd, (slots, 128))
        c_s[rows, :] = (normed * g2[...] + b2[...]).astype(BF)

    stepped(flow, row_total, second_norm)
    m_h = move(hd, h_h)
    for m in spilled:
        m.wait()
    pair_rows = row_total // 2
    for cols_h in gathered[1]:
        ready()

        def hidden(t, cols_h=cols_h):
            u, first = t // pair_rows, 2 * lax.rem(t, pair_rows)
            weight = gi[u, :, :, :, :, cols_h].reshape(width, cols_h.size)
            for s in range(2):
                rows = row(first + s)
                pre = dot_nn(c_s[rows, :], weight) + ib_s[pl.ds(u, 1), cols_h]
                cdf = 0.5 * (1.0 + lax.erf(pre * 0.7071067811865476))
                s1[u, rows, cols_h] = (pre * cdf).astype(BF)
                s2[u, rows, cols_h] = (cdf + pre * (jnp.exp(-0.5 * pre * pre) * 0.3989422804014327)).astype(BF)

        stepped(flow, blocks * pair_rows, hidden)
    m_z = move(s1, z_h)
    flow.finish(count_part)
    m_cot.wait()

    def begin(g, cols):
        i = len(reduce_sems)
        at = pl.ds((2 - g) * width + cols.start, cols.size)

        def emit(u, mine, k, value):
            value = value.astype(F32)
            if g == 0:
                even = (me.y == 0) if mine else (me.y == 1)

                @pl.when(even)
                def _():
                    (d_q, d_k)[k][:, cols] = value

                @pl.when(jnp.logical_not(even))
                def _():
                    (d_v, d_o)[k][:, cols] = value
            elif g == 1:
                d_in[:, pl.ds(pl.multiple_of(u * width + cols.start, 128), cols.size)] = value
            else:
                d_out[pl.ds(pl.multiple_of(u * rows_w, 8), rows_w), cols] = value

        sems = Sems(rsend, rrecv, i)
        reduce_sems.append(sems)
        bufs = [functools.partial(strip, rc, pl.ds(0, cols.size), i % 2)]
        bufs += [functools.partial(strip, t, at) for t in (ry, rx, rz, fin, far)]
        while i >= 2 and flow.count[reduce_base + i - 2] < 4:
            flow.step(reduce_base + i - 2)
        view = view_of(g, cols, pa, None, po) if g != 1 else view_of(2, cols, None, None, go)
        give = i < reduce_total - 2
        flow.begin(reduce_base + i, reduce_part(me, sems, view, bufs, emit, credit, i >= 2, give))
        flow.step(reduce_base + i)

    def scaled(r):
        rows = row(r)
        value = (dattn[rows, :].astype(F32) * tok[rows, 0:1]).astype(BF)
        gb[rows, :] = value
        vec[7:8, :] += down_sum(value.astype(F32))

    stepped(flow, row_total, scaled)
    for cols_h in reduced[0]:
        def out_grad(u, cols_h=cols_h):
            value = dot_tn(s1[u], gb[:, cols_h]).astype(BF)
            po[pl.ds(u * per, per), :, :, :, :, cols_h] = value.reshape(per, 2, 2, 4, rows_w, cols_h.size)

        stepped(flow, blocks, out_grad)
        begin(2, cols_h)
    m_z.wait()
    m_q = [move(qkv_h.at[u], s1.at[u]) for u in range(3)] + [move(a_h, s1.at[3])]
    for _ in gathered[2]:
        ready()
    m_go = move(go, go_h)

    def hidden_grad(t):
        u, rows = t // row_total, row(lax.rem(t, row_total))
        weight = go[pl.ds(u * per, per)].reshape(width, width)
        value = (dot_nt(gb[rows, :], weight) * s2[u, rows, :].astype(F32)).astype(BF)
        s2[u, rows, :] = value
        vec[pl.ds(8 + u, 1), :] += down_sum(value.astype(F32))

    stepped(flow, blocks * row_total, hidden_grad)
    for s in gather_sems:
        s.drain()
    csems.drain()
    m_go.wait()
    for cols_h in reduced[1]:
        def in_grad(u, cols_h=cols_h):
            value = dot_tn(c_s[...], s2[u, :, cols_h]).astype(BF)
            go[:, :, :, u, :, cols_h] = value.reshape(depth, 2, 2, rows_w, cols_h.size)

        stepped(flow, blocks, in_grad)
        begin(1, cols_h)
    m_h.wait()

    def mid_grad(r):
        rows = row(r)
        grad = dot_nt(s2[0, rows, :], gi[0].reshape(width, width))
        for u in range(1, blocks):
            grad = grad + dot_nt(s2[u, rows, :], gi[u].reshape(width, width))
        normed = xh[rows, :].astype(F32)
        vec[5:6, :] += down_sum(grad * normed)
        vec[6:7, :] += down_sum(grad)
        value = dattn[rows, :].astype(F32) * tok[rows, 0:1]
        value = value + norm_back(grad * g2[...], normed, rstd_s[rows, 0:1])
        hd[rows, :] = value
        value = value.astype(BF)
        dattn[rows, :] = value
        vec[4:5, :] += down_sum(value.astype(F32))

    stepped(flow, row_total, mid_grad)
    m_p = move(pb_h, s2)
    for cols_h in reduced[2]:
        value = dot_tn(o_s[...], dattn[:, cols_h]).astype(BF)
        pa[3, :, :, :, :, cols_h] = value.reshape(depth, 2, 2, rows_w, cols_h.size)
        flow.pump()

    def mixed_grad(r):
        rows = row(r)
        gb[rows, :] = dot_nt(dattn[rows, :], ga[3].reshape(width, width)).astype(BF)

    stepped(flow, row_total, mixed_grad)
    for m in m_q:
        m.wait()
    m_p.wait()
    for cols_h in reduced[2]:
        def attend_back(r, cols_h=cols_h):
            rows = row(r)
            for start in range(cols_h.start, cols_h.start + cols_h.size, 128):
                cols = pl.ds(start, 128)
                q2, k2, v2, do2 = s1[0, rows, cols], s1[1, rows, cols], s1[2, rows, cols], gb[rows, cols]
                dq = jnp.zeros((slots, 128), F32)
                dk, dv = dq, dq
                both = do2.astype(F32) * o_s[rows, cols].astype(F32)
                for i in range(2):
                    head = start // 64 + i
                    probs = s2[head // 3, rows, pl.ds((head % 3) * slots, slots)]
                    do1 = do2 * masks[i]
                    dp = dot_nt(do1, v2)
                    wide = probs.astype(F32)
                    inner = jnp.sum(both * masks[i].astype(F32), axis=-1, keepdims=True)
                    ds = (wide * (dp - inner)).astype(BF)
                    dq = dq + dot_nn(ds, k2 * masks[i])
                    dk = dk + dot_tn(ds, q2 * masks[i])
                    dv = dv + dot_tn(probs, do1)
                dq, dv = (dq * 0.125).astype(BF), dv.astype(BF)
                s1[0, rows, cols] = dq
                s1[1, rows, cols] = (dk * 0.125).astype(BF)
                s1[2, rows, cols] = dv
                vec[2:3, cols] += down_sum(dq.astype(F32))
                vec[3:4, cols] += down_sum(dv.astype(F32))

        stepped(flow, row_total, attend_back)
        if cols_h is reduced[2][-1]:
            m_x = move(x_h, x_s)

        def project_grad(u, cols_h=cols_h):
            value = dot_tn(s1[3], s1[u, :, cols_h]).astype(BF)
            pa[u, :, :, :, :, cols_h] = value.reshape(depth, 2, 2, rows_w, cols_h.size)

        stepped(flow, 3, project_grad)
        begin(0, cols_h)
    m_z = move(z_h, s2)
    for i, sems in enumerate(reduce_sems):
        if len(reduced[0]) <= i < len(reduced[0]) + len(reduced[1]):
            flow.finish(reduce_base + i)
            sems.drain()
    m_go = move(go_h, go)
    m_x.wait()

    def h_back(r):
        return pltpu.make_async_copy(h_h.at[row(r), :], hd.at[row(r), :], by_row.at[0, r])

    def dx_back(r):
        return pltpu.make_async_copy(dattn.at[row(r), :], dx_h.at[row(r), :], by_row.at[1, r])

    def last_grad(r):
        rows = row(r)
        grad = dot_nt(s1[0, rows, :], ga[0].reshape(width, width))
        for u in (1, 2):
            grad = grad + dot_nt(s1[u, rows, :], ga[u].reshape(width, width))
        centred, rstd = stats(x_s[rows, :].astype(F32))
        normed = centred * rstd
        vec[0:1, :] += down_sum(grad * normed)
        vec[1:2, :] += down_sum(grad)
        dattn[rows, :] = (hd[rows, :] + norm_back(grad * g1[...], normed, rstd)).astype(BF)
        dx_back(r).start()
        h_back(r).start()

    stepped(flow, row_total, last_grad)
    vsems = Sems(vsend, vrecv, 0)

    def vec_out(total):
        for i, ref in enumerate((d_g1, d_b1, d_qb, d_vb, d_ob, d_g2, d_b2, d_yb)):
            ref[...] = total[i]
        for u in range(blocks):
            d_ib[pl.ds(u * width, width)] = total[8 + u]

    flow.begin(vec_part, all_sum(me, vsems, vec, vec_pair, vec_stack, vec_out))
    flow.step(vec_part)
    m_z.wait()
    m_go.wait()
    for r in range(row_total):
        h_back(r).wait()
        dx_back(r).wait()

    half = width // 2

    def outward(t):
        rows, cols = row(t // 2), pl.ds(pl.multiple_of(lax.rem(t, 2) * half, half), half)
        value = hd[rows, cols] + yb_s[0:1, cols]
        for u in range(blocks):
            value = value + dot_nn(s2[u, rows, :], go[u * per : (u + 1) * per, :, :, :, :, cols].reshape(width, half))
        gb[rows, cols] = value.astype(BF)

    stepped(flow, 2 * row_total, outward)
    m_out = move(gb, out_h)
    flow.pump()
    flow.finish_all()
    for s in reduce_sems:
        s.drain()
    vsems.drain()
    m_out.wait()


def whole_layer(depth, lanes, x, cot, seg, live, expert, vectors, weights):
    tokens, width = x.shape
    row_total, slots = seg.shape
    rows_w = weights[0].shape[0]
    ff = weights[4].shape[1]
    blocks = ff // width
    g_parts, r_parts = [sum(len(sizes) for sizes in cuts) for cuts in (GATHER_CUTS, REDUCE_CUTS)]
    cols = 128 * max(max(sizes) for sizes in REDUCE_CUTS)
    g_per, r_per = gather_copies(depth), reduce_copies(depth, lanes)
    bits = max(lanes.bit_length() - 1, 1)
    pair_n, pair_c, _ = all_sum_sizes(depth, lanes)
    vec_rows = 8 + -(-blocks // 8) * 8
    anyspec = pl.BlockSpec(memory_space=pl.ANY)
    vspec = pl.BlockSpec(memory_space=pltpu.VMEM)
    sspec = pl.BlockSpec(memory_space=pltpu.SMEM)
    like = jax.ShapeDtypeStruct
    unit, unit_o = (4, depth, 2, 2, rows_w, width), (depth, 2, 2, 4, rows_w, width)
    flat, wide = (tokens, width), (blocks, tokens, width)
    o = lambda *s: like(s, F32)
    v = lambda *s: pltpu.VMEM(s, BF)
    f = lambda *s: pltpu.VMEM(s, F32)
    n = lambda *s: pltpu.VMEM(s, jnp.int32)
    dma = lambda *s: pltpu.SemaphoreType.DMA(s)
    return pl.pallas_call(
        functools.partial(layer_kernel, depth, lanes),
        out_shape=[like(flat, BF), like(flat, BF), like((3,), jnp.int32)]
        + [o(rows_w, width)] * 4 + [o(rows_w, ff), o(4 * rows_w, width)]
        + [o(width)] * 7 + [o(ff), o(width)]
        + [like((3, *flat), BF), like(flat, BF), like(wide, BF), like(wide, BF), like(flat, F32), like(unit_o, BF)],
        in_specs=[anyspec] * 2 + [vspec] * 2 + [sspec] + [vspec] * 9 + [anyspec] * 6,
        out_specs=[anyspec] * 2 + [sspec] + [vspec] * 15 + [anyspec] * 6,
        scratch_shapes=[
            v(*unit), v(*unit), v(*unit_o), v(*wide), v(*wide), v(*unit), v(*unit_o),
            v(*flat), v(*flat), v(*flat), v(*flat), v(*flat), f(*flat), f(tokens, 128), f(tokens, 128),
            v(2, 4, depth, 2, rows_w, cols), v(3, depth, rows_w, 3 * width), v(3, depth, rows_w, 3 * width),
            v(2, depth - 1, rows_w, 3 * width), v(bits, 2, rows_w, 3 * width), v(bits, 2, rows_w, 3 * width),
            f(vec_rows, width), f(pair_n, vec_rows, width), f(depth, vec_rows, width),
            n(8, slots), n(pair_n, 8, slots), n(depth, 8, slots), f(-(-blocks // 8) * 8, width), f(8, width),
            dma(64), dma(2, row_total), dma(g_parts, g_per), dma(g_parts, g_per), dma(r_parts, r_per), dma(r_parts, r_per),
            dma(1, pair_c), dma(1, pair_c), dma(1, pair_c), dma(1, pair_c), pltpu.SemaphoreType.REGULAR,
        ],
        compiler_params=pltpu.CompilerParams(collective_id=0, has_side_effects=True, vmem_limit_bytes=VMEM_BYTES),
        name="whole_layer",
    )(x, cot, seg, live, expert, *vectors, *weights)


def hand_over_kernel(count, *refs):
    sources, targets = refs[:count], refs[count + 1 : 2 * count + 1]
    stage, sem = refs[2 * count + 2 : 3 * count + 2], refs[-1]
    into = [pltpu.make_async_copy(s, m, sem.at[0, i]) for i, (s, m) in enumerate(zip(sources, stage))]
    out = [pltpu.make_async_copy(m, t, sem.at[1, i]) for i, (m, t) in enumerate(zip(stage, targets))]
    for m in into:
        m.start()
    for i in range(3):
        refs[2 * count + 1][i] = refs[count][i]
    for i in sorted(range(count), key=lambda i: math.prod(sources[i].shape)):
        into[i].wait()
        out[i].start()
    for m in out:
        m.wait()


def hand_over(counts, arrays):
    anyspec = pl.BlockSpec(memory_space=pl.ANY)
    sspec = pl.BlockSpec(memory_space=pltpu.SMEM)
    count = len(arrays)
    return pl.pallas_call(
        functools.partial(hand_over_kernel, count),
        out_shape=[jax.ShapeDtypeStruct(t.shape, t.dtype) for t in (*arrays, counts)],
        in_specs=[anyspec] * count + [sspec],
        out_specs=[anyspec] * count + [sspec],
        scratch_shapes=[pltpu.VMEM(t.shape, t.dtype) for t in arrays] + [pltpu.SemaphoreType.DMA((2, count))],
        name="hand_over",
    )(*arrays, counts)


def body(
    layer_in, segment_ids, live_mask, expert_ids, cotangent,
    norm1_gain, norm1_bias, q_weight, q_bias, k_weight, v_weight, v_bias, o_weight, o_bias,
    norm2_gain, norm2_bias, in_weight, in_bias, out_weight, out_bias,
):
    row_local, slot_total, width_all = layer_in.shape
    tokens = row_local * slot_total
    depth = lax.axis_size("wide") // 4
    lanes = lax.axis_size("narrow")
    x = layer_in.reshape(tokens, width_all)
    vectors = [norm1_gain, norm1_bias, q_bias, v_bias, o_bias, norm2_gain, norm2_bias, in_bias, out_bias]
    weights = (q_weight, k_weight, v_weight, o_weight, in_weight, out_weight)
    layer_out, input_grad, counts, *grads = whole_layer(
        depth, lanes, x, cotangent.reshape(tokens, width_all), segment_ids, live_mask, expert_ids, vectors, weights
    )
    (
        layer_out, input_grad, d_q, d_k, d_v, d_o, d_in, d_out,
        d_g1, d_b1, d_qb, d_vb, d_ob, d_g2, d_b2, d_ib, d_yb, counts,
    ) = hand_over(counts, (layer_out, input_grad, *grads[:15]))
    return (
        layer_out.reshape(layer_in.shape), input_grad.reshape(layer_in.shape), counts,
        d_g1, d_b1, d_q, d_qb, d_k, d_v, d_vb, d_o, d_ob, d_g2, d_b2, d_in, d_ib, d_out, d_yb,
    )


def solution(mesh):
    rows, row_pair = P(("wide", "narrow"), None, None), P(("wide", "narrow"), None)
    whole, split = P(), P("wide", None)
    return jax.shard_map(
        body,
        mesh=mesh,
        in_specs=(
            rows, row_pair, row_pair, P(("wide", "narrow")), rows,
            whole, whole, split, whole, split, split, whole, split, whole,
            whole, whole, split, whole, split, whole,
        ),
        out_specs=(
            rows, rows, whole, whole, whole, split, whole, split, split, whole, split, whole,
            whole, whole, split, whole, split, whole,
        ),
        check_vma=False,
    )
```
